32 devices in a mesh: req: 8 (over z, y), head: 4 (over x, core).
Axes of the slice: x: 2, y: 2, z: 4, core: 2. Of those that a mesh axis runs over, the one named last changes fastest.
Arguments:
- tokens: bfloat16 [512, 2048], P('req'), may hold values from -6 to 6
- attn_gain: bfloat16 [2048], replicated, may hold values from 0.25 to 1.75
- q_weight: bfloat16 [2048, 2048], P(None, 'head'), may hold values from -0.125 to 0.125
- k_weight: bfloat16 [2048, 2048], P(None, 'head'), may hold values from -0.125 to 0.125
- v_weight: bfloat16 [2048, 2048], P(None, 'head'), may hold values from -0.125 to 0.125
- o_weight: bfloat16 [2048, 2048], P('head'), may hold values from -0.1875 to 0.1875
- k_cache: bfloat16 [512, 16, 128, 128], P('req', 'head'), may hold values from -1500 to 1500
- v_cache: bfloat16 [512, 16, 128, 128], P('req', 'head'), may hold values from -6 to 6
- lengths: int32 [512], P('req'), may hold values from 16 to 128
- moe_gain: bfloat16 [2048], replicated, may hold values from 0.25 to 1.75
- gate_weight: bfloat16 [16, 2048, 1024], P('req', None, 'head'), may hold values from -0.125 to 0.125
- up_weight: bfloat16 [16, 2048, 1024], P('req', None, 'head'), may hold values from -0.125 to 0.125
- down_weight: bfloat16 [16, 1024, 2048], P('req', 'head'), may hold values from -0.25 to 0.25
- expert_ids: int32 [512, 8], P('req'), may hold values from 0 to 15, all different within a row; in each aligned block of 64 rows (0 to 63, 64 to 127, ...) at most 64 rows name the same one
- route_weights: bfloat16 [512, 8], P('req'), may hold values from 0.049804688 to 0.5
Outputs:
- attended: bfloat16 [512, 2048], P('req', 'head')
- expert_out: bfloat16 [512, 2048], P('req', 'head')
The draws below stay inside these ranges and needn't reach their ends.
Inputs may be any that keep to these rules, and one draw needn't show every extreme that they name: `expert_ids`: each row names 8 different experts; within the rows of one device along req (aligned blocks of 64 rows) no expert is named by more than 64 rows.
All inputs are finite; a program needn't handle non-finite values.
Results may differ from the reference program's by a relative error of at most 0.02.
The reference program's roundings to bfloat16 on the way count: a program that leaves them out, or rounds other values in their place, can miss the bound.
Values may be sent and summed in bfloat16 or wider, within the bound.
A program may use at most 128 MiB of HBM per device.

```python
import math
import jax
import jax.numpy as jnp
import numpy as np
from jax import lax

D = 2048
HEADS = 16
HD = 128
FF = 1024
TOP = 8
EXP_DEV = 2
CACHE = 128
REQ_DEV = 64
REQUESTS = 512
EXPERTS = 16
MOST = 64
N_REQ = 8
N_HEAD = 4


def draw_lengths(key, part):
    lowest = CACHE // 8
    first_key, second_key, third_key = jax.random.split(key, 3)
    drawn_lengths = jax.random.randint(first_key, (REQUESTS,), lowest, CACHE + 1, dtype=jnp.int32)
    longest_at = jax.random.randint(second_key, (), 0, REQUESTS // 2, dtype=jnp.int32)
    shortest_at = jax.random.randint(third_key, (), REQUESTS // 2, REQUESTS, dtype=jnp.int32)
    return drawn_lengths.at[longest_at].set(CACHE).at[shortest_at].set(lowest)


def draw_k_cache(key, part):
    base_key = jax.random.fold_in(key, 0)
    normal_part = jnp.clip(jax.random.normal(base_key, (REQUESTS, HEADS, CACHE, HD), jnp.float32), -6.0, 6.0)
    return jnp.clip(normal_part, -1500.0, 1500.0).astype(jnp.bfloat16)


def spiked(values, rng, source, target, shards_of, factor):
    owner, partner = [(jnp.arange(values.shape[dim]) // (values.shape[dim] // shards_of)).reshape([-1 if axis == dim else 1 for axis in range(values.ndim)]) for dim in (source, target)]
    chosen = jax.random.permutation(rng, shards_of)[partner]
    strong = (owner == chosen) | (owner == (partner + shards_of // 2) % shards_of)
    return jnp.where(strong, factor * values, values)


def shard_levels(own_key, dims, cuts, smallest, top_value):
    loudness, own = 1.0, jax.random.fold_in(own_key, 6)
    for position, shards_of in cuts:
        heights = jnp.exp(jax.random.uniform(jax.random.fold_in(own, position), (shards_of,), jnp.float32, smallest / len(cuts), top_value / len(cuts)))
        loudness = loudness * jnp.repeat(heights, dims[position] // shards_of).reshape([-1 if axis == position else 1 for axis in range(len(dims))])
    return loudness


def routed_block(stream_key, own, number, rows, count, top, limit, lean):
    order = jax.random.permutation(stream_key, count)
    packed, common = portions_of(count, rows * top, limit, lean, True), portions_of(count, rows * top, limit, lean, False)
    places = jnp.arange(count)

    def named(sizes, rotation):
        used = int((sizes > 0).sum())
        fixed = max(1, used // 4)
        passed = fixed + (places - fixed + rotation * (used - fixed)) % max(1, count - fixed)
        return jnp.zeros((count,), jnp.int32).at[order[jnp.where(places < fixed, places, passed)]].set(jnp.asarray(sizes, jnp.int32))

    sizes = jnp.where(number % 4 == 0, named(packed, number // 4), named(common, number - number // 4 - 1))
    mixed = jax.random.permutation(jax.random.fold_in(own, 3), count)
    source_of, sink = mixed[0:count // 2 * 2:2], mixed[1:count // 2 * 2:2]
    slack = jnp.minimum(sizes[source_of] - 1, limit - sizes[sink]) // 2
    slack = jnp.where((source_of == order[0]) | (sink == order[0]) | (sizes[sink] == 0), 0, jnp.maximum(slack, 0))
    passed = jax.random.randint(jax.random.fold_in(own, 4), (count // 2,), 0, 1 << 20) % (slack + 1)
    sizes = sizes.at[source_of].add(-passed).at[sink].add(passed)
    members = jnp.searchsorted(jnp.cumsum(sizes), jnp.arange(rows * top), side="right").astype(jnp.int32)
    grid = members.reshape(top, rows).T
    grid = grid[jax.random.permutation(jax.random.fold_in(own, 1), rows)]
    rotation = jax.random.randint(jax.random.fold_in(own, 2), (rows, 1), 0, top)
    return jnp.take_along_axis(grid, (jnp.arange(top)[None, :] + rotation) % top, axis=1)


def portions_of(amount, total, most, skew, full):
    weights = [(1 << 20) // math.isqrt(rank ** skew) + 1 for rank in range(1, amount + 1)]
    largest = most if full else min(most, max(-(-total // amount), total * weights[0] // sum(weights)))
    least = 1 if total - largest >= amount - 1 else 0
    holding, surplus = [largest] + [least] * (amount - 1), total - largest - least * (amount - 1)
    while surplus > 0:
        free = [i for i in range(1, amount) if holding[i] < largest] or [i for i in range(1, amount) if holding[i] < most]
        whole, remaining = sum([weights[i] for i in free]), surplus
        for i in free:
            more = min(most - holding[i], max(1, remaining * weights[i] // whole), surplus)
            holding[i] = holding[i] + more
            surplus = surplus - more
    return np.array(holding)


def scatter_about(key, shape, spread, limit, cuts=(), held_as=jnp.bfloat16):
    values = spread * jax.random.normal(key, shape, jnp.float32)
    if cuts:
        values = values * shard_levels(key, shape, cuts, -0.22, 0.18)
    return jnp.clip(values, -limit, limit).astype(held_as)


def bell_draw_with(rng, dims, deviation, bound, cuts, heavy, held_as=jnp.bfloat16):
    values = deviation * jax.random.normal(rng, dims, jnp.float32)
    if cuts:
        values = values * shard_levels(rng, dims, cuts, -0.22, 0.18)
    return jnp.clip(spiked(values, jax.random.fold_in(rng, 3), *heavy), -bound, bound).astype(held_as)


def setup_inputs(seed: int = 0) -> dict:
    keys = jax.random.split(jax.random.key(seed), 16)
    tokens = scatter_about(keys[0], (REQUESTS, D), 1.0, 6.0, ((0, 8),))
    attn_gain = jnp.clip(1.0 + 0.15 * jax.random.normal(keys[1], (D,), jnp.float32), 0.25, 1.75).astype(jnp.bfloat16)
    q_weight = scatter_about(keys[2], (D, HEADS * HD), D ** -0.5, 0.125, ((1, 4),))
    k_weight = scatter_about(keys[3], (D, HEADS * HD), D ** -0.5, 0.125, ((1, 4),))
    v_weight = scatter_about(keys[4], (D, HEADS * HD), D ** -0.5, 0.125, ((1, 4),))
    o_weight = bell_draw_with(keys[5], (HEADS * HD, D), (HEADS * HD) ** -0.5, 0.1875, ((0, 4),), (0, 1, 4, 2.0))
    k_cache = draw_k_cache(jax.random.fold_in(keys[15], 71), 0)
    v_cache = scatter_about(keys[7], (REQUESTS, HEADS, CACHE, HD), 1.0, 6.0, ((0, 8), (1, 4)))
    lengths = draw_lengths(jax.random.fold_in(keys[15], 71), 0)
    moe_gain = jnp.clip(1.0 + 0.15 * jax.random.normal(keys[9], (D,), jnp.float32), 0.25, 1.75).astype(jnp.bfloat16)
    gate_weight = scatter_about(keys[10], (EXPERTS, D, FF), D ** -0.5, 0.125, ((0, 8), (2, 4)))
    up_weight = scatter_about(keys[11], (EXPERTS, D, FF), D ** -0.5, 0.125, ((0, 8), (2, 4)))
    down_weight = bell_draw_with(keys[12], (EXPERTS, FF, D), FF ** -0.5, 0.25, ((0, 8), (1, 4)), (1, 2, 4, 2.0))
    expert_ids_keys = jax.random.split(jax.random.fold_in(keys[13], 1), REQUESTS // REQ_DEV)
    expert_ids_turns = jax.random.permutation(jax.random.fold_in(keys[13], 3), REQUESTS // REQ_DEV)
    expert_ids = jax.vmap(lambda own, number: routed_block(jax.random.fold_in(keys[13], 2), own, number, REQ_DEV, EXPERTS, TOP, MOST, 2))(expert_ids_keys, expert_ids_turns).reshape((REQUESTS, TOP))
    route_weights = jnp.clip(0.049804688 + 0.4501953 * jax.random.uniform(keys[14], (REQUESTS, TOP), jnp.float32) ** shard_levels(keys[14], (REQUESTS, TOP), ((0, 8),), -0.2, 0.2), 0.049804688, 0.5).astype(jnp.bfloat16)
    return dict(tokens=tokens, attn_gain=attn_gain, q_weight=q_weight, k_weight=k_weight, v_weight=v_weight, o_weight=o_weight, k_cache=k_cache, v_cache=v_cache, lengths=lengths, moe_gain=moe_gain, gate_weight=gate_weight, up_weight=up_weight, down_weight=down_weight, expert_ids=expert_ids, route_weights=route_weights)


epsilon = 1e-05
rope_base = 10000.0

def rms_scale(values, gain_vector):
    widened = values.astype(jnp.float32)
    inverse = lax.rsqrt(lax.optimization_barrier(jnp.mean(widened * widened, axis=-1, keepdims=True)) + epsilon)
    return (widened * inverse * gain_vector.astype(jnp.float32)).astype(jnp.bfloat16)

def rotate(vectors, positions):
    half_dim = vectors.shape[-1] // 2
    exponent = jnp.arange(half_dim, dtype=jnp.float32) * (-2.0 / vectors.shape[-1])
    frequency = jnp.power(rope_base, exponent)
    angles = positions.astype(jnp.float32)[:, None] * frequency[None, :]
    cosine_table = jnp.cos(angles)[:, None, :]
    sine_table = jnp.sin(angles)[:, None, :]
    first_half = vectors[..., :half_dim]
    second = vectors[..., half_dim:]
    return jnp.concatenate([first_half * cosine_table - second * sine_table, second * cosine_table + first_half * sine_table], axis=-1)

def reference(tokens, attn_gain, q_weight, k_weight, v_weight, o_weight, k_cache, v_cache, lengths, moe_gain, gate_weight, up_weight, down_weight, expert_ids, route_weights):
    normed = rms_scale(tokens, attn_gain)
    queries = jnp.dot(normed, q_weight, preferred_element_type=jnp.float32).reshape(REQUESTS, HEADS, HD)
    new_keys = jnp.dot(normed, k_weight, preferred_element_type=jnp.float32).reshape(REQUESTS, HEADS, HD)
    new_values = jnp.dot(normed, v_weight, preferred_element_type=jnp.float32).astype(jnp.bfloat16).reshape(REQUESTS, HEADS, HD)
    queries = rotate(queries, lengths)
    new_keys = rotate(new_keys, lengths)
    scaling = 1.0 / math.sqrt(HD)
    in_cache = jnp.arange(CACHE, dtype=jnp.int32)[None, :] < lengths[:, None]

    def one_head(head_index):
        head_query = lax.dynamic_index_in_dim(queries, head_index, 1, keepdims=False)
        head_new_key = lax.dynamic_index_in_dim(new_keys, head_index, 1, keepdims=False)
        head_new_value = lax.dynamic_index_in_dim(new_values, head_index, 1, keepdims=False)
        cached_keys = lax.dynamic_index_in_dim(k_cache, head_index, 1, keepdims=False).astype(jnp.float32)
        cached_values = lax.dynamic_index_in_dim(v_cache, head_index, 1, keepdims=False).astype(jnp.float32)
        scores = jnp.einsum('rd,rcd->rc', head_query, cached_keys, precision=lax.Precision.HIGHEST) * scaling
        scores = jnp.where(in_cache, scores, -1e+30)
        own_score = lax.optimization_barrier(jnp.sum(head_query * head_new_key, axis=-1)) * scaling
        largest = jnp.maximum(lax.optimization_barrier(jnp.max(scores, axis=-1)), own_score)
        exponent_terms = jnp.exp(scores - largest[:, None])
        own_term = jnp.exp(own_score - largest)
        denominator = lax.optimization_barrier(jnp.sum(exponent_terms, axis=-1)) + own_term
        probability = (exponent_terms / denominator[:, None]).astype(jnp.bfloat16)
        own_prob = (own_term / denominator).astype(jnp.bfloat16)
        mixture = jnp.einsum('rc,rcd->rd', probability.astype(jnp.float32), cached_values, precision=lax.Precision.HIGHEST)
        mixture = mixture + own_prob.astype(jnp.float32)[:, None] * head_new_value.astype(jnp.float32)
        return mixture.astype(jnp.bfloat16)
    per_head = lax.map(one_head, jnp.arange(HEADS, dtype=jnp.int32))
    attention = jnp.transpose(per_head, (1, 0, 2)).reshape(REQUESTS, HEADS * HD)
    attended = (tokens.astype(jnp.float32) + jnp.dot(attention, o_weight, preferred_element_type=jnp.float32)).astype(jnp.bfloat16)
    expert_input = rms_scale(attended, moe_gain)
    capacity = MOST * N_REQ
    quarter = FF // N_HEAD

    def expert_share(expert_index):
        hits = expert_ids == expert_index
        token_weight = lax.optimization_barrier(jnp.sum(jnp.where(hits, route_weights.astype(jnp.float32), 0.0), axis=1))
        chosen = jnp.any(hits, axis=1)
        rows = jnp.nonzero(chosen, size=capacity, fill_value=0)[0].astype(jnp.int32)
        live = jnp.arange(capacity, dtype=jnp.int32) < jnp.sum(chosen.astype(jnp.int32))
        picked = expert_input[rows]
        gate_matrix = lax.dynamic_index_in_dim(gate_weight, expert_index, 0, keepdims=False)
        up_matrix = lax.dynamic_index_in_dim(up_weight, expert_index, 0, keepdims=False)
        down_matrix = lax.dynamic_index_in_dim(down_weight, expert_index, 0, keepdims=False)
        gate_act = jnp.dot(picked, gate_matrix, preferred_element_type=jnp.float32)
        lifted = jnp.dot(picked, up_matrix, preferred_element_type=jnp.float32)
        hidden = (jax.nn.silu(gate_act) * lifted).astype(jnp.bfloat16)
        split_hidden = hidden.reshape(capacity, N_HEAD, quarter).astype(jnp.float32)
        split_down = down_matrix.reshape(N_HEAD, quarter, D).astype(jnp.float32)
        output = jnp.einsum('chf,hfd->hcd', split_hidden, split_down, precision=lax.Precision.HIGHEST)
        output = output * jnp.where(live, token_weight[rows], 0.0)[None, :, None]
        return jnp.zeros((N_HEAD, REQUESTS, D), jnp.float32).at[:, rows].add(output)

    def one_group(accumulated, group_index):
        group_part = jnp.zeros((N_HEAD, REQUESTS, D), jnp.float32)
        for member in range(EXP_DEV):
            group_part = group_part + expert_share(group_index * EXP_DEV + member)
        rounded = lax.optimization_barrier(group_part.astype(jnp.bfloat16)).astype(jnp.float32)
        return (accumulated + lax.optimization_barrier(jnp.sum(rounded, axis=0)), None)
    summed, unused = lax.scan(one_group, jnp.zeros((REQUESTS, D), jnp.float32), jnp.arange(N_REQ, dtype=jnp.int32))
    return (attended, summed.astype(jnp.bfloat16))
```

```python
import functools
import math

import jax
import jax.numpy as jnp
from jax import lax
from jax.experimental import pallas as pl
from jax.experimental.pallas import tpu as pltpu
from jax.sharding import PartitionSpec as P
import numpy as np

epsilon = 1e-05
rope_base = 10000.0


MESH = pl.DeviceIdType.MESH


def moe_kernel(
    req_count,
    tok_ref, norm_gain_ref, gain_ref, freq_ref, len_ref, ids_ref, route_ref,
    q_hbm, k_hbm, v_hbm, kc_hbm, vc_hbm, o_hbm, gate_hbm, up_hbm, down_hbm,
    attended_ref, out_ref,
    q_buf, k_buf, v_buf, kc_buf, vc_buf, o_buf, gate_buf, up_buf, down_buf,
    pieces, score, mixed, own_value, own_score, held, attn_buf, wt_out, wt_in,
    part_out, part_in, gath, part, half_in, cross_out, cross_in, home_out, home_in,
    cache_sem, weight_sem, wt_send, wt_recv, rs_send, rs_recv, ga_send, ga_recv, sib_send, sib_recv, x_send, x_recv, hm_send, hm_recv,
):
    rows, width = attended_ref.shape
    head_dim = 2 * freq_ref.shape[1]
    cache_len = kc_buf.shape[2] // (q_buf.shape[1] // head_dim)
    experts = gate_buf.shape[0]
    req = lax.axis_index("req")
    head = lax.axis_index("head")
    near = head + 1 - 2 * (head % 2)
    cross = (head + 2) % 4
    far = (near + 2) % 4
    quarter = [head, near, cross, far]
    blocks = max(1, req_count // 4)
    chunk_total = req_count // blocks
    chunk_rows = blocks * rows
    step_rows = 128

    slots, batch = kc_buf.shape[0], kc_buf.shape[1]
    groups = rows // batch
    local_heads = q_buf.shape[1] // head_dim
    sources = [q_hbm, k_hbm, v_hbm, o_hbm, gate_hbm, up_hbm, down_hbm]
    targets = [q_buf, k_buf, v_buf, o_buf, gate_buf, up_buf, down_buf]
    weights = [
        pltpu.make_async_copy(source, target, weight_sem.at[i])
        for i, (source, target) in enumerate(zip(sources, targets))
    ]

    def cached(i, at):
        span = pl.ds(i * batch, batch)
        return (
            pltpu.make_async_copy(kc_hbm.at[span], kc_buf.at[at], cache_sem.at[0, at]),
            pltpu.make_async_copy(vc_hbm.at[span], vc_buf.at[at], cache_sem.at[1, at]),
        )

    for copy in weights[:3]:
        copy.start()
    for i in range(slots):
        for copy in cached(i, i):
            copy.start()
    for copy in weights[3:]:
        copy.start()

    barrier = pltpu.get_barrier_semaphore()
    for other in (near, cross, far):
        pl.semaphore_signal(barrier, inc=1, device_id=(req, other), device_id_type=MESH)
    for step in range(1, req_count):
        pl.semaphore_signal(
            barrier, inc=1, device_id=((req + step) % req_count, head), device_id_type=MESH
        )
    pl.semaphore_wait(barrier, 3 + req_count - 1)

    def remote(source, target, send, recv, device):
        return pltpu.make_async_remote_copy(
            src_ref=source, dst_ref=target, send_sem=send, recv_sem=recv,
            device_id=device, device_id_type=MESH,
        )

    def lanes(d):
        return pl.ds(pl.multiple_of(quarter[d] * width, width), width)

    lane = lax.broadcasted_iota(jnp.int32, (rows, 128), 1)
    named_by = lax.broadcasted_iota(jnp.int32, (128, rows), 0)
    identity = (
        lax.broadcasted_iota(jnp.int32, (rows, rows), 0)
        == lax.broadcasted_iota(jnp.int32, (rows, rows), 1)
    ).astype(jnp.bfloat16)

    def upright(across):
        return lax.dot_general(
            identity, across.astype(jnp.bfloat16), (((1,), (1,)), ((), ())),
            preferred_element_type=jnp.float32,
        )

    across = jnp.zeros((128, rows), jnp.float32)
    for k in range(ids_ref.shape[0]):
        across = across + jnp.where(
            named_by == ids_ref[k : k + 1, :],
            route_ref[k : k + 1, :].astype(jnp.float32),
            0.0,
        )
    dense = upright(across).astype(jnp.bfloat16)
    wt_out[...] = dense
    wt_in[0:rows, :] = dense
    lens = upright(jnp.broadcast_to(len_ref[...].astype(jnp.float32), (128, rows)))
    held[...] = lens

    def share(s):
        return remote(
            wt_out, wt_in.at[pl.ds(s * rows, rows)], wt_send.at[s], wt_recv.at[s],
            ((req + req_count - s) % req_count, head),
        )

    for s in range(1, req_count):
        share(s).start()

    tokens = tok_ref[...].astype(jnp.float32)
    spread_of = jnp.mean(tokens * tokens, axis=-1, keepdims=True)
    normed = (tokens * lax.rsqrt(spread_of + epsilon) * norm_gain_ref[...].astype(jnp.float32)).astype(
        jnp.bfloat16
    )
    angles = lens[:, 0 : head_dim // 2] * freq_ref[...]
    cosine, sine = jnp.cos(angles), jnp.sin(angles)
    cosine = jnp.concatenate([cosine, cosine], axis=1)
    sine = jnp.concatenate([-sine, sine], axis=1)
    scaling = 1.0 / math.sqrt(head_dim)
    own_scores = []
    for i in range(3):
        weights[i].wait()
    for n in range(local_heads):
        part_of = slice(n * head_dim, (n + 1) * head_dim)
        query, key, value = [
            jnp.dot(normed, ref[:, part_of], preferred_element_type=jnp.float32)
            for ref in (q_buf, k_buf, v_buf)
        ]
        query = query * cosine + pltpu.roll(query, head_dim // 2, 1) * sine
        key = key * cosine + pltpu.roll(key, head_dim // 2, 1) * sine
        own_value[:, part_of] = value.astype(jnp.bfloat16).astype(jnp.float32)
        own_scores.append(jnp.sum(query * key, axis=-1, keepdims=True) * scaling)
        upper = query.astype(jnp.bfloat16).astype(jnp.float32)
        rest = query - upper
        middle = rest.astype(jnp.bfloat16).astype(jnp.float32)
        for p, piece in enumerate((upper, middle, rest - middle)):
            pieces[pl.ds(3 * n + p, rows, stride=16), :] = piece
    for p in range(3 * local_heads, 16):
        pieces[pl.ds(p, rows, stride=16), :] = jnp.zeros((rows, head_dim), jnp.float32)
    own_all = jnp.zeros((rows, 128), jnp.float32)
    for n in range(local_heads):
        own_all = jnp.where(lane == n, own_scores[n], own_all)
    own_score[...] = own_all

    slab = local_heads * cache_len
    row16 = lax.broadcasted_iota(jnp.int32, (16, slab), 0)
    owner16 = lax.broadcasted_iota(jnp.int32, (16, slab), 1) // cache_len
    of_head = (row16 >= owner16 * 3) & (row16 < owner16 * 3 + 3)
    diagonal = row16 == owner16
    position = lax.broadcasted_iota(jnp.int32, (batch, cache_len), 1)

    @pl.loop(0, groups)
    def _(i):
        at = i % slots
        for copy in cached(i, at):
            copy.wait()
        first = pl.multiple_of(i * batch, batch)
        for r in range(batch):
            query = pieces[pl.ds(pl.multiple_of((first + r) * 16, 16), 16), :].astype(jnp.bfloat16)
            found = lax.dot_general(
                query, kc_buf[at, r], (((1,), (1,)), ((), ())), preferred_element_type=jnp.float32
            )
            score[r : r + 1, :] = jnp.sum(
                jnp.where(of_head, found, 0.0), axis=0, keepdims=True
            )
        members = pl.ds(first, batch)
        inside = position.astype(jnp.float32) < held[members, 0:1]
        own_block = own_score[members, :]
        chances, own_chances = [], []
        for n in range(local_heads):
            values = score[:, n * cache_len : (n + 1) * cache_len] * scaling
            values = jnp.where(inside, values, -1e30)
            own_one = own_block[:, n : n + 1]
            largest = jnp.maximum(jnp.max(values, axis=-1, keepdims=True), own_one)
            terms = jnp.exp(values - largest)
            own_term = jnp.exp(own_one - largest)
            totals = jnp.sum(terms, axis=-1, keepdims=True) + own_term
            chances.append(terms / totals)
            own_chances.append((own_term / totals).astype(jnp.bfloat16).astype(jnp.float32))
        chance = jnp.concatenate(chances, axis=1)
        for r in range(batch):
            spread_out = jnp.where(
                diagonal, jnp.broadcast_to(chance[r : r + 1, :], (16, slab)), 0.0
            ).astype(jnp.bfloat16)
            found = jnp.dot(spread_out, vc_buf[at, r], preferred_element_type=jnp.float32)
            mixed[r * 8 : (r + 1) * 8, :] = found[0:8, :]
        for n in range(local_heads):
            part_of = slice(n * head_dim, (n + 1) * head_dim)
            attn_buf[members, part_of] = (
                mixed[pl.ds(n, batch, stride=8), :] + own_chances[n] * own_value[members, part_of]
            )

        @pl.when(i + slots < groups)
        def _():
            for copy in cached(i + slots, at):
                copy.start()

    weights[3].wait()
    attn = attn_buf[...].astype(jnp.bfloat16)
    rs = []
    for d in (2, 3, 1):
        part_out[d - 1] = jnp.dot(
            attn, o_buf[:, lanes(d)], preferred_element_type=jnp.float32
        ).astype(jnp.bfloat16)
        copy = remote(
            part_out.at[d - 1], part_in.at[d - 1], rs_send.at[d - 1], rs_recv.at[d - 1],
            (req, quarter[d]),
        )
        copy.start()
        rs.append(copy)
    total = tok_ref[:, lanes(0)].astype(jnp.float32) + jnp.dot(
        attn, o_buf[:, lanes(0)], preferred_element_type=jnp.float32
    )
    for copy in rs:
        copy.wait_recv()
    for d in range(3):
        total = total + part_in[d].astype(jnp.float32)
    own = total.astype(jnp.bfloat16)
    attended_ref[...] = total
    gath[0, 0:rows, :] = own

    def slot(s):
        return pl.ds(s * rows, rows)

    def spread(s):
        return remote(
            gath.at[0, slot(0)], gath.at[0, slot(s)], ga_send.at[0, s], ga_recv.at[0, s],
            ((req + req_count - s) % req_count, head),
        )

    def pass_on(d, s):
        origin, device = {1: (0, near), 2: (0, cross), 3: (2, near)}[d]
        return remote(
            gath.at[origin, slot(s)], gath.at[d, slot(s)], ga_send.at[d, s], ga_recv.at[d, s],
            (req, device),
        )

    pass_on(2, 0).start()
    order = sorted(range(1, req_count), key=lambda s: (s + blocks * 0))
    for s in order:
        spread(s).start()
    pass_on(1, 0).start()
    for copy in weights[4:]:
        copy.wait()
    for s in range(1, req_count):
        share(s).wait_recv()

    def home(s):
        return remote(
            home_out.at[slot(s)], home_in.at[slot(s)], hm_send.at[s], hm_recv.at[s],
            ((req + s) % req_count, head),
        )

    def to_near(c, which):
        span = pl.ds(c * chunk_rows, chunk_rows)
        return remote(
            part.at[2 * which + 1, span], half_in.at[which, span],
            sib_send.at[which, c], sib_recv.at[which, c], (req, near),
        )

    def to_cross(c):
        span = pl.ds(c * chunk_rows, chunk_rows)
        return remote(
            cross_out.at[span], cross_in.at[span], x_send.at[c], x_recv.at[c], (req, cross)
        )

    def compute(start):
        span = pl.ds(start, step_rows)
        squares = jnp.zeros((step_rows, 1), jnp.float32)
        for d in range(4):
            x = gath[d, span, :].astype(jnp.float32)
            squares = squares + jnp.sum(x * x, axis=-1, keepdims=True)
        inverse = lax.rsqrt(squares * (1.0 / (4 * width)) + epsilon)
        gates = [jnp.zeros((step_rows, gate_buf.shape[2]), jnp.float32) for _ in range(experts)]
        ups = [jnp.zeros((step_rows, gate_buf.shape[2]), jnp.float32) for _ in range(experts)]
        for d in range(4):
            x = gath[d, span, :].astype(jnp.float32)
            x = (x * inverse * gain_ref[:, lanes(d)].astype(jnp.float32)).astype(jnp.bfloat16)
            depth = pl.ds(pl.multiple_of(quarter[d] * width, width), width)
            for e in range(experts):
                gates[e] = gates[e] + jnp.dot(
                    x, gate_buf[e, depth, :], preferred_element_type=jnp.float32
                )
                ups[e] = ups[e] + jnp.dot(
                    x, up_buf[e, depth, :], preferred_element_type=jnp.float32
                )
        hidden = [
            (g / (1.0 + jnp.exp(-g)) * u).astype(jnp.bfloat16) for g, u in zip(gates, ups)
        ]
        dense_wt = wt_in[span, :].astype(jnp.float32)
        column = lax.broadcasted_iota(jnp.int32, (step_rows, 128), 1)
        wt = [
            jnp.sum(
                jnp.where(column == req * experts + e, dense_wt, 0.0), axis=-1, keepdims=True
            )
            for e in range(experts)
        ]
        for d in (1, 3, 2, 0):
            value = jnp.zeros((step_rows, width), jnp.float32)
            for e in range(experts):
                value = value + wt[e] * jnp.dot(
                    hidden[e], down_buf[e, :, lanes(d)], preferred_element_type=jnp.float32
                )
            part[d, span, :] = value.astype(jnp.bfloat16)

    def reduce_cross(c):
        span = pl.ds(c * chunk_rows, chunk_rows)
        to_near(c, 1).wait_recv()
        cross_out[span, :] = (
            part[2, span, :].astype(jnp.float32) + half_in[1, span, :].astype(jnp.float32)
        ).astype(jnp.bfloat16)
        to_cross(c).start()

    def reduce_home(c):
        span = pl.ds(c * chunk_rows, chunk_rows)
        to_near(c, 0).wait_recv()
        to_cross(c).wait_recv()
        home_out[span, :] = (
            part[0, span, :].astype(jnp.float32)
            + half_in[0, span, :].astype(jnp.float32)
            + cross_in[span, :].astype(jnp.float32)
        ).astype(jnp.bfloat16)
        for s in range(c * blocks, (c + 1) * blocks):
            if s:
                home(s).start()

    def forward(c):
        for s in range(c * blocks, (c + 1) * blocks):
            if s:
                spread(s).wait_recv()
                pass_on(2, s).start()
                pass_on(1, s).start()

    def forward_far(c):
        for s in range(c * blocks, (c + 1) * blocks):
            pass_on(2, s).wait_recv()
            pass_on(3, s).start()

    forward(0)
    forward(1)
    forward_far(0)
    for c in range(chunk_total):
        if c + 2 < chunk_total:
            forward(c + 2)
        if c + 1 < chunk_total:
            forward_far(c + 1)
        for s in range(c * blocks, (c + 1) * blocks):
            pass_on(1, s).wait_recv()
            pass_on(3, s).wait_recv()
        steps = chunk_rows // step_rows
        if steps == 1:
            compute(c * chunk_rows)
        else:
            @pl.loop(0, steps)
            def _(i):
                compute(pl.multiple_of(c * chunk_rows + i * step_rows, step_rows))
        to_near(c, 1).start()
        to_near(c, 0).start()
        if c:
            reduce_cross(c - 1)
        if c > 1:
            reduce_home(c - 2)
    reduce_cross(chunk_total - 1)
    if chunk_total > 1:
        reduce_home(chunk_total - 2)
    reduce_home(chunk_total - 1)
    result = home_out[0:rows, :].astype(jnp.float32)
    for s in range(1, req_count):
        home(s).wait_recv()
        result = result + home_in[s * rows : (s + 1) * rows, :].astype(jnp.float32)
    out_ref[...] = result

    for copy in rs:
        copy.wait_send()
    for s in range(req_count):
        for d in range(1, 4):
            pass_on(d, s).wait_send()
        if s:
            spread(s).wait_send()
            share(s).wait_send()
            home(s).wait_send()
    for c in range(chunk_total):
        to_near(c, 0).wait_send()
        to_near(c, 1).wait_send()
        to_cross(c).wait_send()


def round_kernel(attended_ref, expert_ref, attended_out, expert_out):
    attended_out[...] = attended_ref[...].astype(attended_out.dtype)
    expert_out[...] = expert_ref[...].astype(expert_out.dtype)


def body(
    tokens,
    attn_gain,
    q_weight,
    k_weight,
    v_weight,
    o_weight,
    k_cache,
    v_cache,
    lengths,
    moe_gain,
    gate_weight,
    up_weight,
    down_weight,
    expert_ids,
    route_weights,
):
    rows, model_width = tokens.shape
    local_heads, cache_len, head_dim = k_cache.shape[1:]
    slab = local_heads * cache_len
    req_count = lax.axis_size("req")
    width = model_width // 4
    everyone = req_count * rows
    blocks = max(1, req_count // 4)
    chunks = req_count // blocks
    batch = 16
    slots = 4 if req_count <= 8 else 1
    bf16, f32 = jnp.bfloat16, jnp.float32
    half_dim = head_dim // 2
    frequency = jnp.power(rope_base, jnp.arange(half_dim, dtype=f32) * (-2.0 / head_dim))
    vmem = pl.BlockSpec(memory_space=pltpu.VMEM)
    hbm = pl.BlockSpec(memory_space=pl.ANY)
    dma = pltpu.SemaphoreType.DMA
    attended, expert_out = pl.pallas_call(
        functools.partial(moe_kernel, req_count),
        out_shape=(
            jax.ShapeDtypeStruct((rows, width), f32),
            jax.ShapeDtypeStruct((rows, width), f32),
        ),
        in_specs=[vmem] * 7 + [hbm] * 9,
        out_specs=(vmem, vmem),
        scratch_shapes=[
            pltpu.VMEM(q_weight.shape, bf16),
            pltpu.VMEM(k_weight.shape, bf16),
            pltpu.VMEM(v_weight.shape, bf16),
            pltpu.VMEM((slots, batch, slab, head_dim), bf16),
            pltpu.VMEM((slots, batch, slab, head_dim), bf16),
            pltpu.VMEM(o_weight.shape, bf16),
            pltpu.VMEM(gate_weight.shape, bf16),
            pltpu.VMEM(up_weight.shape, bf16),
            pltpu.VMEM(down_weight.shape, bf16),
            pltpu.VMEM((rows * 16, head_dim), f32),
            pltpu.VMEM((batch, slab), f32),
            pltpu.VMEM((batch * 8, head_dim), f32),
            pltpu.VMEM((rows, local_heads * head_dim), f32),
            pltpu.VMEM((rows, 128), f32),
            pltpu.VMEM((rows, 128), f32),
            pltpu.VMEM((rows, local_heads * head_dim), f32),
            pltpu.VMEM((rows, 128), bf16),
            pltpu.VMEM((everyone, 128), bf16),
            pltpu.VMEM((3, rows, width), bf16),
            pltpu.VMEM((3, rows, width), bf16),
            pltpu.VMEM((4, everyone, width), bf16),
            pltpu.VMEM((4, everyone, width), bf16),
            pltpu.VMEM((2, everyone, width), bf16),
            pltpu.VMEM((everyone, width), bf16),
            pltpu.VMEM((everyone, width), bf16),
            pltpu.VMEM((everyone, width), bf16),
            pltpu.VMEM((everyone, width), bf16),
            dma((2, slots)),
            dma((7,)),
            dma((req_count,)),
            dma((req_count,)),
            dma((3,)),
            dma((3,)),
            dma((4, req_count)),
            dma((4, req_count)),
            dma((2, chunks)),
            dma((2, chunks)),
            dma((chunks,)),
            dma((chunks,)),
            dma((req_count,)),
            dma((req_count,)),
        ],
        compiler_params=pltpu.CompilerParams(
            collective_id=0, has_side_effects=True, vmem_limit_bytes=58 << 20
        ),
    )(
        tokens,
        attn_gain.reshape(1, model_width),
        moe_gain.reshape(1, model_width),
        frequency.reshape(1, half_dim),
        lengths.reshape(1, rows),
        expert_ids.T,
        route_weights.T,
        q_weight,
        k_weight,
        v_weight,
        k_cache.reshape(rows, slab, head_dim),
        v_cache.reshape(rows, slab, head_dim),
        o_weight,
        gate_weight,
        up_weight,
        down_weight,
    )
    return pl.pallas_call(
        round_kernel,
        out_shape=[jax.ShapeDtypeStruct((rows, width), bf16)] * 2,
        in_specs=[vmem, vmem],
        out_specs=[vmem, vmem],
    )(attended, expert_out)


def decode_kernel(
    tok_hbm, norm_gain_hbm, gain_hbm, freq_hbm, len_hbm, ids_hbm, route_hbm,
    q_hbm, k_hbm, v_hbm, kc_hbm, vc_hbm, o_hbm, gate_hbm, up_hbm, down_hbm,
    attended_hbm, lines_hbm,
    tok_ref, norm_gain_ref, gain_ref, freq_ref, len_ref, ids_ref, route_ref,
    q_buf, k_buf, v_buf, kc_buf, vc_buf, o_buf, gate_buf, up_buf, down_buf,
    pieces, score, mixed, own_value, own_score, held, attn_buf, wt_out, wt_in, gain_f32,
    rs_out, rs_in, own_f32, own_buf, gath, part, core_in, s_out, s_in, f_out, f_in, z_out,
    cache_sem, load_sem, local_sem, send_sem, recv_sem,
):
    rows = tok_ref.shape[0]
    width = attended_hbm.shape[1]
    halves = gath.shape[2]
    part_rows = rows // halves
    line_rows = gath.shape[3]
    zs = line_rows // part_rows
    head_dim = 2 * freq_ref.shape[1]
    experts = gate_buf.shape[0]
    local_heads = q_buf.shape[1] // head_dim
    cache_len = kc_buf.shape[2] // local_heads
    groups, batch = kc_buf.shape[0], kc_buf.shape[1]
    slab = local_heads * cache_len
    bf16, f32 = jnp.bfloat16, jnp.float32

    req = lax.axis_index("req")
    head = lax.axis_index("head")
    z, y = req // 2, req % 2
    x, c = head // 2, head % 2
    near = head + 1 - 2 * c
    cross = (head + 2) % 4
    far = (near + 2) % 4
    z_of = [z, z + 1 - 2 * (z % 2), (z + 2) % 4, 3 - z]
    first_peer = (req + (1 - c) * (1 - 2 * y), head + c * (2 - 4 * x))
    second_peer = (req + c * (1 - 2 * y), head + (1 - c) * (2 - 4 * x))
    core_peer = (req, near)

    def z_peer(d):
        return (z_of[d] * 2 + y, head)

    def own_role(dx, dy):
        return [[0, 2 - c], [1 + c, 3]][dx][dy]

    def other_role(dx, dy):
        return [[0, 1 + c], [2 - c, 3]][dx][dy]

    quarters = {(0, 0): head, (0, 1): near, (1, 0): cross, (1, 1): far}

    def lanes(dx, dc):
        return pl.ds(pl.multiple_of(quarters[dx, dc] * width, width), width)

    loads = {}

    def load(name, source, target):
        copy = pltpu.make_async_copy(source, target, load_sem.at[len(loads)])
        loads[name] = copy
        copy.start()

    def cached(i):
        span = pl.ds(i * batch, batch)
        return (
            pltpu.make_async_copy(kc_hbm.at[span], kc_buf.at[i], cache_sem.at[0, i]),
            pltpu.make_async_copy(vc_hbm.at[span], vc_buf.at[i], cache_sem.at[1, i]),
        )

    load("ids", ids_hbm, ids_ref)
    load("route", route_hbm, route_ref)
    load("len", len_hbm, len_ref)
    load("freq", freq_hbm, freq_ref)
    load("norm_gain", norm_gain_hbm, norm_gain_ref)
    load("tok", tok_hbm, tok_ref)
    load("q", q_hbm, q_buf)
    load("k", k_hbm, k_buf)
    load("v", v_hbm, v_buf)
    per_half = groups // halves
    for i in range(groups):
        for copy in cached(i):
            copy.start()
        if i == 0:
            load("o", o_hbm, o_buf)
    load("gain", gain_hbm, gain_ref)
    load("gate", gate_hbm, gate_buf)
    load("up", up_hbm, up_buf)
    load("down", down_hbm, down_buf)

    barrier = pltpu.get_barrier_semaphore()
    for other in (near, cross, far):
        pl.semaphore_signal(barrier, inc=1, device_id=(req, other), device_id_type=MESH)
    for d in range(4):
        for dy in range(2):
            if d or dy:
                other = z_of[d] * 2 + (1 - y if dy else y)
                pl.semaphore_signal(barrier, inc=1, device_id=(other, head), device_id_type=MESH)

    sends = {}

    def remote(key, source, target, device):
        if key not in sends:
            at = len(sends)
            sends[key] = pltpu.make_async_remote_copy(
                src_ref=source, dst_ref=target, send_sem=send_sem.at[at], recv_sem=recv_sem.at[at],
                device_id=device, device_id_type=MESH,
            )
        return sends[key]

    lane = lax.broadcasted_iota(jnp.int32, (rows, 128), 1)
    named_by = lax.broadcasted_iota(jnp.int32, (128, rows), 0)
    identity = (
        lax.broadcasted_iota(jnp.int32, (rows, rows), 0)
        == lax.broadcasted_iota(jnp.int32, (rows, rows), 1)
    ).astype(bf16)

    def upright(across):
        return lax.dot_general(
            identity, across.astype(bf16), (((1,), (1,)), ((), ())), preferred_element_type=f32
        )

    for name in ("ids", "route", "len", "freq", "norm_gain"):
        loads[name].wait()
    across = jnp.zeros((128, rows), f32)
    for k in range(ids_ref.shape[0]):
        across = across + jnp.where(
            named_by == ids_ref[k : k + 1, :], route_ref[k : k + 1, :].astype(f32), 0.0
        )
    dense = upright(across).astype(bf16).reshape(halves, part_rows, 128)
    wt_out[...] = dense
    wt_in[0, :, 0] = dense
    lens = upright(jnp.broadcast_to(len_ref[...].astype(f32), (128, rows)))
    held[...] = lens

    pl.semaphore_wait(barrier, 3 + 7)

    def share(d, dy):
        other = (z_of[d] * 2 + (1 - y if dy else y), head)
        return remote(("share", d, dy), wt_out, wt_in.at[dy, :, d], other)

    for d in range(4):
        for dy in range(2):
            if d or dy:
                share(d, dy).start()

    loads["tok"].wait()
    tokens = tok_ref[...].astype(f32)
    spread_of = jnp.mean(tokens * tokens, axis=-1, keepdims=True)
    scaled = tokens * lax.rsqrt(spread_of + epsilon)
    normed = jnp.concatenate(
        [
            (scaled[:, i * 128 : (i + 1) * 128] * norm_gain_ref[i : i + 1, :].astype(f32)).astype(bf16)
            for i in range(norm_gain_ref.shape[0])
        ],
        axis=1,
    )
    angles = lens[:, 0 : head_dim // 2] * freq_ref[...]
    cosine, sine = jnp.cos(angles), jnp.sin(angles)
    cosine = jnp.concatenate([cosine, cosine], axis=1)
    sine = jnp.concatenate([-sine, sine], axis=1)
    scaling = 1.0 / math.sqrt(head_dim)

    def parts_of(n):
        return slice(n * head_dim, (n + 1) * head_dim)

    loads["q"].wait()
    queries = jnp.dot(normed, q_buf[...], preferred_element_type=f32)
    turned = []
    for n in range(local_heads):
        query = queries[:, parts_of(n)]
        query = query * cosine + pltpu.roll(query, head_dim // 2, 1) * sine
        turned.append(query)
        upper = query.astype(bf16).astype(f32)
        rest = query - upper
        middle = rest.astype(bf16).astype(f32)
        for p, piece in enumerate((upper, middle, rest - middle)):
            pieces[pl.ds(3 * n + p, rows, stride=16), :] = piece
    for p in range(3 * local_heads, 16):
        pieces[pl.ds(p, rows, stride=16), :] = jnp.zeros((rows, head_dim), f32)
    loads["k"].wait()
    keys = jnp.dot(normed, k_buf[...], preferred_element_type=f32)
    own_all = jnp.zeros((rows, 128), f32)
    for n in range(local_heads):
        key = keys[:, parts_of(n)]
        key = key * cosine + pltpu.roll(key, head_dim // 2, 1) * sine
        own_all = jnp.where(
            lane == n, jnp.sum(turned[n] * key, axis=-1, keepdims=True) * scaling, own_all
        )
    own_score[...] = own_all
    loads["v"].wait()
    own_value[...] = (
        jnp.dot(normed, v_buf[...], preferred_element_type=f32).astype(bf16).astype(f32)
    )

    row16 = lax.broadcasted_iota(jnp.int32, (16, slab), 0)
    owner16 = lax.broadcasted_iota(jnp.int32, (16, slab), 1) // cache_len
    of_head = (row16 >= owner16 * 3) & (row16 < owner16 * 3 + 3)
    diagonal = row16 == owner16
    position = lax.broadcasted_iota(jnp.int32, (batch, cache_len), 1)

    def attend(i):
        for copy in cached(i):
            copy.wait()
        first = pl.multiple_of(i * batch, batch)
        for r in range(batch):
            query = pieces[pl.ds(pl.multiple_of((first + r) * 16, 16), 16), :].astype(bf16)
            found = lax.dot_general(
                query, kc_buf[i, r], (((1,), (1,)), ((), ())), preferred_element_type=f32
            )
            score[r : r + 1, :] = jnp.sum(
                jnp.where(of_head, found, 0.0), axis=0, keepdims=True
            )
        members = pl.ds(first, batch)
        inside = position.astype(f32) < held[members, 0:1]
        own_block = own_score[members, :]
        chances, own_chances = [], []
        for n in range(local_heads):
            values = score[:, n * cache_len : (n + 1) * cache_len] * scaling
            values = jnp.where(inside, values, -1e30)
            own_one = own_block[:, n : n + 1]
            largest = jnp.maximum(jnp.max(values, axis=-1, keepdims=True), own_one)
            terms = jnp.exp(values - largest)
            own_term = jnp.exp(own_one - largest)
            totals = jnp.sum(terms, axis=-1, keepdims=True) + own_term
            chances.append(terms / totals)
            own_chances.append((own_term / totals).astype(bf16).astype(f32))
        chance = jnp.concatenate(chances, axis=1)
        for r in range(batch):
            spread_out = jnp.where(
                diagonal, jnp.broadcast_to(chance[r : r + 1, :], (16, slab)), 0.0
            ).astype(bf16)
            found = jnp.dot(spread_out, vc_buf[i, r], preferred_element_type=f32)
            mixed[r * 8 : (r + 1) * 8, :] = found[0:8, :]
        for n in range(local_heads):
            attn_buf[members, parts_of(n)] = (
                mixed[pl.ds(n, batch, stride=8), :] + own_chances[n] * own_value[members, parts_of(n)]
            )

    def attention(h):
        for i in range(h * per_half, (h + 1) * per_half):
            attend(i)

    def mine(h):
        return slice(h * part_rows, (h + 1) * part_rows)

    def project(h):
        if h == 0:
            loads["o"].wait()
        attn = attn_buf[mine(h), :].astype(bf16)
        for at, (dx, dc) in enumerate(((1, 0), (1, 1), (0, 1))):
            rs_out[h, at] = jnp.dot(
                attn, o_buf[:, lanes(dx, dc)], preferred_element_type=f32
            ).astype(bf16)
            remote(
                ("sum", h, at), rs_out.at[h, at], rs_in.at[h, at], (req, quarters[dx, dc])
            ).start()
        own_f32[mine(h), :] = tok_ref[mine(h), lanes(0, 0)].astype(f32) + jnp.dot(
            attn, o_buf[:, lanes(0, 0)], preferred_element_type=f32
        )

    def zrows(first, count=1):
        return pl.ds(first * part_rows, count * part_rows)

    def line(h, d):
        return remote(
            ("line", h, d), gath.at[0, 0, h, zrows(0)], gath.at[0, 0, h, zrows(d)], z_peer(d)
        )

    spans = [(0, 1), (1, zs - 1), (0, zs)]

    def to_first(h, which):
        span = zrows(*spans[which])
        return remote(
            ("first", h, which), gath.at[0, 0, h, span], gath.at[0, 2, h, span], first_peer
        )

    def to_second(h, f, which):
        span = zrows(*spans[which])
        return remote(
            ("second", h, f, which),
            gath.at[0, 2 * f, h, span], gath.at[0, 2 * f + 1, h, span], second_peer,
        )

    def to_core(h, role, which):
        span = zrows(*spans[which])
        return remote(
            ("core", h, role, which),
            gath.at[0, role, h, span], gath.at[1, role, h, span], core_peer,
        )

    def own(h):
        for at in range(3):
            remote(("sum", h, at), None, None, None).wait_recv()
        total = own_f32[mine(h), :]
        for at in range(3):
            total = total + rs_in[h, at].astype(f32)
        rounded = total.astype(bf16)
        gath[0, 0, h, zrows(0), :] = rounded
        for d in (2, 3, 1):
            line(h, d).start()
        to_first(h, 0).start()
        to_second(h, 0, 0).start()
        to_core(h, 0, 0).start()
        own_buf[mine(h), :] = rounded

    def lined(h):
        for d in (1, 2, 3):
            line(h, d).wait_recv()
        to_first(h, 1).start()
        to_second(h, 0, 1).start()
        to_core(h, 0, 1).start()

    def firsts(h):
        for which in (0, 1):
            to_first(h, which).wait_recv()
        to_second(h, 1, 2).start()
        to_core(h, 2, 2).start()

    def seconds(h, f):
        for which in ((2,) if f else (0, 1)):
            to_second(h, f, which).wait_recv()
        to_core(h, 2 * f + 1, 2).start()

    def ready(h):
        for role, which in ((0, 0), (0, 1), (2, 2), (1, 2), (3, 2)):
            to_core(h, role, which).wait_recv()

    def role(dx, dc, dy):
        return other_role(dx, dy) if dc else own_role(dx, dy)

    def arrived(h, dx, dc):
        return jnp.concatenate(
            [gath[dc, role(dx, dc, dy), h] for dy in range(2)], axis=0
        ).astype(f32)

    def half(h):
        return remote(("half", h), part.at[1, :, h], core_in.at[:, h], core_peer)

    def compute(h):
        order = [(0, 0), (0, 1), (1, 0), (1, 1)]
        count = 2 * line_rows
        squares = jnp.zeros((count, 1), f32)
        for dx, dc in order:
            v = arrived(h, dx, dc)
            squares = squares + jnp.sum(v * v, axis=-1, keepdims=True)
        inverse = lax.rsqrt(squares * (1.0 / (4 * width)) + epsilon)
        gates = [jnp.zeros((count, gate_buf.shape[2]), f32) for _ in range(experts)]
        ups = [jnp.zeros((count, gate_buf.shape[2]), f32) for _ in range(experts)]
        for dx, dc in order:
            v = arrived(h, dx, dc)
            gain = jnp.concatenate(
                [
                    gain_f32[pl.ds(quarters[dx, dc] * (width // 128) + i, 1), :]
                    for i in range(width // 128)
                ],
                axis=1,
            )
            v = (v * inverse * gain).astype(bf16)
            depth = lanes(dx, dc)
            for e in range(experts):
                gates[e] = gates[e] + jnp.dot(v, gate_buf[e, depth, :], preferred_element_type=f32)
                ups[e] = ups[e] + jnp.dot(v, up_buf[e, depth, :], preferred_element_type=f32)
        hidden = [(g / (1.0 + jnp.exp(-g)) * u).astype(bf16) for g, u in zip(gates, ups)]
        dense_wt = jnp.concatenate(
            [wt_in[dy, h].reshape(line_rows, 128) for dy in range(2)], axis=0
        ).astype(f32)
        column = lax.broadcasted_iota(jnp.int32, (count, 128), 1)
        wt = [
            jnp.sum(jnp.where(column == req * experts + e, dense_wt, 0.0), axis=-1, keepdims=True)
            for e in range(experts)
        ]
        for dx, dc in ((1, 1), (0, 1), (1, 0), (0, 0)):
            value = jnp.zeros((count, width), f32)
            for e in range(experts):
                value = value + wt[e] * jnp.dot(
                    hidden[e], down_buf[e, :, lanes(dx, dc)], preferred_element_type=f32
                )
            value = value.astype(bf16)
            for dy in range(2):
                part[dc, role(dx, dc, dy), h] = value[dy * line_rows : (dy + 1) * line_rows]
            if (dx, dc) == (0, 1):
                half(h).start()

    def back_second(h, f):
        return remote(("back_second", h, f), s_out.at[f, h], s_in.at[f, h], second_peer)

    def back_first(h):
        return remote(("back_first", h), f_out.at[h], f_in.at[h], first_peer)

    def back_line(h, d):
        return remote(
            ("back_line", h, d), z_out.at[h, zrows(d)], lines_hbm.at[h, d], z_peer(d)
        )

    def both(h, role):
        return part[0, role, h].astype(f32) + core_in[role, h].astype(f32)

    def send_second(h, f):
        s_out[f, h] = both(h, 2 * f + 1).astype(bf16)
        back_second(h, f).start()

    def halved(h):
        half(h).wait_recv()
        for f in (1, 0):
            s_out[f, h] = both(h, 2 * f + 1).astype(bf16)
            back_second(h, f).start()

    def quartered(h):
        back_second(h, 1).wait_recv()
        f_out[h] = (both(h, 2) + s_in[1, h].astype(f32)).astype(bf16)
        back_first(h).start()

    kept = []

    def finished(h):
        back_second(h, 0).wait_recv()
        back_first(h).wait_recv()
        z_out[h] = (both(h, 0) + s_in[0, h].astype(f32) + f_in[h].astype(f32)).astype(bf16)
        for d in (2, 3, 1):
            back_line(h, d).start()
        copy = pltpu.make_async_copy(z_out.at[h, zrows(0)], lines_hbm.at[h, 0], local_sem.at[h])
        copy.start()
        kept.append(copy)

    def store_attended():
        copy = pltpu.make_async_copy(own_buf, attended_hbm, local_sem.at[halves])
        copy.start()
        kept.append(copy)

    def weights():
        for name in ("gain", "gate", "up", "down"):
            loads[name].wait()
        gain_f32[...] = gain_ref[...].astype(f32)
        for d in range(4):
            for dy in range(2):
                if d or dy:
                    share(d, dy).wait_recv()

    steps = {
        "attention": attention, "project": project, "own": own, "lined": lined,
        "firsts": firsts, "seconds": seconds, "ready": ready, "compute": compute,
        "halved": halved, "quartered": quartered, "finished": finished,
        "store": store_attended, "weights": weights,
    }
    for name, *where in plan(halves):
        steps[name](*where)

    for h in range(halves):
        for d in (1, 2, 3):
            back_line(h, d).wait_recv()
    for copy in kept:
        copy.wait()
    for copy in sends.values():
        copy.wait_send()


def plan(parts):
    times = []
    chain = [
        ("own", 2.6), ("lined", 3.0), ("firsts", 2.6), ("seconds0", 0.1), ("seconds1", 3.0), ("ready", 1.0),
        ("compute", 0.0), ("halved", 2.0), ("quartered", 3.0), ("finished", 3.0),
    ]
    for h in range(parts):
        at = 4.5 + 1.3 * h
        times.append((at, ("attention", h)))
        times.append((at + 0.1, ("project", h)))
        at = 6.0 + LAG * h
        for name, after in chain:
            at += after
            step = (name[:-1], h, int(name[-1])) if name[-1].isdigit() else (name, h)
            times.append((at, step))
        if h == 0:
            first = [t for t, s in times if s == ("ready", 0)][0]
            times.append((first - 0.01, ("weights",)))
        if h == parts - 1:
            last = [t for t, s in times if s == ("own", h)][0]
            times.append((last + 0.01, ("store",)))
    return [step for _, step in sorted(times, key=lambda pair: pair[0])]


LAG = 2.0


def finish_kernel(attended_ref, lines_ref, attended_out, expert_out):
    attended_out[...] = attended_ref[...]
    halves, zs, part_rows = lines_ref.shape[:3]
    for h in range(halves):
        total = lines_ref[h, 0].astype(jnp.float32)
        for d in range(1, zs):
            total = total + lines_ref[h, d].astype(jnp.float32)
        expert_out[h * part_rows : (h + 1) * part_rows, :] = total.astype(expert_out.dtype)


def planes_body(
    tokens, attn_gain, q_weight, k_weight, v_weight, o_weight, k_cache, v_cache, lengths,
    moe_gain, gate_weight, up_weight, down_weight, expert_ids, route_weights,
):
    rows, model_width = tokens.shape
    local_heads, cache_len, head_dim = k_cache.shape[1:]
    slab = local_heads * cache_len
    width = model_width // 4
    batch = 16
    groups = rows // batch
    halves = 4
    zs = 4
    part_rows = rows // halves
    line_rows = zs * part_rows
    bf16, f32 = jnp.bfloat16, jnp.float32
    half_dim = head_dim // 2
    frequency = np.power(rope_base, np.arange(half_dim) * (-2.0 / head_dim)).astype(np.float32)
    vmem = pl.BlockSpec(memory_space=pltpu.VMEM)
    hbm = pl.BlockSpec(memory_space=pl.ANY)
    dma = pltpu.SemaphoreType.DMA
    top = expert_ids.shape[1]
    attended, lines = pl.pallas_call(
        decode_kernel,
        out_shape=(
            jax.ShapeDtypeStruct((rows, width), bf16),
            jax.ShapeDtypeStruct((halves, zs, part_rows, width), bf16),
        ),
        in_specs=[hbm] * 16,
        out_specs=(hbm, hbm),
        scratch_shapes=[
            pltpu.VMEM((rows, model_width), bf16),
            pltpu.VMEM((model_width // 128, 128), bf16),
            pltpu.VMEM((model_width // 128, 128), bf16),
            pltpu.VMEM((1, half_dim), f32),
            pltpu.VMEM((1, rows), jnp.int32),
            pltpu.VMEM((top, rows), jnp.int32),
            pltpu.VMEM((top, rows), bf16),
            pltpu.VMEM(q_weight.shape, bf16),
            pltpu.VMEM(k_weight.shape, bf16),
            pltpu.VMEM(v_weight.shape, bf16),
            pltpu.VMEM((groups, batch, slab, head_dim), bf16),
            pltpu.VMEM((groups, batch, slab, head_dim), bf16),
            pltpu.VMEM(o_weight.shape, bf16),
            pltpu.VMEM(gate_weight.shape, bf16),
            pltpu.VMEM(up_weight.shape, bf16),
            pltpu.VMEM(down_weight.shape, bf16),
            pltpu.VMEM((rows * 16, head_dim), f32),
            pltpu.VMEM((batch, slab), f32),
            pltpu.VMEM((batch * 8, head_dim), f32),
            pltpu.VMEM((rows, local_heads * head_dim), f32),
            pltpu.VMEM((rows, 128), f32),
            pltpu.VMEM((rows, 128), f32),
            pltpu.VMEM((rows, local_heads * head_dim), f32),
            pltpu.VMEM((halves, part_rows, 128), bf16),
            pltpu.VMEM((2, halves, zs, part_rows, 128), bf16),
            pltpu.VMEM((model_width // 128, 128), f32),
            pltpu.VMEM((halves, 3, part_rows, width), bf16),
            pltpu.VMEM((halves, 3, part_rows, width), bf16),
            pltpu.VMEM((rows, width), f32),
            pltpu.VMEM((rows, width), bf16),
            pltpu.VMEM((2, 4, halves, line_rows, width), bf16),
            pltpu.VMEM((2, 4, halves, line_rows, width), bf16),
            pltpu.VMEM((4, halves, line_rows, width), bf16),
            pltpu.VMEM((2, halves, line_rows, width), bf16),
            pltpu.VMEM((2, halves, line_rows, width), bf16),
            pltpu.VMEM((halves, line_rows, width), bf16),
            pltpu.VMEM((halves, line_rows, width), bf16),
            pltpu.VMEM((halves, line_rows, width), bf16),
            dma((2, groups)),
            dma((16,)),
            dma((halves + 1,)),
            dma((128,)),
            dma((128,)),
        ],
        compiler_params=pltpu.CompilerParams(
            collective_id=0, has_side_effects=True, vmem_limit_bytes=58 << 20
        ),
    )(
        tokens,
        attn_gain.reshape(model_width // 128, 128),
        moe_gain.reshape(model_width // 128, 128),
        frequency.reshape(1, half_dim),
        lengths.reshape(1, rows),
        expert_ids.T,
        route_weights.T,
        q_weight,
        k_weight,
        v_weight,
        k_cache.reshape(rows, slab, head_dim),
        v_cache.reshape(rows, slab, head_dim),
        o_weight,
        gate_weight,
        up_weight,
        down_weight,
    )
    return pl.pallas_call(
        finish_kernel,
        out_shape=[jax.ShapeDtypeStruct((rows, width), bf16)] * 2,
        in_specs=[vmem, vmem],
        out_specs=[vmem, vmem],
    )(attended, lines)


def solution(mesh):
    by_planes = mesh.shape["req"] == 8 and mesh.shape["head"] == 4
    return jax.shard_map(
        planes_body if by_planes else body,
        mesh=mesh,
        in_specs=(
            P("req", None),
            P(),
            P(None, "head"),
            P(None, "head"),
            P(None, "head"),
            P("head", None),
            P("req", "head", None, None),
            P("req", "head", None, None),
            P("req"),
            P(),
            P("req", None, "head"),
            P("req", None, "head"),
            P("req", "head", None),
            P("req", None),
            P("req", None),
        ),
        out_specs=(P("req", "head"), P("req", "head")),
        check_vma=False,
    )
```

```python
import functools
import math

import jax
import jax.numpy as jnp
from jax import lax
from jax.experimental import pallas as pl
from jax.experimental.pallas import tpu as pltpu
from jax.sharding import PartitionSpec as P
import numpy as np

epsilon = 1e-05
rope_base = 10000.0


MESH = pl.DeviceIdType.MESH


def moe_kernel(
    req_count,
    tok_ref, norm_gain_ref, gain_ref, freq_ref, len_ref, ids_ref, route_ref,
    q_hbm, k_hbm, v_hbm, kc_hbm, vc_hbm, o_hbm, gate_hbm, up_hbm, down_hbm,
    attended_ref, out_ref,
    q_buf, k_buf, v_buf, kc_buf, vc_buf, o_buf, gate_buf, up_buf, down_buf,
    pieces, score, mixed, own_value, own_score, held, attn_buf, wt_out, wt_in,
    part_out, part_in, gath, part, half_in, cross_out, cross_in, home_out, home_in,
    cache_sem, weight_sem, wt_send, wt_recv, rs_send, rs_recv, ga_send, ga_recv, sib_send, sib_recv, x_send, x_recv, hm_send, hm_recv,
):
    rows, width = attended_ref.shape
    head_dim = 2 * freq_ref.shape[1]
    cache_len = kc_buf.shape[2] // (q_buf.shape[1] // head_dim)
    experts = gate_buf.shape[0]
    req = lax.axis_index("req")
    head = lax.axis_index("head")
    near = head + 1 - 2 * (head % 2)
    cross = (head + 2) % 4
    far = (near + 2) % 4
    quarter = [head, near, cross, far]
    blocks = max(1, req_count // 4)
    chunk_total = req_count // blocks
    chunk_rows = blocks * rows
    step_rows = 128

    slots, batch = kc_buf.shape[0], kc_buf.shape[1]
    groups = rows // batch
    local_heads = q_buf.shape[1] // head_dim
    sources = [q_hbm, k_hbm, v_hbm, o_hbm, gate_hbm, up_hbm, down_hbm]
    targets = [q_buf, k_buf, v_buf, o_buf, gate_buf, up_buf, down_buf]
    weights = [
        pltpu.make_async_copy(source, target, weight_sem.at[i])
        for i, (source, target) in enumerate(zip(sources, targets))
    ]

    def cached(i, at):
        span = pl.ds(i * batch, batch)
        return (
            pltpu.make_async_copy(kc_hbm.at[span], kc_buf.at[at], cache_sem.at[0, at]),
            pltpu.make_async_copy(vc_hbm.at[span], vc_buf.at[at], cache_sem.at[1, at]),
        )

    for copy in weights[:3]:
        copy.start()
    for i in range(slots):
        for copy in cached(i, i):
            copy.start()
    for copy in weights[3:]:
        copy.start()

    barrier = pltpu.get_barrier_semaphore()
    for other in (near, cross, far):
        pl.semaphore_signal(barrier, inc=1, device_id=(req, other), device_id_type=MESH)
    for step in range(1, req_count):
        pl.semaphore_signal(
            barrier, inc=1, device_id=((req + step) % req_count, head), device_id_type=MESH
        )
    pl.semaphore_wait(barrier, 3 + req_count - 1)

    def remote(source, target, send, recv, device):
        return pltpu.make_async_remote_copy(
            src_ref=source, dst_ref=target, send_sem=send, recv_sem=recv,
            device_id=device, device_id_type=MESH,
        )

    def lanes(d):
        return pl.ds(pl.multiple_of(quarter[d] * width, width), width)

    lane = lax.broadcasted_iota(jnp.int32, (rows, 128), 1)
    named_by = lax.broadcasted_iota(jnp.int32, (128, rows), 0)
    identity = (
        lax.broadcasted_iota(jnp.int32, (rows, rows), 0)
        == lax.broadcasted_iota(jnp.int32, (rows, rows), 1)
    ).astype(jnp.bfloat16)

    def upright(across):
        return lax.dot_general(
            identity, across.astype(jnp.bfloat16), (((1,), (1,)), ((), ())),
            preferred_element_type=jnp.float32,
        )

    across = jnp.zeros((128, rows), jnp.float32)
    for k in range(ids_ref.shape[0]):
        across = across + jnp.where(
            named_by == ids_ref[k : k + 1, :],
            route_ref[k : k + 1, :].astype(jnp.float32),
            0.0,
        )
    dense = upright(across).astype(jnp.bfloat16)
    wt_out[...] = dense
    wt_in[0:rows, :] = dense
    lens = upright(jnp.broadcast_to(len_ref[...].astype(jnp.float32), (128, rows)))
    held[...] = lens

    def share(s):
        return remote(
            wt_out, wt_in.at[pl.ds(s * rows, rows)], wt_send.at[s], wt_recv.at[s],
            ((req + req_count - s) % req_count, head),
        )

    for s in range(1, req_count):
        share(s).start()

    tokens = tok_ref[...].astype(jnp.float32)
    spread_of = jnp.mean(tokens * tokens, axis=-1, keepdims=True)
    normed = (tokens * lax.rsqrt(spread_of + epsilon) * norm_gain_ref[...].astype(jnp.float32)).astype(
        jnp.bfloat16
    )
    angles = lens[:, 0 : head_dim // 2] * freq_ref[...]
    cosine, sine = jnp.cos(angles), jnp.sin(angles)
    cosine = jnp.concatenate([cosine, cosine], axis=1)
    sine = jnp.concatenate([-sine, sine], axis=1)
    scaling = 1.0 / math.sqrt(head_dim)
    own_scores = []
    for i in range(3):
        weights[i].wait()
    for n in range(local_heads):
        part_of = slice(n * head_dim, (n + 1) * head_dim)
        query, key, value = [
            jnp.dot(normed, ref[:, part_of], preferred_element_type=jnp.float32)
            for ref in (q_buf, k_buf, v_buf)
        ]
        query = query * cosine + pltpu.roll(query, head_dim // 2, 1) * sine
        key = key * cosine + pltpu.roll(key, head_dim // 2, 1) * sine
        own_value[:, part_of] = value.astype(jnp.bfloat16).astype(jnp.float32)
        own_scores.append(jnp.sum(query * key, axis=-1, keepdims=True) * scaling)
        upper = query.astype(jnp.bfloat16).astype(jnp.float32)
        rest = query - upper
        middle = rest.astype(jnp.bfloat16).astype(jnp.float32)
        for p, piece in enumerate((upper, middle, rest - middle)):
            pieces[pl.ds(3 * n + p, rows, stride=16), :] = piece
    for p in range(3 * local_heads, 16):
        pieces[pl.ds(p, rows, stride=16), :] = jnp.zeros((rows, head_dim), jnp.float32)
    own_all = jnp.zeros((rows, 128), jnp.float32)
    for n in range(local_heads):
        own_all = jnp.where(lane == n, own_scores[n], own_all)
    own_score[...] = own_all

    slab = local_heads * cache_len
    row16 = lax.broadcasted_iota(jnp.int32, (16, slab), 0)
    owner16 = lax.broadcasted_iota(jnp.int32, (16, slab), 1) // cache_len
    of_head = (row16 >= owner16 * 3) & (row16 < owner16 * 3 + 3)
    diagonal = row16 == owner16
    position = lax.broadcasted_iota(jnp.int32, (batch, cache_len), 1)

    @pl.loop(0, groups)
    def _(i):
        at = i % slots
        for copy in cached(i, at):
            copy.wait()
        first = pl.multiple_of(i * batch, batch)
        for r in range(batch):
            query = pieces[pl.ds(pl.multiple_of((first + r) * 16, 16), 16), :].astype(jnp.bfloat16)
            found = lax.dot_general(
                query, kc_buf[at, r], (((1,), (1,)), ((), ())), preferred_element_type=jnp.float32
            )
            score[r : r + 1, :] = jnp.sum(
                jnp.where(of_head, found, 0.0), axis=0, keepdims=True
            )
        members = pl.ds(first, batch)
        inside = position.astype(jnp.float32) < held[members, 0:1]
        own_block = own_score[members, :]
        chances, own_chances = [], []
        for n in range(local_heads):
            values = score[:, n * cache_len : (n + 1) * cache_len] * scaling
            values = jnp.where(inside, values, -1e30)
            own_one = own_block[:, n : n + 1]
            largest = jnp.maximum(jnp.max(values, axis=-1, keepdims=True), own_one)
            terms = jnp.exp(values - largest)
            own_term = jnp.exp(own_one - largest)
            totals = jnp.sum(terms, axis=-1, keepdims=True) + own_term
            chances.append(terms / totals)
            own_chances.append((own_term / totals).astype(jnp.bfloat16).astype(jnp.float32))
        chance = jnp.concatenate(chances, axis=1)
        for r in range(batch):
            spread_out = jnp.where(
                diagonal, jnp.broadcast_to(chance[r : r + 1, :], (16, slab)), 0.0
            ).astype(jnp.bfloat16)
            found = jnp.dot(spread_out, vc_buf[at, r], preferred_element_type=jnp.float32)
            mixed[r * 8 : (r + 1) * 8, :] = found[0:8, :]
        for n in range(local_heads):
            part_of = slice(n * head_dim, (n + 1) * head_dim)
            attn_buf[members, part_of] = (
                mixed[pl.ds(n, batch, stride=8), :] + own_chances[n] * own_value[members, part_of]
            )

        @pl.when(i + slots < groups)
        def _():
            for copy in cached(i + slots, at):
                copy.start()

    weights[3].wait()
    attn = attn_buf[...].astype(jnp.bfloat16)
    rs = []
    for d in (2, 3, 1):
        part_out[d - 1] = jnp.dot(
            attn, o_buf[:, lanes(d)], preferred_element_type=jnp.float32
        ).astype(jnp.bfloat16)
        copy = remote(
            part_out.at[d - 1], part_in.at[d - 1], rs_send.at[d - 1], rs_recv.at[d - 1],
            (req, quarter[d]),
        )
        copy.start()
        rs.append(copy)
    total = tok_ref[:, lanes(0)].astype(jnp.float32) + jnp.dot(
        attn, o_buf[:, lanes(0)], preferred_element_type=jnp.float32
    )
    for copy in rs:
        copy.wait_recv()
    for d in range(3):
        total = total + part_in[d].astype(jnp.float32)
    own = total.astype(jnp.bfloat16)
    attended_ref[...] = total
    gath[0, 0:rows, :] = own

    def slot(s):
        return pl.ds(s * rows, rows)

    def spread(s):
        return remote(
            gath.at[0, slot(0)], gath.at[0, slot(s)], ga_send.at[0, s], ga_recv.at[0, s],
            ((req + req_count - s) % req_count, head),
        )

    def pass_on(d, s):
        origin, device = {1: (0, near), 2: (0, cross), 3: (2, near)}[d]
        return remote(
            gath.at[origin, slot(s)], gath.at[d, slot(s)], ga_send.at[d, s], ga_recv.at[d, s],
            (req, device),
        )

    pass_on(2, 0).start()
    order = sorted(range(1, req_count), key=lambda s: (s + blocks * 0))
    for s in order:
        spread(s).start()
    pass_on(1, 0).start()
    for copy in weights[4:]:
        copy.wait()
    for s in range(1, req_count):
        share(s).wait_recv()

    def home(s):
        return remote(
            home_out.at[slot(s)], home_in.at[slot(s)], hm_send.at[s], hm_recv.at[s],
            ((req + s) % req_count, head),
        )

    def to_near(c, which):
        span = pl.ds(c * chunk_rows, chunk_rows)
        return remote(
            part.at[2 * which + 1, span], half_in.at[which, span],
            sib_send.at[which, c], sib_recv.at[which, c], (req, near),
        )

    def to_cross(c):
        span = pl.ds(c * chunk_rows, chunk_rows)
        return remote(
            cross_out.at[span], cross_in.at[span], x_send.at[c], x_recv.at[c], (req, cross)
        )

    def compute(start):
        span = pl.ds(start, step_rows)
        squares = jnp.zeros((step_rows, 1), jnp.float32)
        for d in range(4):
            x = gath[d, span, :].astype(jnp.float32)
            squares = squares + jnp.sum(x * x, axis=-1, keepdims=True)
        inverse = lax.rsqrt(squares * (1.0 / (4 * width)) + epsilon)
        gates = [jnp.zeros((step_rows, gate_buf.shape[2]), jnp.float32) for _ in range(experts)]
        ups = [jnp.zeros((step_rows, gate_buf.shape[2]), jnp.float32) for _ in range(experts)]
        for d in range(4):
            x = gath[d, span, :].astype(jnp.float32)
            x = (x * inverse * gain_ref[:, lanes(d)].astype(jnp.float32)).astype(jnp.bfloat16)
            depth = pl.ds(pl.multiple_of(quarter[d] * width, width), width)
            for e in range(experts):
                gates[e] = gates[e] + jnp.dot(
                    x, gate_buf[e, depth, :], preferred_element_type=jnp.float32
                )
                ups[e] = ups[e] + jnp.dot(
                    x, up_buf[e, depth, :], preferred_element_type=jnp.float32
                )
        hidden = [
            (g / (1.0 + jnp.exp(-g)) * u).astype(jnp.bfloat16) for g, u in zip(gates, ups)
        ]
        dense_wt = wt_in[span, :].astype(jnp.float32)
        column = lax.broadcasted_iota(jnp.int32, (step_rows, 128), 1)
        wt = [
            jnp.sum(
                jnp.where(column == req * experts + e, dense_wt, 0.0), axis=-1, keepdims=True
            )
            for e in range(experts)
        ]
        for d in (1, 3, 2, 0):
            value = jnp.zeros((step_rows, width), jnp.float32)
            for e in range(experts):
                value = value + wt[e] * jnp.dot(
                    hidden[e], down_buf[e, :, lanes(d)], preferred_element_type=jnp.float32
                )
            part[d, span, :] = value.astype(jnp.bfloat16)

    def reduce_cross(c):
        span = pl.ds(c * chunk_rows, chunk_rows)
        to_near(c, 1).wait_recv()
        cross_out[span, :] = (
            part[2, span, :].astype(jnp.float32) + half_in[1, span, :].astype(jnp.float32)
        ).astype(jnp.bfloat16)
        to_cross(c).start()

    def reduce_home(c):
        span = pl.ds(c * chunk_rows, chunk_rows)
        to_near(c, 0).wait_recv()
        to_cross(c).wait_recv()
        home_out[span, :] = (
            part[0, span, :].astype(jnp.float32)
            + half_in[0, span, :].astype(jnp.float32)
            + cross_in[span, :].astype(jnp.float32)
        ).astype(jnp.bfloat16)
        for s in range(c * blocks, (c + 1) * blocks):
            if s:
                home(s).start()

    def forward(c):
        for s in range(c * blocks, (c + 1) * blocks):
            if s:
                spread(s).wait_recv()
                pass_on(2, s).start()
                pass_on(1, s).start()

    def forward_far(c):
        for s in range(c * blocks, (c + 1) * blocks):
            pass_on(2, s).wait_recv()
            pass_on(3, s).start()

    forward(0)
    forward(1)
    forward_far(0)
    for c in range(chunk_total):
        if c + 2 < chunk_total:
            forward(c + 2)
        if c + 1 < chunk_total:
            forward_far(c + 1)
        for s in range(c * blocks, (c + 1) * blocks):
            pass_on(1, s).wait_recv()
            pass_on(3, s).wait_recv()
        steps = chunk_rows // step_rows
        if steps == 1:
            compute(c * chunk_rows)
        else:
            @pl.loop(0, steps)
            def _(i):
                compute(pl.multiple_of(c * chunk_rows + i * step_rows, step_rows))
        to_near(c, 1).start()
        to_near(c, 0).start()
        if c:
            reduce_cross(c - 1)
        if c > 1:
            reduce_home(c - 2)
    reduce_cross(chunk_total - 1)
    if chunk_total > 1:
        reduce_home(chunk_total - 2)
    reduce_home(chunk_total - 1)
    result = home_out[0:rows, :].astype(jnp.float32)
    for s in range(1, req_count):
        home(s).wait_recv()
        result = result + home_in[s * rows : (s + 1) * rows, :].astype(jnp.float32)
    out_ref[...] = result

    for copy in rs:
        copy.wait_send()
    for s in range(req_count):
        for d in range(1, 4):
            pass_on(d, s).wait_send()
        if s:
            spread(s).wait_send()
            share(s).wait_send()
            home(s).wait_send()
    for c in range(chunk_total):
        to_near(c, 0).wait_send()
        to_near(c, 1).wait_send()
        to_cross(c).wait_send()


def round_kernel(attended_ref, expert_ref, attended_out, expert_out):
    attended_out[...] = attended_ref[...].astype(attended_out.dtype)
    expert_out[...] = expert_ref[...].astype(expert_out.dtype)


def body(
    tokens,
    attn_gain,
    q_weight,
    k_weight,
    v_weight,
    o_weight,
    k_cache,
    v_cache,
    lengths,
    moe_gain,
    gate_weight,
    up_weight,
    down_weight,
    expert_ids,
    route_weights,
):
    rows, model_width = tokens.shape
    local_heads, cache_len, head_dim = k_cache.shape[1:]
    slab = local_heads * cache_len
    req_count = lax.axis_size("req")
    width = model_width // 4
    everyone = req_count * rows
    blocks = max(1, req_count // 4)
    chunks = req_count // blocks
    batch = 16
    slots = 4 if req_count <= 8 else 1
    bf16, f32 = jnp.bfloat16, jnp.float32
    half_dim = head_dim // 2
    frequency = jnp.power(rope_base, jnp.arange(half_dim, dtype=f32) * (-2.0 / head_dim))
    vmem = pl.BlockSpec(memory_space=pltpu.VMEM)
    hbm = pl.BlockSpec(memory_space=pl.ANY)
    dma = pltpu.SemaphoreType.DMA
    attended, expert_out = pl.pallas_call(
        functools.partial(moe_kernel, req_count),
        out_shape=(
            jax.ShapeDtypeStruct((rows, width), f32),
            jax.ShapeDtypeStruct((rows, width), f32),
        ),
        in_specs=[vmem] * 7 + [hbm] * 9,
        out_specs=(vmem, vmem),
        scratch_shapes=[
            pltpu.VMEM(q_weight.shape, bf16),
            pltpu.VMEM(k_weight.shape, bf16),
            pltpu.VMEM(v_weight.shape, bf16),
            pltpu.VMEM((slots, batch, slab, head_dim), bf16),
            pltpu.VMEM((slots, batch, slab, head_dim), bf16),
            pltpu.VMEM(o_weight.shape, bf16),
            pltpu.VMEM(gate_weight.shape, bf16),
            pltpu.VMEM(up_weight.shape, bf16),
            pltpu.VMEM(down_weight.shape, bf16),
            pltpu.VMEM((rows * 16, head_dim), f32),
            pltpu.VMEM((batch, slab), f32),
            pltpu.VMEM((batch * 8, head_dim), f32),
            pltpu.VMEM((rows, local_heads * head_dim), f32),
            pltpu.VMEM((rows, 128), f32),
            pltpu.VMEM((rows, 128), f32),
            pltpu.VMEM((rows, local_heads * head_dim), f32),
            pltpu.VMEM((rows, 128), bf16),
            pltpu.VMEM((everyone, 128), bf16),
            pltpu.VMEM((3, rows, width), bf16),
            pltpu.VMEM((3, rows, width), bf16),
            pltpu.VMEM((4, everyone, width), bf16),
            pltpu.VMEM((4, everyone, width), bf16),
            pltpu.VMEM((2, everyone, width), bf16),
            pltpu.VMEM((everyone, width), bf16),
            pltpu.VMEM((everyone, width), bf16),
            pltpu.VMEM((everyone, width), bf16),
            pltpu.VMEM((everyone, width), bf16),
            dma((2, slots)),
            dma((7,)),
            dma((req_count,)),
            dma((req_count,)),
            dma((3,)),
            dma((3,)),
            dma((4, req_count)),
            dma((4, req_count)),
            dma((2, chunks)),
            dma((2, chunks)),
            dma((chunks,)),
            dma((chunks,)),
            dma((req_count,)),
            dma((req_count,)),
        ],
        compiler_params=pltpu.CompilerParams(
            collective_id=0, has_side_effects=True, vmem_limit_bytes=58 << 20
        ),
    )(
        tokens,
        attn_gain.reshape(1, model_width),
        moe_gain.reshape(1, model_width),
        frequency.reshape(1, half_dim),
        lengths.reshape(1, rows),
        expert_ids.T,
        route_weights.T,
        q_weight,
        k_weight,
        v_weight,
        k_cache.reshape(rows, slab, head_dim),
        v_cache.reshape(rows, slab, head_dim),
        o_weight,
        gate_weight,
        up_weight,
        down_weight,
    )
    return pl.pallas_call(
        round_kernel,
        out_shape=[jax.ShapeDtypeStruct((rows, width), bf16)] * 2,
        in_specs=[vmem, vmem],
        out_specs=[vmem, vmem],
    )(attended, expert_out)


def decode_kernel(
    tok_hbm, norm_gain_hbm, gain_hbm, freq_hbm, len_hbm, ids_hbm, route_hbm,
    q_hbm, k_hbm, v_hbm, kc_hbm, vc_hbm, o_hbm, gate_hbm, up_hbm, down_hbm,
    attended_hbm, lines_hbm,
    tok_ref, norm_gain_ref, gain_ref, freq_ref, len_ref, ids_ref, route_ref,
    q_buf, k_buf, v_buf, kc_buf, vc_buf, o_buf, gate_buf, up_buf, down_buf,
    pieces, score, mixed, own_value, own_score, held, attn_buf, wt_out, wt_in, gain_f32,
    rs_out, rs_in, own_f32, own_buf, gath, part, core_in, s_out, s_in, f_out, f_in, z_out,
    cache_sem, load_sem, local_sem, send_sem, recv_sem,
):
    rows = tok_ref.shape[0]
    width = attended_hbm.shape[1]
    halves = gath.shape[2]
    part_rows = rows // halves
    line_rows = gath.shape[3]
    zs = line_rows // part_rows
    head_dim = 2 * freq_ref.shape[1]
    experts = gate_buf.shape[0]
    local_heads = q_buf.shape[1] // head_dim
    cache_len = kc_buf.shape[2] // local_heads
    groups, batch = kc_buf.shape[0], kc_buf.shape[1]
    slab = local_heads * cache_len
    bf16, f32 = jnp.bfloat16, jnp.float32

    req = lax.axis_index("req")
    head = lax.axis_index("head")
    z, y = req // 2, req % 2
    x, c = head // 2, head % 2
    near = head + 1 - 2 * c
    cross = (head + 2) % 4
    far = (near + 2) % 4
    z_of = [z, z + 1 - 2 * (z % 2), (z + 2) % 4, 3 - z]
    first_peer = (req + (1 - c) * (1 - 2 * y), head + c * (2 - 4 * x))
    second_peer = (req + c * (1 - 2 * y), head + (1 - c) * (2 - 4 * x))
    core_peer = (req, near)
    corner_peer = (req + 1 - 2 * y, cross)

    def z_peer(d):
        return (z_of[d] * 2 + y, head)

    def own_role(dx, dy):
        return [[0, 2 - c], [1 + c, 3]][dx][dy]

    def other_role(dx, dy):
        return [[0, 1 + c], [2 - c, 3]][dx][dy]

    quarters = {(0, 0): head, (0, 1): near, (1, 0): cross, (1, 1): far}

    def lanes(dx, dc):
        return pl.ds(pl.multiple_of(quarters[dx, dc] * width, width), width)

    loads = {}

    def load(name, source, target):
        copy = pltpu.make_async_copy(source, target, load_sem.at[len(loads)])
        loads[name] = copy
        copy.start()

    def cached(i):
        span = pl.ds(i * batch, batch)
        return (
            pltpu.make_async_copy(kc_hbm.at[span], kc_buf.at[i], cache_sem.at[0, i]),
            pltpu.make_async_copy(vc_hbm.at[span], vc_buf.at[i], cache_sem.at[1, i]),
        )

    load("ids", ids_hbm, ids_ref)
    load("route", route_hbm, route_ref)
    load("len", len_hbm, len_ref)
    load("freq", freq_hbm, freq_ref)
    load("norm_gain", norm_gain_hbm, norm_gain_ref)
    load("tok", tok_hbm, tok_ref)
    load("q", q_hbm, q_buf)
    load("k", k_hbm, k_buf)
    load("v", v_hbm, v_buf)
    per_half = groups // halves
    for i in range(groups):
        for copy in cached(i):
            copy.start()
        if i == 0:
            load("o", o_hbm, o_buf)
    load("gain", gain_hbm, gain_ref)
    load("gate", gate_hbm, gate_buf)
    load("up", up_hbm, up_buf)
    load("down", down_hbm, down_buf)

    barrier = pltpu.get_barrier_semaphore()
    for other in (near, cross, far):
        pl.semaphore_signal(barrier, inc=1, device_id=(req, other), device_id_type=MESH)
    pl.semaphore_signal(barrier, inc=1, device_id=corner_peer, device_id_type=MESH)
    for d in range(4):
        for dy in range(2):
            if d or dy:
                other = z_of[d] * 2 + (1 - y if dy else y)
                pl.semaphore_signal(barrier, inc=1, device_id=(other, head), device_id_type=MESH)

    sends = {}

    def remote(key, source, target, device):
        if key not in sends:
            at = len(sends)
            sends[key] = pltpu.make_async_remote_copy(
                src_ref=source, dst_ref=target, send_sem=send_sem.at[at], recv_sem=recv_sem.at[at],
                device_id=device, device_id_type=MESH,
            )
        return sends[key]

    lane = lax.broadcasted_iota(jnp.int32, (rows, 128), 1)
    named_by = lax.broadcasted_iota(jnp.int32, (128, rows), 0)
    identity = (
        lax.broadcasted_iota(jnp.int32, (rows, rows), 0)
        == lax.broadcasted_iota(jnp.int32, (rows, rows), 1)
    ).astype(bf16)

    def upright(across):
        return lax.dot_general(
            identity, across.astype(bf16), (((1,), (1,)), ((), ())), preferred_element_type=f32
        )

    for name in ("ids", "route", "len", "freq", "norm_gain"):
        loads[name].wait()
    across = jnp.zeros((128, rows), f32)
    for k in range(ids_ref.shape[0]):
        across = across + jnp.where(
            named_by == ids_ref[k : k + 1, :], route_ref[k : k + 1, :].astype(f32), 0.0
        )
    dense = upright(across).astype(bf16).reshape(halves, part_rows, 128)
    wt_out[...] = dense
    wt_in[0, :, 0] = dense
    lens = upright(jnp.broadcast_to(len_ref[...].astype(f32), (128, rows)))
    held[...] = lens

    pl.semaphore_wait(barrier, 4 + 7)

    def share(d, dy):
        other = (z_of[d] * 2 + (1 - y if dy else y), head)
        return remote(("share", d, dy), wt_out, wt_in.at[dy, :, d], other)

    for d in range(4):
        for dy in range(2):
            if d or dy:
                share(d, dy).start()

    loads["tok"].wait()
    tokens = tok_ref[...].astype(f32)
    spread_of = jnp.mean(tokens * tokens, axis=-1, keepdims=True)
    scaled = tokens * lax.rsqrt(spread_of + epsilon)
    normed = jnp.concatenate(
        [
            (scaled[:, i * 128 : (i + 1) * 128] * norm_gain_ref[i : i + 1, :].astype(f32)).astype(bf16)
            for i in range(norm_gain_ref.shape[0])
        ],
        axis=1,
    )
    angles = lens[:, 0 : head_dim // 2] * freq_ref[...]
    cosine, sine = jnp.cos(angles), jnp.sin(angles)
    cosine = jnp.concatenate([cosine, cosine], axis=1)
    sine = jnp.concatenate([-sine, sine], axis=1)
    scaling = 1.0 / math.sqrt(head_dim)

    def parts_of(n):
        return slice(n * head_dim, (n + 1) * head_dim)

    loads["q"].wait()
    queries = jnp.dot(normed, q_buf[...], preferred_element_type=f32)
    turned = []
    for n in range(local_heads):
        query = queries[:, parts_of(n)]
        query = query * cosine + pltpu.roll(query, head_dim // 2, 1) * sine
        turned.append(query)
        upper = query.astype(bf16).astype(f32)
        rest = query - upper
        middle = rest.astype(bf16).astype(f32)
        for p, piece in enumerate((upper, middle, rest - middle)):
            pieces[pl.ds(3 * n + p, rows, stride=16), :] = piece
    for p in range(3 * local_heads, 16):
        pieces[pl.ds(p, rows, stride=16), :] = jnp.zeros((rows, head_dim), f32)
    loads["k"].wait()
    keys = jnp.dot(normed, k_buf[...], preferred_element_type=f32)
    own_all = jnp.zeros((rows, 128), f32)
    for n in range(local_heads):
        key = keys[:, parts_of(n)]
        key = key * cosine + pltpu.roll(key, head_dim // 2, 1) * sine
        own_all = jnp.where(
            lane == n, jnp.sum(turned[n] * key, axis=-1, keepdims=True) * scaling, own_all
        )
    own_score[...] = own_all
    loads["v"].wait()
    own_value[...] = (
        jnp.dot(normed, v_buf[...], preferred_element_type=f32).astype(bf16).astype(f32)
    )

    row16 = lax.broadcasted_iota(jnp.int32, (16, slab), 0)
    owner16 = lax.broadcasted_iota(jnp.int32, (16, slab), 1) // cache_len
    of_head = (row16 >= owner16 * 3) & (row16 < owner16 * 3 + 3)
    diagonal = row16 == owner16
    position = lax.broadcasted_iota(jnp.int32, (batch, cache_len), 1)

    def attend(i):
        for copy in cached(i):
            copy.wait()
        first = pl.multiple_of(i * batch, batch)
        for r in range(batch):
            query = pieces[pl.ds(pl.multiple_of((first + r) * 16, 16), 16), :].astype(bf16)
            found = lax.dot_general(
                query, kc_buf[i, r], (((1,), (1,)), ((), ())), preferred_element_type=f32
            )
            score[r : r + 1, :] = jnp.sum(
                jnp.where(of_head, found, 0.0), axis=0, keepdims=True
            )
        members = pl.ds(first, batch)
        inside = position.astype(f32) < held[members, 0:1]
        own_block = own_score[members, :]
        chances, own_chances = [], []
        for n in range(local_heads):
            values = score[:, n * cache_len : (n + 1) * cache_len] * scaling
            values = jnp.where(inside, values, -1e30)
            own_one = own_block[:, n : n + 1]
            largest = jnp.maximum(jnp.max(values, axis=-1, keepdims=True), own_one)
            terms = jnp.exp(values - largest)
            own_term = jnp.exp(own_one - largest)
            totals = jnp.sum(terms, axis=-1, keepdims=True) + own_term
            chances.append(terms / totals)
            own_chances.append((own_term / totals).astype(bf16).astype(f32))
        chance = jnp.concatenate(chances, axis=1)
        for r in range(batch):
            spread_out = jnp.where(
                diagonal, jnp.broadcast_to(chance[r : r + 1, :], (16, slab)), 0.0
            ).astype(bf16)
            found = jnp.dot(spread_out, vc_buf[i, r], preferred_element_type=f32)
            mixed[r * 8 : (r + 1) * 8, :] = found[0:8, :]
        for n in range(local_heads):
            attn_buf[members, parts_of(n)] = (
                mixed[pl.ds(n, batch, stride=8), :] + own_chances[n] * own_value[members, parts_of(n)]
            )

    def attention(h):
        for i in range(h * per_half, (h + 1) * per_half):
            attend(i)

    def mine(h):
        return slice(h * part_rows, (h + 1) * part_rows)

    def project(h):
        if h == 0:
            loads["o"].wait()
        attn = attn_buf[mine(h), :].astype(bf16)
        for at, (dx, dc) in enumerate(((1, 0), (1, 1), (0, 1))):
            rs_out[h, at] = jnp.dot(
                attn, o_buf[:, lanes(dx, dc)], preferred_element_type=f32
            ).astype(bf16)
            remote(
                ("sum", h, at), rs_out.at[h, at], rs_in.at[h, at], (req, quarters[dx, dc])
            ).start()
        own_f32[mine(h), :] = tok_ref[mine(h), lanes(0, 0)].astype(f32) + jnp.dot(
            attn, o_buf[:, lanes(0, 0)], preferred_element_type=f32
        )

    def zrows(first, count=1):
        return pl.ds(first * part_rows, count * part_rows)

    def line(h, d):
        return remote(
            ("line", h, d), gath.at[0, 0, h, zrows(0)], gath.at[0, 0, h, zrows(d)], z_peer(d)
        )

    spans = [(0, 1), (1, zs - 1), (0, zs)]

    def to_first(h, which):
        span = zrows(*spans[which])
        return remote(
            ("first", h, which), gath.at[0, 0, h, span], gath.at[0, 2, h, span], first_peer
        )

    def to_second(h, f, which):
        span = zrows(*spans[which])
        return remote(
            ("second", h, f, which),
            gath.at[0, 2 * f, h, span], gath.at[0, 2 * f + 1, h, span], second_peer,
        )

    def to_corner(h, which):
        span = zrows(*spans[which])
        return remote(
            ("corner", h, which), gath.at[0, 0, h, span], gath.at[0, 3, h, span], corner_peer
        )

    def to_core(h, role, which):
        span = zrows(*spans[which])
        return remote(
            ("core", h, role, which),
            gath.at[0, role, h, span], gath.at[1, role, h, span], core_peer,
        )

    def own(h):
        for at in range(3):
            remote(("sum", h, at), None, None, None).wait_recv()
        total = own_f32[mine(h), :]
        for at in range(3):
            total = total + rs_in[h, at].astype(f32)
        rounded = total.astype(bf16)
        gath[0, 0, h, zrows(0), :] = rounded
        for d in (2, 3, 1):
            line(h, d).start()
        if GATHER[h]:
            to_corner(h, 0).start()
        to_first(h, 0).start()
        to_second(h, 0, 0).start()
        to_core(h, 0, 0).start()
        own_buf[mine(h), :] = rounded

    def lined(h):
        for d in (1, 2, 3):
            line(h, d).wait_recv()
        if GATHER[h]:
            to_corner(h, 1).start()
        to_first(h, 1).start()
        to_second(h, 0, 1).start()
        to_core(h, 0, 1).start()

    def firsts(h):
        for which in (0, 1):
            to_first(h, which).wait_recv()
        if not GATHER[h]:
            to_second(h, 1, 2).start()
        to_core(h, 2, 2).start()

    def seconds(h, f):
        if f and GATHER[h]:
            for which in (0, 1):
                to_corner(h, which).wait_recv()
        else:
            for which in ((2,) if f else (0, 1)):
                to_second(h, f, which).wait_recv()
        to_core(h, 2 * f + 1, 2).start()

    def ready(h):
        for role, which in ((0, 0), (0, 1), (2, 2), (1, 2), (3, 2)):
            to_core(h, role, which).wait_recv()

    def role(dx, dc, dy):
        return other_role(dx, dy) if dc else own_role(dx, dy)

    def arrived(h, dx, dc):
        return jnp.concatenate(
            [gath[dc, role(dx, dc, dy), h] for dy in range(2)], axis=0
        ).astype(f32)

    def half(h):
        return remote(("half", h), part.at[1, :, h], core_in.at[:, h], core_peer)

    def compute(h):
        order = [(0, 0), (0, 1), (1, 0), (1, 1)]
        count = 2 * line_rows
        squares = jnp.zeros((count, 1), f32)
        for dx, dc in order:
            v = arrived(h, dx, dc)
            squares = squares + jnp.sum(v * v, axis=-1, keepdims=True)
        inverse = lax.rsqrt(squares * (1.0 / (4 * width)) + epsilon)
        gates = [jnp.zeros((count, gate_buf.shape[2]), f32) for _ in range(experts)]
        ups = [jnp.zeros((count, gate_buf.shape[2]), f32) for _ in range(experts)]
        for dx, dc in order:
            v = arrived(h, dx, dc)
            gain = jnp.concatenate(
                [
                    gain_f32[pl.ds(quarters[dx, dc] * (width // 128) + i, 1), :]
                    for i in range(width // 128)
                ],
                axis=1,
            )
            v = (v * inverse * gain).astype(bf16)
            depth = lanes(dx, dc)
            for e in range(experts):
                gates[e] = gates[e] + jnp.dot(v, gate_buf[e, depth, :], preferred_element_type=f32)
                ups[e] = ups[e] + jnp.dot(v, up_buf[e, depth, :], preferred_element_type=f32)
        hidden = [(g / (1.0 + jnp.exp(-g)) * u).astype(bf16) for g, u in zip(gates, ups)]
        dense_wt = jnp.concatenate(
            [wt_in[dy, h].reshape(line_rows, 128) for dy in range(2)], axis=0
        ).astype(f32)
        column = lax.broadcasted_iota(jnp.int32, (count, 128), 1)
        wt = [
            jnp.sum(jnp.where(column == req * experts + e, dense_wt, 0.0), axis=-1, keepdims=True)
            for e in range(experts)
        ]
        for dx, dc in ((1, 1), (0, 1), (1, 0), (0, 0)):
            value = jnp.zeros((count, width), f32)
            for e in range(experts):
                value = value + wt[e] * jnp.dot(
                    hidden[e], down_buf[e, :, lanes(dx, dc)], preferred_element_type=f32
                )
            value = value.astype(bf16)
            for dy in range(2):
                part[dc, role(dx, dc, dy), h] = value[dy * line_rows : (dy + 1) * line_rows]
            if (dx, dc) == (0, 1):
                half(h).start()

    def back_second(h, f):
        return remote(("back_second", h, f), s_out.at[f, h], s_in.at[f, h], second_peer)

    def back_corner(h):
        return remote(("back_corner", h), s_out.at[1, h], s_in.at[1, h], corner_peer)

    def back_first(h):
        return remote(("back_first", h), f_out.at[h], f_in.at[h], first_peer)

    def back_line(h, d):
        return remote(
            ("back_line", h, d), z_out.at[h, zrows(d)], lines_hbm.at[h, d], z_peer(d)
        )

    def both(h, role):
        return part[0, role, h].astype(f32) + core_in[role, h].astype(f32)

    def send_second(h, f):
        s_out[f, h] = both(h, 2 * f + 1).astype(bf16)
        back_second(h, f).start()

    def halved(h):
        half(h).wait_recv()
        for f in (1, 0):
            s_out[f, h] = both(h, 2 * f + 1).astype(bf16)
            (back_corner(h) if f and RETURN[h] else back_second(h, f)).start()
        if RETURN[h]:
            f_out[h] = both(h, 2).astype(bf16)
            back_first(h).start()

    def quartered(h):
        if RETURN[h]:
            return
        back_second(h, 1).wait_recv()
        f_out[h] = (both(h, 2) + s_in[1, h].astype(f32)).astype(bf16)
        back_first(h).start()

    kept = []

    def finished(h):
        back_second(h, 0).wait_recv()
        back_first(h).wait_recv()
        total = both(h, 0) + s_in[0, h].astype(f32) + f_in[h].astype(f32)
        if RETURN[h]:
            back_corner(h).wait_recv()
            total = total + s_in[1, h].astype(f32)
        z_out[h] = total.astype(bf16)
        for d in (2, 3, 1):
            back_line(h, d).start()
        copy = pltpu.make_async_copy(z_out.at[h, zrows(0)], lines_hbm.at[h, 0], local_sem.at[h])
        copy.start()
        kept.append(copy)

    def store_attended():
        copy = pltpu.make_async_copy(own_buf, attended_hbm, local_sem.at[halves])
        copy.start()
        kept.append(copy)

    def weights():
        for name in ("gain", "gate", "up", "down"):
            loads[name].wait()
        gain_f32[...] = gain_ref[...].astype(f32)
        for d in range(4):
            for dy in range(2):
                if d or dy:
                    share(d, dy).wait_recv()

    steps = {
        "attention": attention, "project": project, "own": own, "lined": lined,
        "firsts": firsts, "seconds": seconds, "ready": ready, "compute": compute,
        "halved": halved, "quartered": quartered, "finished": finished,
        "store": store_attended, "weights": weights,
    }
    for name, *where in SCHEDULE:
        steps[name](*where)

    for h in range(halves):
        for d in (1, 2, 3):
            back_line(h, d).wait_recv()
    for copy in kept:
        copy.wait()
    for copy in sends.values():
        copy.wait_send()


GATHER = (1, 1, 1, 1)
RETURN = (1, 1, 1, 1)
SCHEDULE = (
    ("attention", 0), ("project", 0), ("attention", 1), ("project", 1), ("attention", 2),
    ("own", 0), ("project", 2), ("attention", 3), ("own", 1), ("project", 3), ("lined", 0),
    ("lined", 1), ("own", 2), ("seconds", 0, 1), ("own", 3), ("store",), ("firsts", 0), ("seconds", 0, 0),
    ("lined", 2), ("lined", 3), ("seconds", 1, 1), ("firsts", 1), ("seconds", 1, 0), ("weights",), ("ready", 0),
    ("compute", 0), ("halved", 0), ("ready", 1), ("compute", 1), ("seconds", 3, 1),
    ("seconds", 2, 1), ("firsts", 2), ("seconds", 2, 0), ("halved", 1), ("ready", 2), ("compute", 2), ("firsts", 3), ("seconds", 3, 0),
    ("halved", 2), ("ready", 3), ("compute", 3), ("finished", 0), ("halved", 3), ("finished", 2),
    ("finished", 1), ("finished", 3),
)


def finish_kernel(attended_ref, lines_ref, attended_out, expert_out):
    attended_out[...] = attended_ref[...]
    halves, zs, part_rows = lines_ref.shape[:3]
    for h in range(halves):
        total = lines_ref[h, 0].astype(jnp.float32)
        for d in range(1, zs):
            total = total + lines_ref[h, d].astype(jnp.float32)
        expert_out[h * part_rows : (h + 1) * part_rows, :] = total.astype(expert_out.dtype)


def planes_body(
    tokens, attn_gain, q_weight, k_weight, v_weight, o_weight, k_cache, v_cache, lengths,
    moe_gain, gate_weight, up_weight, down_weight, expert_ids, route_weights,
):
    rows, model_width = tokens.shape
    local_heads, cache_len, head_dim = k_cache.shape[1:]
    slab = local_heads * cache_len
    width = model_width // 4
    batch = 16
    groups = rows // batch
    halves = 4
    zs = 4
    part_rows = rows // halves
    line_rows = zs * part_rows
    bf16, f32 = jnp.bfloat16, jnp.float32
    half_dim = head_dim // 2
    frequency = np.power(rope_base, np.arange(half_dim) * (-2.0 / head_dim)).astype(np.float32)
    vmem = pl.BlockSpec(memory_space=pltpu.VMEM)
    hbm = pl.BlockSpec(memory_space=pl.ANY)
    dma = pltpu.SemaphoreType.DMA
    top = expert_ids.shape[1]
    attended, lines = pl.pallas_call(
        decode_kernel,
        out_shape=(
            jax.ShapeDtypeStruct((rows, width), bf16),
            jax.ShapeDtypeStruct((halves, zs, part_rows, width), bf16),
        ),
        in_specs=[hbm] * 16,
        out_specs=(hbm, hbm),
        scratch_shapes=[
            pltpu.VMEM((rows, model_width), bf16),
            pltpu.VMEM((model_width // 128, 128), bf16),
            pltpu.VMEM((model_width // 128, 128), bf16),
            pltpu.VMEM((1, half_dim), f32),
            pltpu.VMEM((1, rows), jnp.int32),
            pltpu.VMEM((top, rows), jnp.int32),
            pltpu.VMEM((top, rows), bf16),
            pltpu.VMEM(q_weight.shape, bf16),
            pltpu.VMEM(k_weight.shape, bf16),
            pltpu.VMEM(v_weight.shape, bf16),
            pltpu.VMEM((groups, batch, slab, head_dim), bf16),
            pltpu.VMEM((groups, batch, slab, head_dim), bf16),
            pltpu.VMEM(o_weight.shape, bf16),
            pltpu.VMEM(gate_weight.shape, bf16),
            pltpu.VMEM(up_weight.shape, bf16),
            pltpu.VMEM(down_weight.shape, bf16),
            pltpu.VMEM((rows * 16, head_dim), f32),
            pltpu.VMEM((batch, slab), f32),
            pltpu.VMEM((batch * 8, head_dim), f32),
            pltpu.VMEM((rows, local_heads * head_dim), f32),
            pltpu.VMEM((rows, 128), f32),
            pltpu.VMEM((rows, 128), f32),
            pltpu.VMEM((rows, local_heads * head_dim), f32),
            pltpu.VMEM((halves, part_rows, 128), bf16),
            pltpu.VMEM((2, halves, zs, part_rows, 128), bf16),
            pltpu.VMEM((model_width // 128, 128), f32),
            pltpu.VMEM((halves, 3, part_rows, width), bf16),
            pltpu.VMEM((halves, 3, part_rows, width), bf16),
            pltpu.VMEM((rows, width), f32),
            pltpu.VMEM((rows, width), bf16),
            pltpu.VMEM((2, 4, halves, line_rows, width), bf16),
            pltpu.VMEM((2, 4, halves, line_rows, width), bf16),
            pltpu.VMEM((4, halves, line_rows, width), bf16),
            pltpu.VMEM((2, halves, line_rows, width), bf16),
            pltpu.VMEM((2, halves, line_rows, width), bf16),
            pltpu.VMEM((halves, line_rows, width), bf16),
            pltpu.VMEM((halves, line_rows, width), bf16),
            pltpu.VMEM((halves, line_rows, width), bf16),
            dma((2, groups)),
            dma((16,)),
            dma((halves + 1,)),
            dma((128,)),
            dma((128,)),
        ],
        compiler_params=pltpu.CompilerParams(
            collective_id=0, has_side_effects=True, vmem_limit_bytes=58 << 20
        ),
    )(
        tokens,
        attn_gain.reshape(model_width // 128, 128),
        moe_gain.reshape(model_width // 128, 128),
        frequency.reshape(1, half_dim),
        lengths.reshape(1, rows),
        expert_ids.T,
        route_weights.T,
        q_weight,
        k_weight,
        v_weight,
        k_cache.reshape(rows, slab, head_dim),
        v_cache.reshape(rows, slab, head_dim),
        o_weight,
        gate_weight,
        up_weight,
        down_weight,
    )
    return pl.pallas_call(
        finish_kernel,
        out_shape=[jax.ShapeDtypeStruct((rows, width), bf16)] * 2,
        in_specs=[vmem, vmem],
        out_specs=[vmem, vmem],
    )(attended, lines)


def solution(mesh):
    by_planes = mesh.shape["req"] == 8 and mesh.shape["head"] == 4
    return jax.shard_map(
        planes_body if by_planes else body,
        mesh=mesh,
        in_specs=(
            P("req", None),
            P(),
            P(None, "head"),
            P(None, "head"),
            P(None, "head"),
            P("head", None),
            P("req", "head", None, None),
            P("req", "head", None, None),
            P("req"),
            P(),
            P("req", None, "head"),
            P("req", None, "head"),
            P("req", "head", None),
            P("req", None),
            P("req", None),
        ),
        out_specs=(P("req", "head"), P("req", "head")),
        check_vma=False,
    )
```

```python
import functools
import math

import jax
import jax.numpy as jnp
from jax import lax
from jax.experimental import pallas as pl
from jax.experimental.pallas import tpu as pltpu
from jax.sharding import PartitionSpec as P
import numpy as np

epsilon = 1e-05
rope_base = 10000.0


MESH = pl.DeviceIdType.MESH


def moe_kernel(
    req_count,
    tok_ref, norm_gain_ref, gain_ref, freq_ref, len_ref, ids_ref, route_ref,
    q_hbm, k_hbm, v_hbm, kc_hbm, vc_hbm, o_hbm, gate_hbm, up_hbm, down_hbm,
    attended_ref, out_ref,
    q_buf, k_buf, v_buf, kc_buf, vc_buf, o_buf, gate_buf, up_buf, down_buf,
    pieces, score, mixed, own_value, own_score, held, attn_buf, wt_out, wt_in,
    part_out, part_in, gath, part, half_in, cross_out, cross_in, home_out, home_in,
    cache_sem, weight_sem, wt_send, wt_recv, rs_send, rs_recv, ga_send, ga_recv, sib_send, sib_recv, x_send, x_recv, hm_send, hm_recv,
):
    rows, width = attended_ref.shape
    head_dim = 2 * freq_ref.shape[1]
    cache_len = kc_buf.shape[2] // (q_buf.shape[1] // head_dim)
    experts = gate_buf.shape[0]
    req = lax.axis_index("req")
    head = lax.axis_index("head")
    near = head + 1 - 2 * (head % 2)
    cross = (head + 2) % 4
    far = (near + 2) % 4
    quarter = [head, near, cross, far]
    blocks = max(1, req_count // 4)
    chunk_total = req_count // blocks
    chunk_rows = blocks * rows
    step_rows = 128

    slots, batch = kc_buf.shape[0], kc_buf.shape[1]
    groups = rows // batch
    local_heads = q_buf.shape[1] // head_dim
    sources = [q_hbm, k_hbm, v_hbm, o_hbm, gate_hbm, up_hbm, down_hbm]
    targets = [q_buf, k_buf, v_buf, o_buf, gate_buf, up_buf, down_buf]
    weights = [
        pltpu.make_async_copy(source, target, weight_sem.at[i])
        for i, (source, target) in enumerate(zip(sources, targets))
    ]

    def cached(i, at):
        span = pl.ds(i * batch, batch)
        return (
            pltpu.make_async_copy(kc_hbm.at[span], kc_buf.at[at], cache_sem.at[0, at]),
            pltpu.make_async_copy(vc_hbm.at[span], vc_buf.at[at], cache_sem.at[1, at]),
        )

    for copy in weights[:3]:
        copy.start()
    for i in range(slots):
        for copy in cached(i, i):
            copy.start()
    for copy in weights[3:]:
        copy.start()

    barrier = pltpu.get_barrier_semaphore()
    for other in (near, cross, far):
        pl.semaphore_signal(barrier, inc=1, device_id=(req, other), device_id_type=MESH)
    for step in range(1, req_count):
        pl.semaphore_signal(
            barrier, inc=1, device_id=((req + step) % req_count, head), device_id_type=MESH
        )
    pl.semaphore_wait(barrier, 3 + req_count - 1)

    def remote(source, target, send, recv, device):
        return pltpu.make_async_remote_copy(
            src_ref=source, dst_ref=target, send_sem=send, recv_sem=recv,
            device_id=device, device_id_type=MESH,
        )

    def lanes(d):
        return pl.ds(pl.multiple_of(quarter[d] * width, width), width)

    lane = lax.broadcasted_iota(jnp.int32, (rows, 128), 1)
    named_by = lax.broadcasted_iota(jnp.int32, (128, rows), 0)
    identity = (
        lax.broadcasted_iota(jnp.int32, (rows, rows), 0)
        == lax.broadcasted_iota(jnp.int32, (rows, rows), 1)
    ).astype(jnp.bfloat16)

    def upright(across):
        return lax.dot_general(
            identity, across.astype(jnp.bfloat16), (((1,), (1,)), ((), ())),
            preferred_element_type=jnp.float32,
        )

    across = jnp.zeros((128, rows), jnp.float32)
    for k in range(ids_ref.shape[0]):
        across = across + jnp.where(
            named_by == ids_ref[k : k + 1, :],
            route_ref[k : k + 1, :].astype(jnp.float32),
            0.0,
        )
    dense = upright(across).astype(jnp.bfloat16)
    wt_out[...] = dense
    wt_in[0:rows, :] = dense
    lens = upright(jnp.broadcast_to(len_ref[...].astype(jnp.float32), (128, rows)))
    held[...] = lens

    def share(s):
        return remote(
            wt_out, wt_in.at[pl.ds(s * rows, rows)], wt_send.at[s], wt_recv.at[s],
            ((req + req_count - s) % req_count, head),
        )

    for s in range(1, req_count):
        share(s).start()

    tokens = tok_ref[...].astype(jnp.float32)
    spread_of = jnp.mean(tokens * tokens, axis=-1, keepdims=True)
    normed = (tokens * lax.rsqrt(spread_of + epsilon) * norm_gain_ref[...].astype(jnp.float32)).astype(
        jnp.bfloat16
    )
    angles = lens[:, 0 : head_dim // 2] * freq_ref[...]
    cosine, sine = jnp.cos(angles), jnp.sin(angles)
    cosine = jnp.concatenate([cosine, cosine], axis=1)
    sine = jnp.concatenate([-sine, sine], axis=1)
    scaling = 1.0 / math.sqrt(head_dim)
    own_scores = []
    for i in range(3):
        weights[i].wait()
    for n in range(local_heads):
        part_of = slice(n * head_dim, (n + 1) * head_dim)
        query, key, value = [
            jnp.dot(normed, ref[:, part_of], preferred_element_type=jnp.float32)
            for ref in (q_buf, k_buf, v_buf)
        ]
        query = query * cosine + pltpu.roll(query, head_dim // 2, 1) * sine
        key = key * cosine + pltpu.roll(key, head_dim // 2, 1) * sine
        own_value[:, part_of] = value.astype(jnp.bfloat16).astype(jnp.float32)
        own_scores.append(jnp.sum(query * key, axis=-1, keepdims=True) * scaling)
        upper = query.astype(jnp.bfloat16).astype(jnp.float32)
        rest = query - upper
        middle = rest.astype(jnp.bfloat16).astype(jnp.float32)
        for p, piece in enumerate((upper, middle, rest - middle)):
            pieces[pl.ds(3 * n + p, rows, stride=16), :] = piece
    for p in range(3 * local_heads, 16):
        pieces[pl.ds(p, rows, stride=16), :] = jnp.zeros((rows, head_dim), jnp.float32)
    own_all = jnp.zeros((rows, 128), jnp.float32)
    for n in range(local_heads):
        own_all = jnp.where(lane == n, own_scores[n], own_all)
    own_score[...] = own_all

    slab = local_heads * cache_len
    row16 = lax.broadcasted_iota(jnp.int32, (16, slab), 0)
    owner16 = lax.broadcasted_iota(jnp.int32, (16, slab), 1) // cache_len
    of_head = (row16 >= owner16 * 3) & (row16 < owner16 * 3 + 3)
    diagonal = row16 == owner16
    position = lax.broadcasted_iota(jnp.int32, (batch, cache_len), 1)

    @pl.loop(0, groups)
    def _(i):
        at = i % slots
        for copy in cached(i, at):
            copy.wait()
        first = pl.multiple_of(i * batch, batch)
        for r in range(batch):
            query = pieces[pl.ds(pl.multiple_of((first + r) * 16, 16), 16), :].astype(jnp.bfloat16)
            found = lax.dot_general(
                query, kc_buf[at, r], (((1,), (1,)), ((), ())), preferred_element_type=jnp.float32
            )
            score[r : r + 1, :] = jnp.sum(
                jnp.where(of_head, found, 0.0), axis=0, keepdims=True
            )
        members = pl.ds(first, batch)
        inside = position.astype(jnp.float32) < held[members, 0:1]
        own_block = own_score[members, :]
        chances, own_chances = [], []
        for n in range(local_heads):
            values = score[:, n * cache_len : (n + 1) * cache_len] * scaling
            values = jnp.where(inside, values, -1e30)
            own_one = own_block[:, n : n + 1]
            largest = jnp.maximum(jnp.max(values, axis=-1, keepdims=True), own_one)
            terms = jnp.exp(values - largest)
            own_term = jnp.exp(own_one - largest)
            totals = jnp.sum(terms, axis=-1, keepdims=True) + own_term
            chances.append(terms / totals)
            own_chances.append((own_term / totals).astype(jnp.bfloat16).astype(jnp.float32))
        chance = jnp.concatenate(chances, axis=1)
        for r in range(batch):
            spread_out = jnp.where(
                diagonal, jnp.broadcast_to(chance[r : r + 1, :], (16, slab)), 0.0
            ).astype(jnp.bfloat16)
            found = jnp.dot(spread_out, vc_buf[at, r], preferred_element_type=jnp.float32)
            mixed[r * 8 : (r + 1) * 8, :] = found[0:8, :]
        for n in range(local_heads):
            part_of = slice(n * head_dim, (n + 1) * head_dim)
            attn_buf[members, part_of] = (
                mixed[pl.ds(n, batch, stride=8), :] + own_chances[n] * own_value[members, part_of]
            )

        @pl.when(i + slots < groups)
        def _():
            for copy in cached(i + slots, at):
                copy.start()

    weights[3].wait()
    attn = attn_buf[...].astype(jnp.bfloat16)
    rs = []
    for d in (2, 3, 1):
        part_out[d - 1] = jnp.dot(
            attn, o_buf[:, lanes(d)], preferred_element_type=jnp.float32
        ).astype(jnp.bfloat16)
        copy = remote(
            part_out.at[d - 1], part_in.at[d - 1], rs_send.at[d - 1], rs_recv.at[d - 1],
            (req, quarter[d]),
        )
        copy.start()
        rs.append(copy)
    total = tok_ref[:, lanes(0)].astype(jnp.float32) + jnp.dot(
        attn, o_buf[:, lanes(0)], preferred_element_type=jnp.float32
    )
    for copy in rs:
        copy.wait_recv()
    for d in range(3):
        total = total + part_in[d].astype(jnp.float32)
    own = total.astype(jnp.bfloat16)
    attended_ref[...] = total
    gath[0, 0:rows, :] = own

    def slot(s):
        return pl.ds(s * rows, rows)

    def spread(s):
        return remote(
            gath.at[0, slot(0)], gath.at[0, slot(s)], ga_send.at[0, s], ga_recv.at[0, s],
            ((req + req_count - s) % req_count, head),
        )

    def pass_on(d, s):
        origin, device = {1: (0, near), 2: (0, cross), 3: (2, near)}[d]
        return remote(
            gath.at[origin, slot(s)], gath.at[d, slot(s)], ga_send.at[d, s], ga_recv.at[d, s],
            (req, device),
        )

    pass_on(2, 0).start()
    order = sorted(range(1, req_count), key=lambda s: (s + blocks * 0))
    for s in order:
        spread(s).start()
    pass_on(1, 0).start()
    for copy in weights[4:]:
        copy.wait()
    for s in range(1, req_count):
        share(s).wait_recv()

    def home(s):
        return remote(
            home_out.at[slot(s)], home_in.at[slot(s)], hm_send.at[s], hm_recv.at[s],
            ((req + s) % req_count, head),
        )

    def to_near(c, which):
        span = pl.ds(c * chunk_rows, chunk_rows)
        return remote(
            part.at[2 * which + 1, span], half_in.at[which, span],
            sib_send.at[which, c], sib_recv.at[which, c], (req, near),
        )

    def to_cross(c):
        span = pl.ds(c * chunk_rows, chunk_rows)
        return remote(
            cross_out.at[span], cross_in.at[span], x_send.at[c], x_recv.at[c], (req, cross)
        )

    def compute(start):
        span = pl.ds(start, step_rows)
        squares = jnp.zeros((step_rows, 1), jnp.float32)
        for d in range(4):
            x = gath[d, span, :].astype(jnp.float32)
            squares = squares + jnp.sum(x * x, axis=-1, keepdims=True)
        inverse = lax.rsqrt(squares * (1.0 / (4 * width)) + epsilon)
        gates = [jnp.zeros((step_rows, gate_buf.shape[2]), jnp.float32) for _ in range(experts)]
        ups = [jnp.zeros((step_rows, gate_buf.shape[2]), jnp.float32) for _ in range(experts)]
        for d in range(4):
            x = gath[d, span, :].astype(jnp.float32)
            x = (x * inverse * gain_ref[:, lanes(d)].astype(jnp.float32)).astype(jnp.bfloat16)
            depth = pl.ds(pl.multiple_of(quarter[d] * width, width), width)
            for e in range(experts):
                gates[e] = gates[e] + jnp.dot(
                    x, gate_buf[e, depth, :], preferred_element_type=jnp.float32
                )
                ups[e] = ups[e] + jnp.dot(
                    x, up_buf[e, depth, :], preferred_element_type=jnp.float32
                )
        hidden = [
            (g / (1.0 + jnp.exp(-g)) * u).astype(jnp.bfloat16) for g, u in zip(gates, ups)
        ]
        dense_wt = wt_in[span, :].astype(jnp.float32)
        column = lax.broadcasted_iota(jnp.int32, (step_rows, 128), 1)
        wt = [
            jnp.sum(
                jnp.where(column == req * experts + e, dense_wt, 0.0), axis=-1, keepdims=True
            )
            for e in range(experts)
        ]
        for d in (1, 3, 2, 0):
            value = jnp.zeros((step_rows, width), jnp.float32)
            for e in range(experts):
                value = value + wt[e] * jnp.dot(
                    hidden[e], down_buf[e, :, lanes(d)], preferred_element_type=jnp.float32
                )
            part[d, span, :] = value.astype(jnp.bfloat16)

    def reduce_cross(c):
        span = pl.ds(c * chunk_rows, chunk_rows)
        to_near(c, 1).wait_recv()
        cross_out[span, :] = (
            part[2, span, :].astype(jnp.float32) + half_in[1, span, :].astype(jnp.float32)
        ).astype(jnp.bfloat16)
        to_cross(c).start()

    def reduce_home(c):
        span = pl.ds(c * chunk_rows, chunk_rows)
        to_near(c, 0).wait_recv()
        to_cross(c).wait_recv()
        home_out[span, :] = (
            part[0, span, :].astype(jnp.float32)
            + half_in[0, span, :].astype(jnp.float32)
            + cross_in[span, :].astype(jnp.float32)
        ).astype(jnp.bfloat16)
        for s in range(c * blocks, (c + 1) * blocks):
            if s:
                home(s).start()

    def forward(c):
        for s in range(c * blocks, (c + 1) * blocks):
            if s:
                spread(s).wait_recv()
                pass_on(2, s).start()
                pass_on(1, s).start()

    def forward_far(c):
        for s in range(c * blocks, (c + 1) * blocks):
            pass_on(2, s).wait_recv()
            pass_on(3, s).start()

    forward(0)
    forward(1)
    forward_far(0)
    for c in range(chunk_total):
        if c + 2 < chunk_total:
            forward(c + 2)
        if c + 1 < chunk_total:
            forward_far(c + 1)
        for s in range(c * blocks, (c + 1) * blocks):
            pass_on(1, s).wait_recv()
            pass_on(3, s).wait_recv()
        steps = chunk_rows // step_rows
        if steps == 1:
            compute(c * chunk_rows)
        else:
            @pl.loop(0, steps)
            def _(i):
                compute(pl.multiple_of(c * chunk_rows + i * step_rows, step_rows))
        to_near(c, 1).start()
        to_near(c, 0).start()
        if c:
            reduce_cross(c - 1)
        if c > 1:
            reduce_home(c - 2)
    reduce_cross(chunk_total - 1)
    if chunk_total > 1:
        reduce_home(chunk_total - 2)
    reduce_home(chunk_total - 1)
    result = home_out[0:rows, :].astype(jnp.float32)
    for s in range(1, req_count):
        home(s).wait_recv()
        result = result + home_in[s * rows : (s + 1) * rows, :].astype(jnp.float32)
    out_ref[...] = result

    for copy in rs:
        copy.wait_send()
    for s in range(req_count):
        for d in range(1, 4):
            pass_on(d, s).wait_send()
        if s:
            spread(s).wait_send()
            share(s).wait_send()
            home(s).wait_send()
    for c in range(chunk_total):
        to_near(c, 0).wait_send()
        to_near(c, 1).wait_send()
        to_cross(c).wait_send()


def round_kernel(attended_ref, expert_ref, attended_out, expert_out):
    attended_out[...] = attended_ref[...].astype(attended_out.dtype)
    expert_out[...] = expert_ref[...].astype(expert_out.dtype)


def body(
    tokens,
    attn_gain,
    q_weight,
    k_weight,
    v_weight,
    o_weight,
    k_cache,
    v_cache,
    lengths,
    moe_gain,
    gate_weight,
    up_weight,
    down_weight,
    expert_ids,
    route_weights,
):
    rows, model_width = tokens.shape
    local_heads, cache_len, head_dim = k_cache.shape[1:]
    slab = local_heads * cache_len
    req_count = lax.axis_size("req")
    width = model_width // 4
    everyone = req_count * rows
    blocks = max(1, req_count // 4)
    chunks = req_count // blocks
    batch = 16
    slots = 4 if req_count <= 8 else 1
    bf16, f32 = jnp.bfloat16, jnp.float32
    half_dim = head_dim // 2
    frequency = jnp.power(rope_base, jnp.arange(half_dim, dtype=f32) * (-2.0 / head_dim))
    vmem = pl.BlockSpec(memory_space=pltpu.VMEM)
    hbm = pl.BlockSpec(memory_space=pl.ANY)
    dma = pltpu.SemaphoreType.DMA
    attended, expert_out = pl.pallas_call(
        functools.partial(moe_kernel, req_count),
        out_shape=(
            jax.ShapeDtypeStruct((rows, width), f32),
            jax.ShapeDtypeStruct((rows, width), f32),
        ),
        in_specs=[vmem] * 7 + [hbm] * 9,
        out_specs=(vmem, vmem),
        scratch_shapes=[
            pltpu.VMEM(q_weight.shape, bf16),
            pltpu.VMEM(k_weight.shape, bf16),
            pltpu.VMEM(v_weight.shape, bf16),
            pltpu.VMEM((slots, batch, slab, head_dim), bf16),
            pltpu.VMEM((slots, batch, slab, head_dim), bf16),
            pltpu.VMEM(o_weight.shape, bf16),
            pltpu.VMEM(gate_weight.shape, bf16),
            pltpu.VMEM(up_weight.shape, bf16),
            pltpu.VMEM(down_weight.shape, bf16),
            pltpu.VMEM((rows * 16, head_dim), f32),
            pltpu.VMEM((batch, slab), f32),
            pltpu.VMEM((batch * 8, head_dim), f32),
            pltpu.VMEM((rows, local_heads * head_dim), f32),
            pltpu.VMEM((rows, 128), f32),
            pltpu.VMEM((rows, 128), f32),
            pltpu.VMEM((rows, local_heads * head_dim), f32),
            pltpu.VMEM((rows, 128), bf16),
            pltpu.VMEM((everyone, 128), bf16),
            pltpu.VMEM((3, rows, width), bf16),
            pltpu.VMEM((3, rows, width), bf16),
            pltpu.VMEM((4, everyone, width), bf16),
            pltpu.VMEM((4, everyone, width), bf16),
            pltpu.VMEM((2, everyone, width), bf16),
            pltpu.VMEM((everyone, width), bf16),
            pltpu.VMEM((everyone, width), bf16),
            pltpu.VMEM((everyone, width), bf16),
            pltpu.VMEM((everyone, width), bf16),
            dma((2, slots)),
            dma((7,)),
            dma((req_count,)),
            dma((req_count,)),
            dma((3,)),
            dma((3,)),
            dma((4, req_count)),
            dma((4, req_count)),
            dma((2, chunks)),
            dma((2, chunks)),
            dma((chunks,)),
            dma((chunks,)),
            dma((req_count,)),
            dma((req_count,)),
        ],
        compiler_params=pltpu.CompilerParams(
            collective_id=0, has_side_effects=True, vmem_limit_bytes=58 << 20
        ),
    )(
        tokens,
        attn_gain.reshape(1, model_width),
        moe_gain.reshape(1, model_width),
        frequency.reshape(1, half_dim),
        lengths.reshape(1, rows),
        expert_ids.T,
        route_weights.T,
        q_weight,
        k_weight,
        v_weight,
        k_cache.reshape(rows, slab, head_dim),
        v_cache.reshape(rows, slab, head_dim),
        o_weight,
        gate_weight,
        up_weight,
        down_weight,
    )
    return pl.pallas_call(
        round_kernel,
        out_shape=[jax.ShapeDtypeStruct((rows, width), bf16)] * 2,
        in_specs=[vmem, vmem],
        out_specs=[vmem, vmem],
    )(attended, expert_out)


def decode_kernel(
    tok_hbm, norm_gain_hbm, gain_hbm, freq_hbm, len_hbm, ids_hbm, route_hbm,
    q_hbm, k_hbm, v_hbm, kc_hbm, vc_hbm, o_hbm, gate_hbm, up_hbm, down_hbm,
    attended_ref, lines_ref,
    tok_ref, norm_gain_ref, gain_ref, freq_ref, len_ref, ids_ref, route_ref,
    q_buf, k_buf, v_buf, kc_buf, vc_buf, o_buf, gate_buf, up_buf, down_buf,
    pieces, score, mixed, own_value, own_score, held, attn_buf, wt_out, wt_in, gain_f32,
    rs_out, rs_in, own_f32, gath, part, core_in, s_out, s_in, f_out, f_in, z_out,
    cache_sem, load_sem, send_sem, recv_sem,
):
    rows = tok_ref.shape[0]
    width = attended_ref.shape[1]
    halves = gath.shape[2]
    part_rows = rows // halves
    line_rows = gath.shape[3]
    zs = line_rows // part_rows
    head_dim = 2 * freq_ref.shape[1]
    experts = gate_buf.shape[0]
    local_heads = q_buf.shape[1] // head_dim
    cache_len = kc_buf.shape[2] // local_heads
    groups, batch = kc_buf.shape[0], kc_buf.shape[1]
    slab = local_heads * cache_len
    bf16, f32 = jnp.bfloat16, jnp.float32

    req = lax.axis_index("req")
    head = lax.axis_index("head")
    z, y = req // 2, req % 2
    x, c = head // 2, head % 2
    near = head + 1 - 2 * c
    cross = (head + 2) % 4
    far = (near + 2) % 4
    z_of = [z, z + 1 - 2 * (z % 2), (z + 2) % 4, 3 - z]
    first_peer = (req + (1 - c) * (1 - 2 * y), head + c * (2 - 4 * x))
    second_peer = (req + c * (1 - 2 * y), head + (1 - c) * (2 - 4 * x))
    core_peer = (req, near)
    corner_peer = (req + 1 - 2 * y, cross)

    def z_peer(d):
        return (z_of[d] * 2 + y, head)

    def own_role(dx, dy):
        return [[0, 2 - c], [1 + c, 3]][dx][dy]

    def other_role(dx, dy):
        return [[0, 1 + c], [2 - c, 3]][dx][dy]

    quarters = {(0, 0): head, (0, 1): near, (1, 0): cross, (1, 1): far}

    def lanes(dx, dc):
        return pl.ds(pl.multiple_of(quarters[dx, dc] * width, width), width)

    loads = {}

    def load(name, source, target):
        copy = pltpu.make_async_copy(source, target, load_sem.at[len(loads)])
        loads[name] = copy
        copy.start()

    def cached(i):
        span = pl.ds(i * batch, batch)
        return (
            pltpu.make_async_copy(kc_hbm.at[span], kc_buf.at[i], cache_sem.at[0, i]),
            pltpu.make_async_copy(vc_hbm.at[span], vc_buf.at[i], cache_sem.at[1, i]),
        )

    load("ids", ids_hbm, ids_ref)
    load("route", route_hbm, route_ref)
    load("len", len_hbm, len_ref)
    load("freq", freq_hbm, freq_ref)
    load("norm_gain", norm_gain_hbm, norm_gain_ref)
    load("tok", tok_hbm, tok_ref)
    load("q", q_hbm, q_buf)
    load("k", k_hbm, k_buf)
    load("v", v_hbm, v_buf)
    per_half = groups // halves
    for i in range(groups):
        for copy in cached(i):
            copy.start()
        if i == 0:
            load("o", o_hbm, o_buf)
    load("gain", gain_hbm, gain_ref)
    load("gate", gate_hbm, gate_buf)
    load("up", up_hbm, up_buf)
    load("down", down_hbm, down_buf)

    barrier = pltpu.get_barrier_semaphore()
    for other in (near, cross, far):
        pl.semaphore_signal(barrier, inc=1, device_id=(req, other), device_id_type=MESH)
    pl.semaphore_signal(barrier, inc=1, device_id=corner_peer, device_id_type=MESH)
    for d in range(4):
        for dy in range(2):
            if d or dy:
                other = z_of[d] * 2 + (1 - y if dy else y)
                pl.semaphore_signal(barrier, inc=1, device_id=(other, head), device_id_type=MESH)

    sends = {}

    def remote(key, source, target, device):
        if key not in sends:
            at = len(sends)
            sends[key] = pltpu.make_async_remote_copy(
                src_ref=source, dst_ref=target, send_sem=send_sem.at[at], recv_sem=recv_sem.at[at],
                device_id=device, device_id_type=MESH,
            )
        return sends[key]

    lane = lax.broadcasted_iota(jnp.int32, (rows, 128), 1)
    named_by = lax.broadcasted_iota(jnp.int32, (128, rows), 0)
    identity = (
        lax.broadcasted_iota(jnp.int32, (rows, rows), 0)
        == lax.broadcasted_iota(jnp.int32, (rows, rows), 1)
    ).astype(bf16)

    def upright(across):
        return lax.dot_general(
            identity, across.astype(bf16), (((1,), (1,)), ((), ())), preferred_element_type=f32
        )

    for name in ("ids", "route", "len", "freq", "norm_gain"):
        loads[name].wait()
    across = jnp.zeros((128, rows), f32)
    for k in range(ids_ref.shape[0]):
        across = across + jnp.where(
            named_by == ids_ref[k : k + 1, :], route_ref[k : k + 1, :].astype(f32), 0.0
        )
    dense = upright(across).astype(bf16).reshape(halves, part_rows, 128)
    wt_out[...] = dense
    wt_in[0, :, 0] = dense
    lens = upright(jnp.broadcast_to(len_ref[...].astype(f32), (128, rows)))
    held[...] = lens

    pl.semaphore_wait(barrier, 4 + 7)

    def share(d, dy):
        other = (z_of[d] * 2 + (1 - y if dy else y), head)
        return remote(("share", d, dy), wt_out, wt_in.at[dy, :, d], other)

    for d in range(4):
        for dy in range(2):
            if d or dy:
                share(d, dy).start()

    loads["tok"].wait()
    tokens = tok_ref[...].astype(f32)
    spread_of = jnp.mean(tokens * tokens, axis=-1, keepdims=True)
    scaled = tokens * lax.rsqrt(spread_of + epsilon)
    normed = jnp.concatenate(
        [
            (scaled[:, i * 128 : (i + 1) * 128] * norm_gain_ref[i : i + 1, :].astype(f32)).astype(bf16)
            for i in range(norm_gain_ref.shape[0])
        ],
        axis=1,
    )
    angles = lens[:, 0 : head_dim // 2] * freq_ref[...]
    cosine, sine = jnp.cos(angles), jnp.sin(angles)
    cosine = jnp.concatenate([cosine, cosine], axis=1)
    sine = jnp.concatenate([-sine, sine], axis=1)
    scaling = 1.0 / math.sqrt(head_dim)

    def parts_of(n):
        return slice(n * head_dim, (n + 1) * head_dim)

    loads["q"].wait()
    queries = jnp.dot(normed, q_buf[...], preferred_element_type=f32)
    turned = []
    for n in range(local_heads):
        query = queries[:, parts_of(n)]
        query = query * cosine + pltpu.roll(query, head_dim // 2, 1) * sine
        turned.append(query)
        upper = query.astype(bf16).astype(f32)
        rest = query - upper
        middle = rest.astype(bf16).astype(f32)
        for p, piece in enumerate((upper, middle, rest - middle)):
            pieces[pl.ds(3 * n + p, rows, stride=16), :] = piece
    for p in range(3 * local_heads, 16):
        pieces[pl.ds(p, rows, stride=16), :] = jnp.zeros((rows, head_dim), f32)
    loads["k"].wait()
    keys = jnp.dot(normed, k_buf[...], preferred_element_type=f32)
    own_all = jnp.zeros((rows, 128), f32)
    for n in range(local_heads):
        key = keys[:, parts_of(n)]
        key = key * cosine + pltpu.roll(key, head_dim // 2, 1) * sine
        own_all = jnp.where(
            lane == n, jnp.sum(turned[n] * key, axis=-1, keepdims=True) * scaling, own_all
        )
    own_score[...] = own_all
    loads["v"].wait()
    own_value[...] = (
        jnp.dot(normed, v_buf[...], preferred_element_type=f32).astype(bf16).astype(f32)
    )

    row16 = lax.broadcasted_iota(jnp.int32, (16, slab), 0)
    owner16 = lax.broadcasted_iota(jnp.int32, (16, slab), 1) // cache_len
    of_head = (row16 >= owner16 * 3) & (row16 < owner16 * 3 + 3)
    diagonal = row16 == owner16
    position = lax.broadcasted_iota(jnp.int32, (batch, cache_len), 1)

    def attend(i):
        for copy in cached(i):
            copy.wait()
        first = pl.multiple_of(i * batch, batch)
        for r in range(batch):
            query = pieces[pl.ds(pl.multiple_of((first + r) * 16, 16), 16), :].astype(bf16)
            found = lax.dot_general(
                query, kc_buf[i, r], (((1,), (1,)), ((), ())), preferred_element_type=f32
            )
            score[r : r + 1, :] = jnp.sum(
                jnp.where(of_head, found, 0.0), axis=0, keepdims=True
            )
        members = pl.ds(first, batch)
        inside = position.astype(f32) < held[members, 0:1]
        own_block = own_score[members, :]
        chances, own_chances = [], []
        for n in range(local_heads):
            values = score[:, n * cache_len : (n + 1) * cache_len] * scaling
            values = jnp.where(inside, values, -1e30)
            own_one = own_block[:, n : n + 1]
            largest = jnp.maximum(jnp.max(values, axis=-1, keepdims=True), own_one)
            terms = jnp.exp(values - largest)
            own_term = jnp.exp(own_one - largest)
            totals = jnp.sum(terms, axis=-1, keepdims=True) + own_term
            chances.append(terms / totals)
            own_chances.append((own_term / totals).astype(bf16).astype(f32))
        chance = jnp.concatenate(chances, axis=1)
        for r in range(batch):
            spread_out = jnp.where(
                diagonal, jnp.broadcast_to(chance[r : r + 1, :], (16, slab)), 0.0
            ).astype(bf16)
            found = jnp.dot(spread_out, vc_buf[i, r], preferred_element_type=f32)
            mixed[r * 8 : (r + 1) * 8, :] = found[0:8, :]
        for n in range(local_heads):
            attn_buf[members, parts_of(n)] = (
                mixed[pl.ds(n, batch, stride=8), :] + own_chances[n] * own_value[members, parts_of(n)]
            )

    def attention(h):
        for i in range(h * per_half, (h + 1) * per_half):
            attend(i)

    def mine(h):
        return slice(h * part_rows, (h + 1) * part_rows)

    def project(h):
        if h == 0:
            loads["o"].wait()
        attn = attn_buf[mine(h), :].astype(bf16)
        for at, (dx, dc) in enumerate(((1, 0), (1, 1), (0, 1))):
            rs_out[h, at] = jnp.dot(
                attn, o_buf[:, lanes(dx, dc)], preferred_element_type=f32
            ).astype(bf16)
            remote(
                ("sum", h, at), rs_out.at[h, at], rs_in.at[h, at], (req, quarters[dx, dc])
            ).start()
        own_f32[mine(h), :] = tok_ref[mine(h), lanes(0, 0)].astype(f32) + jnp.dot(
            attn, o_buf[:, lanes(0, 0)], preferred_element_type=f32
        )

    def zrows(first, count=1):
        return pl.ds(first * part_rows, count * part_rows)

    def line(h, d):
        return remote(
            ("line", h, d), gath.at[0, 0, h, zrows(0)], gath.at[0, 0, h, zrows(d)], z_peer(d)
        )

    spans = [(0, 1), (1, zs - 1), (0, zs)]

    def to_first(h, which):
        span = zrows(*spans[which])
        return remote(
            ("first", h, which), gath.at[0, 0, h, span], gath.at[0, 2, h, span], first_peer
        )

    def to_second(h, f, which):
        span = zrows(*spans[which])
        return remote(
            ("second", h, f, which),
            gath.at[0, 2 * f, h, span], gath.at[0, 2 * f + 1, h, span], second_peer,
        )

    def to_corner(h, which):
        span = zrows(*spans[which])
        return remote(
            ("corner", h, which), gath.at[0, 0, h, span], gath.at[0, 3, h, span], corner_peer
        )

    def to_core(h, role, which):
        span = zrows(*spans[which])
        return remote(
            ("core", h, role, which),
            gath.at[0, role, h, span], gath.at[1, role, h, span], core_peer,
        )

    def own(h):
        for at in range(3):
            remote(("sum", h, at), None, None, None).wait_recv()
        total = own_f32[mine(h), :]
        for at in range(3):
            total = total + rs_in[h, at].astype(f32)
        rounded = total.astype(bf16)
        gath[0, 0, h, zrows(0), :] = rounded
        for d in (2, 3, 1):
            line(h, d).start()
        if GATHER[h]:
            to_corner(h, 0).start()
        to_first(h, 0).start()
        to_second(h, 0, 0).start()
        to_core(h, 0, 0).start()
        attended_ref[mine(h), :] = rounded

    def lined(h):
        for d in (1, 2, 3):
            line(h, d).wait_recv()
        if GATHER[h]:
            to_corner(h, 1).start()
        to_first(h, 1).start()
        to_second(h, 0, 1).start()
        to_core(h, 0, 1).start()

    def firsts(h):
        for which in (0, 1):
            to_first(h, which).wait_recv()
        if not GATHER[h]:
            to_second(h, 1, 2).start()
        to_core(h, 2, 2).start()

    def seconds(h, f):
        if f and GATHER[h]:
            for which in (0, 1):
                to_corner(h, which).wait_recv()
        else:
            for which in ((2,) if f else (0, 1)):
                to_second(h, f, which).wait_recv()
        to_core(h, 2 * f + 1, 2).start()

    def ready(h):
        for role, which in ((0, 0), (0, 1), (2, 2), (1, 2), (3, 2)):
            to_core(h, role, which).wait_recv()

    def role(dx, dc, dy):
        return other_role(dx, dy) if dc else own_role(dx, dy)

    def arrived(h, dx, dc):
        return jnp.concatenate(
            [gath[dc, role(dx, dc, dy), h] for dy in range(2)], axis=0
        ).astype(f32)

    def half(h):
        return remote(("half", h), part.at[1, :, h], core_in.at[:, h], core_peer)

    def compute(h):
        order = [(0, 0), (0, 1), (1, 0), (1, 1)]
        count = 2 * line_rows
        squares = jnp.zeros((count, 1), f32)
        for dx, dc in order:
            v = arrived(h, dx, dc)
            squares = squares + jnp.sum(v * v, axis=-1, keepdims=True)
        inverse = lax.rsqrt(squares * (1.0 / (4 * width)) + epsilon)
        gates = [jnp.zeros((count, gate_buf.shape[2]), f32) for _ in range(experts)]
        ups = [jnp.zeros((count, gate_buf.shape[2]), f32) for _ in range(experts)]
        for dx, dc in order:
            v = arrived(h, dx, dc)
            gain = jnp.concatenate(
                [
                    gain_f32[pl.ds(quarters[dx, dc] * (width // 128) + i, 1), :]
                    for i in range(width // 128)
                ],
                axis=1,
            )
            v = (v * inverse * gain).astype(bf16)
            depth = lanes(dx, dc)
            for e in range(experts):
                gates[e] = gates[e] + jnp.dot(v, gate_buf[e, depth, :], preferred_element_type=f32)
                ups[e] = ups[e] + jnp.dot(v, up_buf[e, depth, :], preferred_element_type=f32)
        hidden = [(g / (1.0 + jnp.exp(-g)) * u).astype(bf16) for g, u in zip(gates, ups)]
        dense_wt = jnp.concatenate(
            [wt_in[dy, h].reshape(line_rows, 128) for dy in range(2)], axis=0
        ).astype(f32)
        column = lax.broadcasted_iota(jnp.int32, (count, 128), 1)
        wt = [
            jnp.sum(jnp.where(column == req * experts + e, dense_wt, 0.0), axis=-1, keepdims=True)
            for e in range(experts)
        ]
        for dx, dc in ((1, 1), (0, 1), (1, 0), (0, 0)):
            value = jnp.zeros((count, width), f32)
            for e in range(experts):
                value = value + wt[e] * jnp.dot(
                    hidden[e], down_buf[e, :, lanes(dx, dc)], preferred_element_type=f32
                )
            value = value.astype(bf16)
            for dy in range(2):
                part[dc, role(dx, dc, dy), h] = value[dy * line_rows : (dy + 1) * line_rows]
            if (dx, dc) == (0, 1):
                half(h).start()

    def back_second(h, f):
        return remote(("back_second", h, f), s_out.at[f, h], s_in.at[f, h], second_peer)

    def back_corner(h):
        return remote(("back_corner", h), s_out.at[1, h], s_in.at[1, h], corner_peer)

    def back_first(h):
        return remote(("back_first", h), f_out.at[h], f_in.at[h], first_peer)

    def back_line(h, d):
        return remote(
            ("back_line", h, d), z_out.at[h, zrows(d)], lines_ref.at[h, d], z_peer(d)
        )

    def both(h, role):
        return part[0, role, h].astype(f32) + core_in[role, h].astype(f32)

    def send_second(h, f):
        s_out[f, h] = both(h, 2 * f + 1).astype(bf16)
        back_second(h, f).start()

    def halved(h):
        half(h).wait_recv()
        for f in (1, 0):
            s_out[f, h] = both(h, 2 * f + 1).astype(bf16)
            (back_corner(h) if f and RETURN[h] else back_second(h, f)).start()
        if RETURN[h]:
            f_out[h] = both(h, 2).astype(bf16)
            back_first(h).start()

    def quartered(h):
        if RETURN[h]:
            return
        back_second(h, 1).wait_recv()
        f_out[h] = (both(h, 2) + s_in[1, h].astype(f32)).astype(bf16)
        back_first(h).start()

    def finished(h):
        back_second(h, 0).wait_recv()
        back_first(h).wait_recv()
        total = both(h, 0) + s_in[0, h].astype(f32) + f_in[h].astype(f32)
        if RETURN[h]:
            back_corner(h).wait_recv()
            total = total + s_in[1, h].astype(f32)
        z_out[h] = total.astype(bf16)
        for d in (2, 3, 1):
            back_line(h, d).start()
        lines_ref[h, 0] = z_out[h, zrows(0), :]

    def weights():
        for name in ("gain", "gate", "up", "down"):
            loads[name].wait()
        gain_f32[...] = gain_ref[...].astype(f32)
        for d in range(4):
            for dy in range(2):
                if d or dy:
                    share(d, dy).wait_recv()

    steps = {
        "attention": attention, "project": project, "own": own, "lined": lined,
        "firsts": firsts, "seconds": seconds, "ready": ready, "compute": compute,
        "halved": halved, "quartered": quartered, "finished": finished,
        "weights": weights,
    }
    for name, *where in SCHEDULE:
        steps[name](*where)

    for h in range(halves):
        for d in (1, 2, 3):
            back_line(h, d).wait_recv()
    for copy in sends.values():
        copy.wait_send()


GATHER = (1, 1, 1, 1)
RETURN = (1, 1, 1, 1)
SCHEDULE = (
    ("attention", 0), ("project", 0), ("attention", 1), ("project", 1), ("attention", 2),
    ("project", 2), ("own", 0), ("attention", 3), ("own", 1), ("project", 3), ("lined", 0),
    ("own", 2), ("lined", 1), ("own", 3), ("seconds", 0, 1), ("lined", 2),
    ("firsts", 0), ("seconds", 0, 0), ("weights",), ("ready", 0), ("compute", 0), ("lined", 3), ("seconds", 1, 1),
    ("halved", 0), ("firsts", 1), ("seconds", 1, 0), ("seconds", 2, 1), ("ready", 1), ("compute", 1), ("firsts", 2), ("seconds", 2, 0),
    ("halved", 1), ("ready", 2), ("compute", 2), ("firsts", 3), ("seconds", 3, 0), ("seconds", 3, 1), ("halved", 2),
    ("ready", 3), ("compute", 3), ("halved", 3), ("finished", 0), ("finished", 1), ("finished", 2),
    ("finished", 3),
)


def finish_kernel(attended_ref, lines_ref, attended_out, expert_out):
    attended_out[...] = attended_ref[...]
    halves, zs, part_rows = lines_ref.shape[:3]
    for h in range(halves):
        total = lines_ref[h, 0].astype(jnp.float32)
        for d in range(1, zs):
            total = total + lines_ref[h, d].astype(jnp.float32)
        expert_out[h * part_rows : (h + 1) * part_rows, :] = total.astype(expert_out.dtype)


def planes_body(
    tokens, attn_gain, q_weight, k_weight, v_weight, o_weight, k_cache, v_cache, lengths,
    moe_gain, gate_weight, up_weight, down_weight, expert_ids, route_weights,
):
    rows, model_width = tokens.shape
    local_heads, cache_len, head_dim = k_cache.shape[1:]
    slab = local_heads * cache_len
    width = model_width // 4
    batch = 16
    groups = rows // batch
    halves = 4
    zs = 4
    part_rows = rows // halves
    line_rows = zs * part_rows
    bf16, f32 = jnp.bfloat16, jnp.float32
    half_dim = head_dim // 2
    frequency = np.power(rope_base, np.arange(half_dim) * (-2.0 / head_dim)).astype(np.float32)
    vmem = pl.BlockSpec(memory_space=pltpu.VMEM)
    hbm = pl.BlockSpec(memory_space=pl.ANY)
    dma = pltpu.SemaphoreType.DMA
    top = expert_ids.shape[1]
    attended, lines = pl.pallas_call(
        decode_kernel,
        out_shape=(
            pltpu.VMEM((rows, width), bf16),
            pltpu.VMEM((halves, zs, part_rows, width), bf16),
        ),
        in_specs=[hbm] * 16,
        out_specs=(vmem, vmem),
        scratch_shapes=[
            pltpu.VMEM((rows, model_width), bf16),
            pltpu.VMEM((model_width // 128, 128), bf16),
            pltpu.VMEM((model_width // 128, 128), bf16),
            pltpu.VMEM((1, half_dim), f32),
            pltpu.VMEM((1, rows), jnp.int32),
            pltpu.VMEM((top, rows), jnp.int32),
            pltpu.VMEM((top, rows), bf16),
            pltpu.VMEM(q_weight.shape, bf16),
            pltpu.VMEM(k_weight.shape, bf16),
            pltpu.VMEM(v_weight.shape, bf16),
            pltpu.VMEM((groups, batch, slab, head_dim), bf16),
            pltpu.VMEM((groups, batch, slab, head_dim), bf16),
            pltpu.VMEM(o_weight.shape, bf16),
            pltpu.VMEM(gate_weight.shape, bf16),
            pltpu.VMEM(up_weight.shape, bf16),
            pltpu.VMEM(down_weight.shape, bf16),
            pltpu.VMEM((rows * 16, head_dim), f32),
            pltpu.VMEM((batch, slab), f32),
            pltpu.VMEM((batch * 8, head_dim), f32),
            pltpu.VMEM((rows, local_heads * head_dim), f32),
            pltpu.VMEM((rows, 128), f32),
            pltpu.VMEM((rows, 128), f32),
            pltpu.VMEM((rows, local_heads * head_dim), f32),
            pltpu.VMEM((halves, part_rows, 128), bf16),
            pltpu.VMEM((2, halves, zs, part_rows, 128), bf16),
            pltpu.VMEM((model_width // 128, 128), f32),
            pltpu.VMEM((halves, 3, part_rows, width), bf16),
            pltpu.VMEM((halves, 3, part_rows, width), bf16),
            pltpu.VMEM((rows, width), f32),
            pltpu.VMEM((2, 4, halves, line_rows, width), bf16),
            pltpu.VMEM((2, 4, halves, line_rows, width), bf16),
            pltpu.VMEM((4, halves, line_rows, width), bf16),
            pltpu.VMEM((2, halves, line_rows, width), bf16),
            pltpu.VMEM((2, halves, line_rows, width), bf16),
            pltpu.VMEM((halves, line_rows, width), bf16),
            pltpu.VMEM((halves, line_rows, width), bf16),
            pltpu.VMEM((halves, line_rows, width), bf16),
            dma((2, groups)),
            dma((16,)),
            dma((128,)),
            dma((128,)),
        ],
        compiler_params=pltpu.CompilerParams(
            collective_id=0, has_side_effects=True, vmem_limit_bytes=58 << 20
        ),
    )(
        tokens,
        attn_gain.reshape(model_width // 128, 128),
        moe_gain.reshape(model_width // 128, 128),
        frequency.reshape(1, half_dim),
        lengths.reshape(1, rows),
        expert_ids.T,
        route_weights.T,
        q_weight,
        k_weight,
        v_weight,
        k_cache.reshape(rows, slab, head_dim),
        v_cache.reshape(rows, slab, head_dim),
        o_weight,
        gate_weight,
        up_weight,
        down_weight,
    )
    return pl.pallas_call(
        finish_kernel,
        out_shape=[jax.ShapeDtypeStruct((rows, width), bf16)] * 2,
        in_specs=[vmem, vmem],
        out_specs=[vmem, vmem],
    )(
        pltpu.with_memory_space_constraint(attended, pltpu.VMEM),
        pltpu.with_memory_space_constraint(lines, pltpu.VMEM),
    )


def solution(mesh):
    by_planes = mesh.shape["req"] == 8 and mesh.shape["head"] == 4
    return jax.shard_map(
        planes_body if by_planes else body,
        mesh=mesh,
        in_specs=(
            P("req", None),
            P(),
            P(None, "head"),
            P(None, "head"),
            P(None, "head"),
            P("head", None),
            P("req", "head", None, None),
            P("req", "head", None, None),
            P("req"),
            P(),
            P("req", None, "head"),
            P("req", None, "head"),
            P("req", "head", None),
            P("req", None),
            P("req", None),
        ),
        out_specs=(P("req", "head"), P("req", "head")),
        check_vma=False,
    )
```

```python
import functools
import math

import jax
import jax.numpy as jnp
from jax import lax
from jax.experimental import pallas as pl
from jax.experimental.pallas import tpu as pltpu
from jax.sharding import PartitionSpec as P
import numpy as np

epsilon = 1e-05
rope_base = 10000.0


MESH = pl.DeviceIdType.MESH


def moe_kernel(
    req_count,
    tok_ref, norm_gain_ref, gain_ref, freq_ref, len_ref, ids_ref, route_ref,
    q_hbm, k_hbm, v_hbm, kc_hbm, vc_hbm, o_hbm, gate_hbm, up_hbm, down_hbm,
    attended_ref, out_ref,
    q_buf, k_buf, v_buf, kc_buf, vc_buf, o_buf, gate_buf, up_buf, down_buf,
    pieces, score, mixed, own_value, own_score, held, attn_buf, wt_out, wt_in,
    part_out, part_in, gath, part, half_in, cross_out, cross_in, home_out, home_in,
    cache_sem, weight_sem, wt_send, wt_recv, rs_send, rs_recv, ga_send, ga_recv, sib_send, sib_recv, x_send, x_recv, hm_send, hm_recv,
):
    rows, width = attended_ref.shape
    head_dim = 2 * freq_ref.shape[1]
    cache_len = kc_buf.shape[2] // (q_buf.shape[1] // head_dim)
    experts = gate_buf.shape[0]
    req = lax.axis_index("req")
    head = lax.axis_index("head")
    near = head + 1 - 2 * (head % 2)
    cross = (head + 2) % 4
    far = (near + 2) % 4
    quarter = [head, near, cross, far]
    blocks = max(1, req_count // 4)
    chunk_total = req_count // blocks
    chunk_rows = blocks * rows
    step_rows = 128

    slots, batch = kc_buf.shape[0], kc_buf.shape[1]
    groups = rows // batch
    local_heads = q_buf.shape[1] // head_dim
    sources = [q_hbm, k_hbm, v_hbm, o_hbm, gate_hbm, up_hbm, down_hbm]
    targets = [q_buf, k_buf, v_buf, o_buf, gate_buf, up_buf, down_buf]
    weights = [
        pltpu.make_async_copy(source, target, weight_sem.at[i])
        for i, (source, target) in enumerate(zip(sources, targets))
    ]

    def cached(i, at):
        span = pl.ds(i * batch, batch)
        return (
            pltpu.make_async_copy(kc_hbm.at[span], kc_buf.at[at], cache_sem.at[0, at]),
            pltpu.make_async_copy(vc_hbm.at[span], vc_buf.at[at], cache_sem.at[1, at]),
        )

    for copy in weights[:3]:
        copy.start()
    for i in range(slots):
        for copy in cached(i, i):
            copy.start()
    for copy in weights[3:]:
        copy.start()

    barrier = pltpu.get_barrier_semaphore()
    for other in (near, cross, far):
        pl.semaphore_signal(barrier, inc=1, device_id=(req, other), device_id_type=MESH)
    for step in range(1, req_count):
        pl.semaphore_signal(
            barrier, inc=1, device_id=((req + step) % req_count, head), device_id_type=MESH
        )
    pl.semaphore_wait(barrier, 3 + req_count - 1)

    def remote(source, target, send, recv, device):
        return pltpu.make_async_remote_copy(
            src_ref=source, dst_ref=target, send_sem=send, recv_sem=recv,
            device_id=device, device_id_type=MESH,
        )

    def lanes(d):
        return pl.ds(pl.multiple_of(quarter[d] * width, width), width)

    lane = lax.broadcasted_iota(jnp.int32, (rows, 128), 1)
    named_by = lax.broadcasted_iota(jnp.int32, (128, rows), 0)
    identity = (
        lax.broadcasted_iota(jnp.int32, (rows, rows), 0)
        == lax.broadcasted_iota(jnp.int32, (rows, rows), 1)
    ).astype(jnp.bfloat16)

    def upright(across):
        return lax.dot_general(
            identity, across.astype(jnp.bfloat16), (((1,), (1,)), ((), ())),
            preferred_element_type=jnp.float32,
        )

    across = jnp.zeros((128, rows), jnp.float32)
    for k in range(ids_ref.shape[0]):
        across = across + jnp.where(
            named_by == ids_ref[k : k + 1, :],
            route_ref[k : k + 1, :].astype(jnp.float32),
            0.0,
        )
    dense = upright(across).astype(jnp.bfloat16)
    wt_out[...] = dense
    wt_in[0:rows, :] = dense
    lens = upright(jnp.broadcast_to(len_ref[...].astype(jnp.float32), (128, rows)))
    held[...] = lens

    def share(s):
        return remote(
            wt_out, wt_in.at[pl.ds(s * rows, rows)], wt_send.at[s], wt_recv.at[s],
            ((req + req_count - s) % req_count, head),
        )

    for s in range(1, req_count):
        share(s).start()

    tokens = tok_ref[...].astype(jnp.float32)
    spread_of = jnp.mean(tokens * tokens, axis=-1, keepdims=True)
    normed = (tokens * lax.rsqrt(spread_of + epsilon) * norm_gain_ref[...].astype(jnp.float32)).astype(
        jnp.bfloat16
    )
    angles = lens[:, 0 : head_dim // 2] * freq_ref[...]
    cosine, sine = jnp.cos(angles), jnp.sin(angles)
    cosine = jnp.concatenate([cosine, cosine], axis=1)
    sine = jnp.concatenate([-sine, sine], axis=1)
    scaling = 1.0 / math.sqrt(head_dim)
    own_scores = []
    for i in range(3):
        weights[i].wait()
    for n in range(local_heads):
        part_of = slice(n * head_dim, (n + 1) * head_dim)
        query, key, value = [
            jnp.dot(normed, ref[:, part_of], preferred_element_type=jnp.float32)
            for ref in (q_buf, k_buf, v_buf)
        ]
        query = query * cosine + pltpu.roll(query, head_dim // 2, 1) * sine
        key = key * cosine + pltpu.roll(key, head_dim // 2, 1) * sine
        own_value[:, part_of] = value.astype(jnp.bfloat16).astype(jnp.float32)
        own_scores.append(jnp.sum(query * key, axis=-1, keepdims=True) * scaling)
        upper = query.astype(jnp.bfloat16).astype(jnp.float32)
        rest = query - upper
        middle = rest.astype(jnp.bfloat16).astype(jnp.float32)
        for p, piece in enumerate((upper, middle, rest - middle)):
            pieces[pl.ds(3 * n + p, rows, stride=16), :] = piece
    for p in range(3 * local_heads, 16):
        pieces[pl.ds(p, rows, stride=16), :] = jnp.zeros((rows, head_dim), jnp.float32)
    own_all = jnp.zeros((rows, 128), jnp.float32)
    for n in range(local_heads):
        own_all = jnp.where(lane == n, own_scores[n], own_all)
    own_score[...] = own_all

    slab = local_heads * cache_len
    row16 = lax.broadcasted_iota(jnp.int32, (16, slab), 0)
    owner16 = lax.broadcasted_iota(jnp.int32, (16, slab), 1) // cache_len
    of_head = (row16 >= owner16 * 3) & (row16 < owner16 * 3 + 3)
    diagonal = row16 == owner16
    position = lax.broadcasted_iota(jnp.int32, (batch, cache_len), 1)

    @pl.loop(0, groups)
    def _(i):
        at = i % slots
        for copy in cached(i, at):
            copy.wait()
        first = pl.multiple_of(i * batch, batch)
        for r in range(batch):
            query = pieces[pl.ds(pl.multiple_of((first + r) * 16, 16), 16), :].astype(jnp.bfloat16)
            found = lax.dot_general(
                query, kc_buf[at, r], (((1,), (1,)), ((), ())), preferred_element_type=jnp.float32
            )
            score[r : r + 1, :] = jnp.sum(
                jnp.where(of_head, found, 0.0), axis=0, keepdims=True
            )
        members = pl.ds(first, batch)
        inside = position.astype(jnp.float32) < held[members, 0:1]
        own_block = own_score[members, :]
        chances, own_chances = [], []
        for n in range(local_heads):
            values = score[:, n * cache_len : (n + 1) * cache_len] * scaling
            values = jnp.where(inside, values, -1e30)
            own_one = own_block[:, n : n + 1]
            largest = jnp.maximum(jnp.max(values, axis=-1, keepdims=True), own_one)
            terms = jnp.exp(values - largest)
            own_term = jnp.exp(own_one - largest)
            totals = jnp.sum(terms, axis=-1, keepdims=True) + own_term
            chances.append(terms / totals)
            own_chances.append((own_term / totals).astype(jnp.bfloat16).astype(jnp.float32))
        chance = jnp.concatenate(chances, axis=1)
        for r in range(batch):
            spread_out = jnp.where(
                diagonal, jnp.broadcast_to(chance[r : r + 1, :], (16, slab)), 0.0
            ).astype(jnp.bfloat16)
            found = jnp.dot(spread_out, vc_buf[at, r], preferred_element_type=jnp.float32)
            mixed[r * 8 : (r + 1) * 8, :] = found[0:8, :]
        for n in range(local_heads):
            part_of = slice(n * head_dim, (n + 1) * head_dim)
            attn_buf[members, part_of] = (
                mixed[pl.ds(n, batch, stride=8), :] + own_chances[n] * own_value[members, part_of]
            )

        @pl.when(i + slots < groups)
        def _():
            for copy in cached(i + slots, at):
                copy.start()

    weights[3].wait()
    attn = attn_buf[...].astype(jnp.bfloat16)
    rs = []
    for d in (2, 3, 1):
        part_out[d - 1] = jnp.dot(
            attn, o_buf[:, lanes(d)], preferred_element_type=jnp.float32
        ).astype(jnp.bfloat16)
        copy = remote(
            part_out.at[d - 1], part_in.at[d - 1], rs_send.at[d - 1], rs_recv.at[d - 1],
            (req, quarter[d]),
        )
        copy.start()
        rs.append(copy)
    total = tok_ref[:, lanes(0)].astype(jnp.float32) + jnp.dot(
        attn, o_buf[:, lanes(0)], preferred_element_type=jnp.float32
    )
    for copy in rs:
        copy.wait_recv()
    for d in range(3):
        total = total + part_in[d].astype(jnp.float32)
    own = total.astype(jnp.bfloat16)
    attended_ref[...] = total
    gath[0, 0:rows, :] = own

    def slot(s):
        return pl.ds(s * rows, rows)

    def spread(s):
        return remote(
            gath.at[0, slot(0)], gath.at[0, slot(s)], ga_send.at[0, s], ga_recv.at[0, s],
            ((req + req_count - s) % req_count, head),
        )

    def pass_on(d, s):
        origin, device = {1: (0, near), 2: (0, cross), 3: (2, near)}[d]
        return remote(
            gath.at[origin, slot(s)], gath.at[d, slot(s)], ga_send.at[d, s], ga_recv.at[d, s],
            (req, device),
        )

    pass_on(2, 0).start()
    order = sorted(range(1, req_count), key=lambda s: (s + blocks * 0))
    for s in order:
        spread(s).start()
    pass_on(1, 0).start()
    for copy in weights[4:]:
        copy.wait()
    for s in range(1, req_count):
        share(s).wait_recv()

    def home(s):
        return remote(
            home_out.at[slot(s)], home_in.at[slot(s)], hm_send.at[s], hm_recv.at[s],
            ((req + s) % req_count, head),
        )

    def to_near(c, which):
        span = pl.ds(c * chunk_rows, chunk_rows)
        return remote(
            part.at[2 * which + 1, span], half_in.at[which, span],
            sib_send.at[which, c], sib_recv.at[which, c], (req, near),
        )

    def to_cross(c):
        span = pl.ds(c * chunk_rows, chunk_rows)
        return remote(
            cross_out.at[span], cross_in.at[span], x_send.at[c], x_recv.at[c], (req, cross)
        )

    def compute(start):
        span = pl.ds(start, step_rows)
        squares = jnp.zeros((step_rows, 1), jnp.float32)
        for d in range(4):
            x = gath[d, span, :].astype(jnp.float32)
            squares = squares + jnp.sum(x * x, axis=-1, keepdims=True)
        inverse = lax.rsqrt(squares * (1.0 / (4 * width)) + epsilon)
        gates = [jnp.zeros((step_rows, gate_buf.shape[2]), jnp.float32) for _ in range(experts)]
        ups = [jnp.zeros((step_rows, gate_buf.shape[2]), jnp.float32) for _ in range(experts)]
        for d in range(4):
            x = gath[d, span, :].astype(jnp.float32)
            x = (x * inverse * gain_ref[:, lanes(d)].astype(jnp.float32)).astype(jnp.bfloat16)
            depth = pl.ds(pl.multiple_of(quarter[d] * width, width), width)
            for e in range(experts):
                gates[e] = gates[e] + jnp.dot(
                    x, gate_buf[e, depth, :], preferred_element_type=jnp.float32
                )
                ups[e] = ups[e] + jnp.dot(
                    x, up_buf[e, depth, :], preferred_element_type=jnp.float32
                )
        hidden = [
            (g / (1.0 + jnp.exp(-g)) * u).astype(jnp.bfloat16) for g, u in zip(gates, ups)
        ]
        dense_wt = wt_in[span, :].astype(jnp.float32)
        column = lax.broadcasted_iota(jnp.int32, (step_rows, 128), 1)
        wt = [
            jnp.sum(
                jnp.where(column == req * experts + e, dense_wt, 0.0), axis=-1, keepdims=True
            )
            for e in range(experts)
        ]
        for d in (1, 3, 2, 0):
            value = jnp.zeros((step_rows, width), jnp.float32)
            for e in range(experts):
                value = value + wt[e] * jnp.dot(
                    hidden[e], down_buf[e, :, lanes(d)], preferred_element_type=jnp.float32
                )
            part[d, span, :] = value.astype(jnp.bfloat16)

    def reduce_cross(c):
        span = pl.ds(c * chunk_rows, chunk_rows)
        to_near(c, 1).wait_recv()
        cross_out[span, :] = (
            part[2, span, :].astype(jnp.float32) + half_in[1, span, :].astype(jnp.float32)
        ).astype(jnp.bfloat16)
        to_cross(c).start()

    def reduce_home(c):
        span = pl.ds(c * chunk_rows, chunk_rows)
        to_near(c, 0).wait_recv()
        to_cross(c).wait_recv()
        home_out[span, :] = (
            part[0, span, :].astype(jnp.float32)
            + half_in[0, span, :].astype(jnp.float32)
            + cross_in[span, :].astype(jnp.float32)
        ).astype(jnp.bfloat16)
        for s in range(c * blocks, (c + 1) * blocks):
            if s:
                home(s).start()

    def forward(c):
        for s in range(c * blocks, (c + 1) * blocks):
            if s:
                spread(s).wait_recv()
                pass_on(2, s).start()
                pass_on(1, s).start()

    def forward_far(c):
        for s in range(c * blocks, (c + 1) * blocks):
            pass_on(2, s).wait_recv()
            pass_on(3, s).start()

    forward(0)
    forward(1)
    forward_far(0)
    for c in range(chunk_total):
        if c + 2 < chunk_total:
            forward(c + 2)
        if c + 1 < chunk_total:
            forward_far(c + 1)
        for s in range(c * blocks, (c + 1) * blocks):
            pass_on(1, s).wait_recv()
            pass_on(3, s).wait_recv()
        steps = chunk_rows // step_rows
        if steps == 1:
            compute(c * chunk_rows)
        else:
            @pl.loop(0, steps)
            def _(i):
                compute(pl.multiple_of(c * chunk_rows + i * step_rows, step_rows))
        to_near(c, 1).start()
        to_near(c, 0).start()
        if c:
            reduce_cross(c - 1)
        if c > 1:
            reduce_home(c - 2)
    reduce_cross(chunk_total - 1)
    if chunk_total > 1:
        reduce_home(chunk_total - 2)
    reduce_home(chunk_total - 1)
    result = home_out[0:rows, :].astype(jnp.float32)
    for s in range(1, req_count):
        home(s).wait_recv()
        result = result + home_in[s * rows : (s + 1) * rows, :].astype(jnp.float32)
    out_ref[...] = result

    for copy in rs:
        copy.wait_send()
    for s in range(req_count):
        for d in range(1, 4):
            pass_on(d, s).wait_send()
        if s:
            spread(s).wait_send()
            share(s).wait_send()
            home(s).wait_send()
    for c in range(chunk_total):
        to_near(c, 0).wait_send()
        to_near(c, 1).wait_send()
        to_cross(c).wait_send()


def round_kernel(attended_ref, expert_ref, attended_out, expert_out):
    attended_out[...] = attended_ref[...].astype(attended_out.dtype)
    expert_out[...] = expert_ref[...].astype(expert_out.dtype)


def body(
    tokens,
    attn_gain,
    q_weight,
    k_weight,
    v_weight,
    o_weight,
    k_cache,
    v_cache,
    lengths,
    moe_gain,
    gate_weight,
    up_weight,
    down_weight,
    expert_ids,
    route_weights,
):
    rows, model_width = tokens.shape
    local_heads, cache_len, head_dim = k_cache.shape[1:]
    slab = local_heads * cache_len
    req_count = lax.axis_size("req")
    width = model_width // 4
    everyone = req_count * rows
    blocks = max(1, req_count // 4)
    chunks = req_count // blocks
    batch = 16
    slots = 4 if req_count <= 8 else 1
    bf16, f32 = jnp.bfloat16, jnp.float32
    half_dim = head_dim // 2
    frequency = jnp.power(rope_base, jnp.arange(half_dim, dtype=f32) * (-2.0 / head_dim))
    vmem = pl.BlockSpec(memory_space=pltpu.VMEM)
    hbm = pl.BlockSpec(memory_space=pl.ANY)
    dma = pltpu.SemaphoreType.DMA
    attended, expert_out = pl.pallas_call(
        functools.partial(moe_kernel, req_count),
        out_shape=(
            jax.ShapeDtypeStruct((rows, width), f32),
            jax.ShapeDtypeStruct((rows, width), f32),
        ),
        in_specs=[vmem] * 7 + [hbm] * 9,
        out_specs=(vmem, vmem),
        scratch_shapes=[
            pltpu.VMEM(q_weight.shape, bf16),
            pltpu.VMEM(k_weight.shape, bf16),
            pltpu.VMEM(v_weight.shape, bf16),
            pltpu.VMEM((slots, batch, slab, head_dim), bf16),
            pltpu.VMEM((slots, batch, slab, head_dim), bf16),
            pltpu.VMEM(o_weight.shape, bf16),
            pltpu.VMEM(gate_weight.shape, bf16),
            pltpu.VMEM(up_weight.shape, bf16),
            pltpu.VMEM(down_weight.shape, bf16),
            pltpu.VMEM((rows * 16, head_dim), f32),
            pltpu.VMEM((batch, slab), f32),
            pltpu.VMEM((batch * 8, head_dim), f32),
            pltpu.VMEM((rows, local_heads * head_dim), f32),
            pltpu.VMEM((rows, 128), f32),
            pltpu.VMEM((rows, 128), f32),
            pltpu.VMEM((rows, local_heads * head_dim), f32),
            pltpu.VMEM((rows, 128), bf16),
            pltpu.VMEM((everyone, 128), bf16),
            pltpu.VMEM((3, rows, width), bf16),
            pltpu.VMEM((3, rows, width), bf16),
            pltpu.VMEM((4, everyone, width), bf16),
            pltpu.VMEM((4, everyone, width), bf16),
            pltpu.VMEM((2, everyone, width), bf16),
            pltpu.VMEM((everyone, width), bf16),
            pltpu.VMEM((everyone, width), bf16),
            pltpu.VMEM((everyone, width), bf16),
            pltpu.VMEM((everyone, width), bf16),
            dma((2, slots)),
            dma((7,)),
            dma((req_count,)),
            dma((req_count,)),
            dma((3,)),
            dma((3,)),
            dma((4, req_count)),
            dma((4, req_count)),
            dma((2, chunks)),
            dma((2, chunks)),
            dma((chunks,)),
            dma((chunks,)),
            dma((req_count,)),
            dma((req_count,)),
        ],
        compiler_params=pltpu.CompilerParams(
            collective_id=0, has_side_effects=True, vmem_limit_bytes=58 << 20
        ),
    )(
        tokens,
        attn_gain.reshape(1, model_width),
        moe_gain.reshape(1, model_width),
        frequency.reshape(1, half_dim),
        lengths.reshape(1, rows),
        expert_ids.T,
        route_weights.T,
        q_weight,
        k_weight,
        v_weight,
        k_cache.reshape(rows, slab, head_dim),
        v_cache.reshape(rows, slab, head_dim),
        o_weight,
        gate_weight,
        up_weight,
        down_weight,
    )
    return pl.pallas_call(
        round_kernel,
        out_shape=[jax.ShapeDtypeStruct((rows, width), bf16)] * 2,
        in_specs=[vmem, vmem],
        out_specs=[vmem, vmem],
    )(attended, expert_out)


def decode_kernel(
    tok_hbm, norm_gain_hbm, gain_hbm, freq_hbm, len_hbm, ids_hbm, route_hbm,
    q_hbm, k_hbm, v_hbm, kc_hbm, vc_hbm, o_hbm, gate_hbm, up_hbm, down_hbm,
    attended_ref, lines_ref,
    tok_ref, norm_gain_ref, gain_ref, freq_ref, len_ref, ids_ref, route_ref,
    q_buf, k_buf, v_buf, kc_buf, vc_buf, o_buf, gate_buf, up_buf, down_buf,
    pieces, score, mixed, own_value, own_score, held, attn_buf, wt_out, wt_in, gain_f32,
    rs_out, rs_in, own_f32, gath, part, core_in, s_out, s_in, f_out, f_in, z_out,
    cache_sem, load_sem, send_sem, recv_sem,
):
    rows = tok_ref.shape[0]
    width = attended_ref.shape[1]
    halves = gath.shape[2]
    part_rows = rows // halves
    line_rows = gath.shape[3]
    zs = line_rows // part_rows
    head_dim = 2 * freq_ref.shape[1]
    experts = gate_buf.shape[0]
    local_heads = q_buf.shape[1] // head_dim
    cache_len = kc_buf.shape[2] // local_heads
    groups, batch = kc_buf.shape[0], kc_buf.shape[1]
    slab = local_heads * cache_len
    bf16, f32 = jnp.bfloat16, jnp.float32

    req = lax.axis_index("req")
    head = lax.axis_index("head")
    z, y = req // 2, req % 2
    x, c = head // 2, head % 2
    near = head + 1 - 2 * c
    cross = (head + 2) % 4
    far = (near + 2) % 4
    z_of = [z, z + 1 - 2 * (z % 2), (z + 2) % 4, 3 - z]
    first_peer = (req + (1 - c) * (1 - 2 * y), head + c * (2 - 4 * x))
    second_peer = (req + c * (1 - 2 * y), head + (1 - c) * (2 - 4 * x))
    core_peer = (req, near)
    corner_peer = (req + 1 - 2 * y, cross)

    def z_peer(d):
        return (z_of[d] * 2 + y, head)

    def own_role(dx, dy):
        return [[0, 2 - c], [1 + c, 3]][dx][dy]

    def other_role(dx, dy):
        return [[0, 1 + c], [2 - c, 3]][dx][dy]

    quarters = {(0, 0): head, (0, 1): near, (1, 0): cross, (1, 1): far}

    def lanes(dx, dc):
        return pl.ds(pl.multiple_of(quarters[dx, dc] * width, width), width)

    loads = {}

    def load(name, source, target):
        copy = pltpu.make_async_copy(source, target, load_sem.at[len(loads)])
        loads[name] = copy
        copy.start()

    def cached(i):
        span = pl.ds(i * batch, batch)
        return (
            pltpu.make_async_copy(kc_hbm.at[span], kc_buf.at[i], cache_sem.at[0, i]),
            pltpu.make_async_copy(vc_hbm.at[span], vc_buf.at[i], cache_sem.at[1, i]),
        )

    load("ids", ids_hbm, ids_ref)
    load("route", route_hbm, route_ref)
    load("len", len_hbm, len_ref)
    load("freq", freq_hbm, freq_ref)
    load("norm_gain", norm_gain_hbm, norm_gain_ref)
    load("tok", tok_hbm, tok_ref)
    load("q", q_hbm, q_buf)
    load("k", k_hbm, k_buf)
    load("v", v_hbm, v_buf)
    per_half = groups // halves
    for i in range(groups):
        for copy in cached(i):
            copy.start()
        if i == 0:
            load("o", o_hbm, o_buf)

    barrier = pltpu.get_barrier_semaphore()
    for other in (near, cross, far):
        pl.semaphore_signal(barrier, inc=1, device_id=(req, other), device_id_type=MESH)
    pl.semaphore_signal(barrier, inc=1, device_id=corner_peer, device_id_type=MESH)
    for d in range(4):
        for dy in range(2):
            if d or dy:
                other = z_of[d] * 2 + (1 - y if dy else y)
                pl.semaphore_signal(barrier, inc=1, device_id=(other, head), device_id_type=MESH)

    sends = {}

    def remote(key, source, target, device):
        if key not in sends:
            at = len(sends)
            sends[key] = pltpu.make_async_remote_copy(
                src_ref=source, dst_ref=target, send_sem=send_sem.at[at], recv_sem=recv_sem.at[at],
                device_id=device, device_id_type=MESH,
            )
        return sends[key]

    lane = lax.broadcasted_iota(jnp.int32, (rows, 128), 1)
    named_by = lax.broadcasted_iota(jnp.int32, (128, rows), 0)
    identity = (
        lax.broadcasted_iota(jnp.int32, (rows, rows), 0)
        == lax.broadcasted_iota(jnp.int32, (rows, rows), 1)
    ).astype(bf16)

    def upright(across):
        return lax.dot_general(
            identity, across.astype(bf16), (((1,), (1,)), ((), ())), preferred_element_type=f32
        )

    for name in ("ids", "route", "len", "freq", "norm_gain"):
        loads[name].wait()
    across = jnp.zeros((128, rows), f32)
    for k in range(ids_ref.shape[0]):
        across = across + jnp.where(
            named_by == ids_ref[k : k + 1, :], route_ref[k : k + 1, :].astype(f32), 0.0
        )
    dense = upright(across).astype(bf16).reshape(halves, part_rows, 128)
    wt_out[...] = dense
    wt_in[0, :, 0] = dense
    lens = upright(jnp.broadcast_to(len_ref[...].astype(f32), (128, rows)))
    held[...] = lens

    pl.semaphore_wait(barrier, 4 + 7)

    def share(d, dy):
        other = (z_of[d] * 2 + (1 - y if dy else y), head)
        return remote(("share", d, dy), wt_out, wt_in.at[dy, :, d], other)

    for d in range(4):
        for dy in range(2):
            if d or dy:
                share(d, dy).start()

    loads["tok"].wait()
    tokens = tok_ref[...].astype(f32)
    spread_of = jnp.mean(tokens * tokens, axis=-1, keepdims=True)
    scaled = tokens * lax.rsqrt(spread_of + epsilon)
    normed = jnp.concatenate(
        [
            (scaled[:, i * 128 : (i + 1) * 128] * norm_gain_ref[i : i + 1, :].astype(f32)).astype(bf16)
            for i in range(norm_gain_ref.shape[0])
        ],
        axis=1,
    )
    angles = lens[:, 0 : head_dim // 2] * freq_ref[...]
    cosine, sine = jnp.cos(angles), jnp.sin(angles)
    cosine = jnp.concatenate([cosine, cosine], axis=1)
    sine = jnp.concatenate([-sine, sine], axis=1)
    scaling = 1.0 / math.sqrt(head_dim)

    def parts_of(n):
        return slice(n * head_dim, (n + 1) * head_dim)

    loads["q"].wait()
    queries = jnp.dot(normed, q_buf[...], preferred_element_type=f32)
    turned = []
    for n in range(local_heads):
        query = queries[:, parts_of(n)]
        query = query * cosine + pltpu.roll(query, head_dim // 2, 1) * sine
        turned.append(query)
        upper = query.astype(bf16).astype(f32)
        rest = query - upper
        middle = rest.astype(bf16).astype(f32)
        for p, piece in enumerate((upper, middle, rest - middle)):
            pieces[pl.ds(3 * n + p, rows, stride=16), :] = piece
    for p in range(3 * local_heads, 16):
        pieces[pl.ds(p, rows, stride=16), :] = jnp.zeros((rows, head_dim), f32)
    loads["k"].wait()
    keys = jnp.dot(normed, k_buf[...], preferred_element_type=f32)
    own_all = jnp.zeros((rows, 128), f32)
    for n in range(local_heads):
        key = keys[:, parts_of(n)]
        key = key * cosine + pltpu.roll(key, head_dim // 2, 1) * sine
        own_all = jnp.where(
            lane == n, jnp.sum(turned[n] * key, axis=-1, keepdims=True) * scaling, own_all
        )
    own_score[...] = own_all
    loads["v"].wait()
    own_value[...] = (
        jnp.dot(normed, v_buf[...], preferred_element_type=f32).astype(bf16).astype(f32)
    )

    row16 = lax.broadcasted_iota(jnp.int32, (16, slab), 0)
    owner16 = lax.broadcasted_iota(jnp.int32, (16, slab), 1) // cache_len
    of_head = (row16 >= owner16 * 3) & (row16 < owner16 * 3 + 3)
    diagonal = row16 == owner16
    position = lax.broadcasted_iota(jnp.int32, (batch, cache_len), 1)

    def attend(i):
        for copy in cached(i):
            copy.wait()
        first = pl.multiple_of(i * batch, batch)
        for r in range(batch):
            query = pieces[pl.ds(pl.multiple_of((first + r) * 16, 16), 16), :].astype(bf16)
            found = lax.dot_general(
                query, kc_buf[i, r], (((1,), (1,)), ((), ())), preferred_element_type=f32
            )
            score[r : r + 1, :] = jnp.sum(
                jnp.where(of_head, found, 0.0), axis=0, keepdims=True
            )
        members = pl.ds(first, batch)
        inside = position.astype(f32) < held[members, 0:1]
        own_block = own_score[members, :]
        chances, own_chances = [], []
        for n in range(local_heads):
            values = score[:, n * cache_len : (n + 1) * cache_len] * scaling
            values = jnp.where(inside, values, -1e30)
            own_one = own_block[:, n : n + 1]
            largest = jnp.maximum(jnp.max(values, axis=-1, keepdims=True), own_one)
            terms = jnp.exp(values - largest)
            own_term = jnp.exp(own_one - largest)
            totals = jnp.sum(terms, axis=-1, keepdims=True) + own_term
            chances.append(terms / totals)
            own_chances.append((own_term / totals).astype(bf16).astype(f32))
        chance = jnp.concatenate(chances, axis=1)
        for r in range(batch):
            spread_out = jnp.where(
                diagonal, jnp.broadcast_to(chance[r : r + 1, :], (16, slab)), 0.0
            ).astype(bf16)
            found = jnp.dot(spread_out, vc_buf[i, r], preferred_element_type=f32)
            mixed[r * 8 : (r + 1) * 8, :] = found[0:8, :]
        for n in range(local_heads):
            attn_buf[members, parts_of(n)] = (
                mixed[pl.ds(n, batch, stride=8), :] + own_chances[n] * own_value[members, parts_of(n)]
            )

    def attention(h):
        if h == 1:
            load("gain", gain_hbm, gain_ref)
            load("gate", gate_hbm, gate_buf)
            load("up", up_hbm, up_buf)
            load("down", down_hbm, down_buf)
        for i in range(h * per_half, (h + 1) * per_half):
            attend(i)

    def mine(h):
        return slice(h * part_rows, (h + 1) * part_rows)

    def project(h):
        if h == 0:
            loads["o"].wait()
        attn = attn_buf[mine(h), :].astype(bf16)
        for at, (dx, dc) in enumerate(((1, 0), (1, 1), (0, 1))):
            rs_out[h, at] = jnp.dot(
                attn, o_buf[:, lanes(dx, dc)], preferred_element_type=f32
            ).astype(bf16)
            remote(
                ("sum", h, at), rs_out.at[h, at], rs_in.at[h, at], (req, quarters[dx, dc])
            ).start()
        own_f32[mine(h), :] = tok_ref[mine(h), lanes(0, 0)].astype(f32) + jnp.dot(
            attn, o_buf[:, lanes(0, 0)], preferred_element_type=f32
        )

    def zrows(first, count=1):
        return pl.ds(first * part_rows, count * part_rows)

    def line(h, d):
        return remote(
            ("line", h, d), gath.at[0, 0, h, zrows(0)], gath.at[0, 0, h, zrows(d)], z_peer(d)
        )

    spans = [(0, 1), (1, zs - 1), (0, zs)]

    def to_first(h, which):
        span = zrows(*spans[which])
        return remote(
            ("first", h, which), gath.at[0, 0, h, span], gath.at[0, 2, h, span], first_peer
        )

    def to_second(h, f, which):
        span = zrows(*spans[which])
        return remote(
            ("second", h, f, which),
            gath.at[0, 2 * f, h, span], gath.at[0, 2 * f + 1, h, span], second_peer,
        )

    def to_corner(h, which):
        span = zrows(*spans[which])
        return remote(
            ("corner", h, which), gath.at[0, 0, h, span], gath.at[0, 3, h, span], corner_peer
        )

    def to_core(h, role, which):
        span = zrows(*spans[which])
        return remote(
            ("core", h, role, which),
            gath.at[0, role, h, span], gath.at[1, role, h, span], core_peer,
        )

    def own(h):
        for at in range(3):
            remote(("sum", h, at), None, None, None).wait_recv()
        total = own_f32[mine(h), :]
        for at in range(3):
            total = total + rs_in[h, at].astype(f32)
        rounded = total.astype(bf16)
        gath[0, 0, h, zrows(0), :] = rounded
        for d in (2, 3, 1):
            line(h, d).start()
        if GATHER[h]:
            to_corner(h, 0).start()
        to_first(h, 0).start()
        to_second(h, 0, 0).start()
        to_core(h, 0, 0).start()
        attended_ref[mine(h), :] = rounded

    def lined(h):
        for d in (1, 2, 3):
            line(h, d).wait_recv()
        if GATHER[h]:
            to_corner(h, 1).start()
        to_first(h, 1).start()
        to_second(h, 0, 1).start()
        to_core(h, 0, 1).start()

    def firsts(h):
        for which in (0, 1):
            to_first(h, which).wait_recv()
        if not GATHER[h]:
            to_second(h, 1, 2).start()
        to_core(h, 2, 2).start()

    def seconds(h, f):
        if f and GATHER[h]:
            for which in (0, 1):
                to_corner(h, which).wait_recv()
        else:
            for which in ((2,) if f else (0, 1)):
                to_second(h, f, which).wait_recv()
        to_core(h, 2 * f + 1, 2).start()

    def ready(h):
        for role, which in ((0, 0), (0, 1), (2, 2), (1, 2), (3, 2)):
            to_core(h, role, which).wait_recv()

    def role(dx, dc, dy):
        return other_role(dx, dy) if dc else own_role(dx, dy)

    def arrived(h, dx, dc):
        return jnp.concatenate(
            [gath[dc, role(dx, dc, dy), h] for dy in range(2)], axis=0
        ).astype(f32)

    def half(h):
        return remote(("half", h), part.at[1, :, h], core_in.at[:, h], core_peer)

    def compute(h):
        order = [(0, 0), (0, 1), (1, 0), (1, 1)]
        count = 2 * line_rows
        squares = jnp.zeros((count, 1), f32)
        for dx, dc in order:
            v = arrived(h, dx, dc)
            squares = squares + jnp.sum(v * v, axis=-1, keepdims=True)
        inverse = lax.rsqrt(squares * (1.0 / (4 * width)) + epsilon)
        gates = [jnp.zeros((count, gate_buf.shape[2]), f32) for _ in range(experts)]
        ups = [jnp.zeros((count, gate_buf.shape[2]), f32) for _ in range(experts)]
        for dx, dc in order:
            v = arrived(h, dx, dc)
            gain = jnp.concatenate(
                [
                    gain_f32[pl.ds(quarters[dx, dc] * (width // 128) + i, 1), :]
                    for i in range(width // 128)
                ],
                axis=1,
            )
            v = (v * inverse * gain).astype(bf16)
            depth = lanes(dx, dc)
            for e in range(experts):
                gates[e] = gates[e] + jnp.dot(v, gate_buf[e, depth, :], preferred_element_type=f32)
                ups[e] = ups[e] + jnp.dot(v, up_buf[e, depth, :], preferred_element_type=f32)
        hidden = [(g / (1.0 + jnp.exp(-g)) * u).astype(bf16) for g, u in zip(gates, ups)]
        dense_wt = jnp.concatenate(
            [wt_in[dy, h].reshape(line_rows, 128) for dy in range(2)], axis=0
        ).astype(f32)
        column = lax.broadcasted_iota(jnp.int32, (count, 128), 1)
        wt = [
            jnp.sum(jnp.where(column == req * experts + e, dense_wt, 0.0), axis=-1, keepdims=True)
            for e in range(experts)
        ]
        for dx, dc in ((1, 1), (0, 1), (1, 0), (0, 0)):
            value = jnp.zeros((count, width), f32)
            for e in range(experts):
                value = value + wt[e] * jnp.dot(
                    hidden[e], down_buf[e, :, lanes(dx, dc)], preferred_element_type=f32
                )
            value = value.astype(bf16)
            for dy in range(2):
                part[dc, role(dx, dc, dy), h] = value[dy * line_rows : (dy + 1) * line_rows]
            if (dx, dc) == (0, 1):
                half(h).start()

    def back_second(h, f):
        return remote(("back_second", h, f), s_out.at[f, h], s_in.at[f, h], second_peer)

    def back_corner(h):
        return remote(("back_corner", h), s_out.at[1, h], s_in.at[1, h], corner_peer)

    def back_first(h):
        return remote(("back_first", h), f_out.at[h], f_in.at[h], first_peer)

    def back_line(h, d):
        return remote(
            ("back_line", h, d), z_out.at[h, zrows(d)], lines_ref.at[h, d], z_peer(d)
        )

    def both(h, role):
        return part[0, role, h].astype(f32) + core_in[role, h].astype(f32)

    def send_second(h, f):
        s_out[f, h] = both(h, 2 * f + 1).astype(bf16)
        back_second(h, f).start()

    def halved(h):
        half(h).wait_recv()
        for f in (1, 0):
            s_out[f, h] = both(h, 2 * f + 1).astype(bf16)
            (back_corner(h) if f and RETURN[h] else back_second(h, f)).start()
        if RETURN[h]:
            f_out[h] = both(h, 2).astype(bf16)
            back_first(h).start()

    def quartered(h):
        if RETURN[h]:
            return
        back_second(h, 1).wait_recv()
        f_out[h] = (both(h, 2) + s_in[1, h].astype(f32)).astype(bf16)
        back_first(h).start()

    def finished(h):
        back_second(h, 0).wait_recv()
        back_first(h).wait_recv()
        total = both(h, 0) + s_in[0, h].astype(f32) + f_in[h].astype(f32)
        if RETURN[h]:
            back_corner(h).wait_recv()
            total = total + s_in[1, h].astype(f32)
        z_out[h] = total.astype(bf16)
        for d in (2, 3, 1):
            back_line(h, d).start()
        lines_ref[h, 0] = z_out[h, zrows(0), :]

    def weights():
        for name in ("gain", "gate", "up", "down"):
            loads[name].wait()
        gain_f32[...] = gain_ref[...].astype(f32)
        for d in range(4):
            for dy in range(2):
                if d or dy:
                    share(d, dy).wait_recv()

    steps = {
        "attention": attention, "project": project, "own": own, "lined": lined,
        "firsts": firsts, "seconds": seconds, "ready": ready, "compute": compute,
        "halved": halved, "quartered": quartered, "finished": finished,
        "weights": weights,
    }
    for name, *where in SCHEDULE:
        steps[name](*where)

    for h in range(halves):
        for d in (1, 2, 3):
            back_line(h, d).wait_recv()
    for copy in sends.values():
        copy.wait_send()


GATHER = (1, 1, 1, 1)
RETURN = (1, 1, 1, 1)
SCHEDULE = (
    ("attention", 0), ("project", 0), ("attention", 1), ("project", 1), ("attention", 2),
    ("project", 2), ("own", 0), ("attention", 3), ("own", 1), ("project", 3), ("lined", 0),
    ("own", 2), ("lined", 1), ("own", 3), ("seconds", 0, 1), ("lined", 2),
    ("firsts", 0), ("seconds", 0, 0), ("weights",), ("ready", 0), ("compute", 0), ("lined", 3), ("seconds", 1, 1),
    ("halved", 0), ("firsts", 1), ("seconds", 1, 0), ("seconds", 2, 1), ("ready", 1), ("compute", 1), ("firsts", 2), ("seconds", 2, 0),
    ("halved", 1), ("ready", 2), ("compute", 2), ("firsts", 3), ("seconds", 3, 0), ("seconds", 3, 1), ("halved", 2),
    ("ready", 3), ("compute", 3), ("halved", 3), ("finished", 0), ("finished", 1), ("finished", 2),
    ("finished", 3),
)


def finish_kernel(attended_ref, lines_ref, attended_out, expert_out):
    attended_out[...] = attended_ref[...]
    halves, zs, part_rows = lines_ref.shape[:3]
    for h in range(halves):
        total = lines_ref[h, 0].astype(jnp.float32)
        for d in range(1, zs):
            total = total + lines_ref[h, d].astype(jnp.float32)
        expert_out[h * part_rows : (h + 1) * part_rows, :] = total.astype(expert_out.dtype)


def planes_body(
    tokens, attn_gain, q_weight, k_weight, v_weight, o_weight, k_cache, v_cache, lengths,
    moe_gain, gate_weight, up_weight, down_weight, expert_ids, route_weights,
):
    rows, model_width = tokens.shape
    local_heads, cache_len, head_dim = k_cache.shape[1:]
    slab = local_heads * cache_len
    width = model_width // 4
    batch = 16
    groups = rows // batch
    halves = 4
    zs = 4
    part_rows = rows // halves
    line_rows = zs * part_rows
    bf16, f32 = jnp.bfloat16, jnp.float32
    half_dim = head_dim // 2
    frequency = np.power(rope_base, np.arange(half_dim) * (-2.0 / head_dim)).astype(np.float32)
    vmem = pl.BlockSpec(memory_space=pltpu.VMEM)
    hbm = pl.BlockSpec(memory_space=pl.ANY)
    dma = pltpu.SemaphoreType.DMA
    top = expert_ids.shape[1]
    attended, lines = pl.pallas_call(
        decode_kernel,
        out_shape=(
            pltpu.VMEM((rows, width), bf16),
            pltpu.VMEM((halves, zs, part_rows, width), bf16),
        ),
        in_specs=[hbm] * 16,
        out_specs=(vmem, vmem),
        scratch_shapes=[
            pltpu.VMEM((rows, model_width), bf16),
            pltpu.VMEM((model_width // 128, 128), bf16),
            pltpu.VMEM((model_width // 128, 128), bf16),
            pltpu.VMEM((1, half_dim), f32),
            pltpu.VMEM((1, rows), jnp.int32),
            pltpu.VMEM((top, rows), jnp.int32),
            pltpu.VMEM((top, rows), bf16),
            pltpu.VMEM(q_weight.shape, bf16),
            pltpu.VMEM(k_weight.shape, bf16),
            pltpu.VMEM(v_weight.shape, bf16),
            pltpu.VMEM((groups, batch, slab, head_dim), bf16),
            pltpu.VMEM((groups, batch, slab, head_dim), bf16),
            pltpu.VMEM(o_weight.shape, bf16),
            pltpu.VMEM(gate_weight.shape, bf16),
            pltpu.VMEM(up_weight.shape, bf16),
            pltpu.VMEM(down_weight.shape, bf16),
            pltpu.VMEM((rows * 16, head_dim), f32),
            pltpu.VMEM((batch, slab), f32),
            pltpu.VMEM((batch * 8, head_dim), f32),
            pltpu.VMEM((rows, local_heads * head_dim), f32),
            pltpu.VMEM((rows, 128), f32),
            pltpu.VMEM((rows, 128), f32),
            pltpu.VMEM((rows, local_heads * head_dim), f32),
            pltpu.VMEM((halves, part_rows, 128), bf16),
            pltpu.VMEM((2, halves, zs, part_rows, 128), bf16),
            pltpu.VMEM((model_width // 128, 128), f32),
            pltpu.VMEM((halves, 3, part_rows, width), bf16),
            pltpu.VMEM((halves, 3, part_rows, width), bf16),
            pltpu.VMEM((rows, width), f32),
            pltpu.VMEM((2, 4, halves, line_rows, width), bf16),
            pltpu.VMEM((2, 4, halves, line_rows, width), bf16),
            pltpu.VMEM((4, halves, line_rows, width), bf16),
            pltpu.VMEM((2, halves, line_rows, width), bf16),
            pltpu.VMEM((2, halves, line_rows, width), bf16),
            pltpu.VMEM((halves, line_rows, width), bf16),
            pltpu.VMEM((halves, line_rows, width), bf16),
            pltpu.VMEM((halves, line_rows, width), bf16),
            dma((2, groups)),
            dma((16,)),
            dma((128,)),
            dma((128,)),
        ],
        compiler_params=pltpu.CompilerParams(
            collective_id=0, has_side_effects=True, vmem_limit_bytes=58 << 20
        ),
    )(
        tokens,
        attn_gain.reshape(model_width // 128, 128),
        moe_gain.reshape(model_width // 128, 128),
        frequency.reshape(1, half_dim),
        lengths.reshape(1, rows),
        expert_ids.T,
        route_weights.T,
        q_weight,
        k_weight,
        v_weight,
        k_cache.reshape(rows, slab, head_dim),
        v_cache.reshape(rows, slab, head_dim),
        o_weight,
        gate_weight,
        up_weight,
        down_weight,
    )
    return pl.pallas_call(
        finish_kernel,
        out_shape=[jax.ShapeDtypeStruct((rows, width), bf16)] * 2,
        in_specs=[vmem, vmem],
        out_specs=[vmem, vmem],
    )(
        pltpu.with_memory_space_constraint(attended, pltpu.VMEM),
        pltpu.with_memory_space_constraint(lines, pltpu.VMEM),
    )


def solution(mesh):
    by_planes = mesh.shape["req"] == 8 and mesh.shape["head"] == 4
    return jax.shard_map(
        planes_body if by_planes else body,
        mesh=mesh,
        in_specs=(
            P("req", None),
            P(),
            P(None, "head"),
            P(None, "head"),
            P(None, "head"),
            P("head", None),
            P("req", "head", None, None),
            P("req", "head", None, None),
            P("req"),
            P(),
            P("req", None, "head"),
            P("req", None, "head"),
            P("req", "head", None),
            P("req", None),
            P("req", None),
        ),
        out_specs=(P("req", "head"), P("req", "head")),
        check_vma=False,
    )
```
